32 devices in a mesh: depth: 4 (over z), height: 8 (over y, x, core).
Axes of the slice: x: 2, y: 2, z: 4, core: 2. Of those that a mesh axis runs over, the one named last changes fastest.
Arguments:
- density: float32 [32, 512, 128], P('depth', 'height'), may hold values from -6 to 6
- light_vector: float32 [3], replicated, may hold values from -1 to 1
- colour_gain: float32 [3], replicated, may hold values from 0.5 to 3
- colour_bias: float32 [3], replicated, may hold values from -1 to 1
- shear_step: int32 [4], replicated, may hold values from 0 to 32
- reverse_view: int32 [4], replicated, may hold values from 0 to 1
Outputs:
- images: float32 [4, 4, 512, 128], P(None, None, ('height', 'depth'))
The draws below stay inside these ranges and needn't reach their ends.
All inputs are finite; a program needn't handle non-finite values.
Results may differ from the reference program's by a relative error of at most 0.0003.
Values sent between devices are 32-bit elements; how exact they have to be, the bound alone decides.
A program may use at most 64 MiB of HBM per device.

```python
import jax
import jax.numpy as jnp
from jax import lax

NX = 128
VIEWS = 4
SHEAR_MAX = 32
NZ = 32
NY = 512


def place_ends(result, key, least, largest):
    place = [jax.random.randint(jax.random.fold_in(key, axis), (), 0, length) for axis, length in enumerate(result.shape)]
    widest = result.shape.index(max(result.shape))
    beside = place[:widest] + [(place[widest] + 1) % result.shape[widest]] + place[widest + 1:]
    return result.at[tuple(place)].set(least).at[tuple(beside)].set(largest)


def block_scale(key, shape, cuts, least, high):
    gain, own = 1.0, jax.random.fold_in(key, 6)
    for axis_at, parts in cuts:
        steps = jnp.exp(jax.random.uniform(jax.random.fold_in(own, axis_at), (parts,), jnp.float32, least / len(cuts), high / len(cuts)))
        gain = gain * jnp.repeat(steps, shape[axis_at] // parts).reshape([-1 if axis == axis_at else 1 for axis in range(len(shape))])
    return gain


def noise(key, shape, scale, limit, shards=(), kind=jnp.bfloat16):
    entries = jax.random.normal(key, shape, jnp.float32) * scale
    if len(shards) > 0:
        entries = block_scale(key, shape, shards, -0.22, 0.18) * entries
    return jnp.clip(entries, min=-limit, max=limit).astype(kind)


def setup_inputs(seed: int = 0) -> dict:
    key_of = jax.random.split(jax.random.key(seed), 7)
    density = noise(key_of[0], (NZ, NY, NX), 1.0, 6.0, ((0, 4), (1, 8)), jnp.float32)
    light_vector = jnp.clip(jax.random.uniform(key_of[1], (3,), jnp.float32, -1.0, 1.0), -1.0, 1.0)
    colour_gain = jnp.clip(jax.random.uniform(key_of[2], (3,), jnp.float32, 0.5, 3.0), 0.5, 3.0)
    colour_bias = jnp.clip(jax.random.uniform(key_of[3], (3,), jnp.float32, -1.0, 1.0), -1.0, 1.0)
    shear_step = place_ends(jax.random.randint(key_of[4], (VIEWS,), 0, SHEAR_MAX + 1), jax.random.fold_in(key_of[4], 1), 0, SHEAR_MAX).astype(jnp.int32)
    reverse_view = place_ends(jax.random.randint(key_of[5], (VIEWS,), 0, 2), jax.random.fold_in(key_of[5], 1), 0, 1).astype(jnp.int32)
    return {"density": density, "light_vector": light_vector, "colour_gain": colour_gain, "colour_bias": colour_bias, "shear_step": shear_step, "reverse_view": reverse_view}


EXTINCTION = 2.5

def shade_block(padded, light_vector, colour_gain, colour_bias, extinction):
    centre = padded[1:-1, 1:-1, 1:-1]
    tilt_depth = 0.5 * (padded[2:, 1:-1, 1:-1] - padded[:-2, 1:-1, 1:-1])
    tilt_rows = 0.5 * (padded[1:-1, 2:, 1:-1] - padded[1:-1, :-2, 1:-1])
    tilt_cols = 0.5 * (padded[1:-1, 1:-1, 2:] - padded[1:-1, 1:-1, :-2])
    facing = (light_vector[0] * tilt_depth + light_vector[1] * tilt_rows + light_vector[2] * tilt_cols) * lax.rsqrt(1.0 + tilt_depth * tilt_depth + tilt_rows * tilt_rows + tilt_cols * tilt_cols)
    shading = 0.25 + 1.5 * jnp.maximum(facing, 0.0)
    optical = extinction * jax.nn.softplus(centre)
    opacity = -jnp.expm1(-optical)
    colour = jax.nn.sigmoid(colour_gain[:, None, None, None] * centre[None] + colour_bias[:, None, None, None])
    emitted = (opacity * shading)[None] * colour
    return jnp.concatenate([emitted, optical[None]], 0)

def reference(density, light_vector, colour_gain, colour_bias, shear_step, reverse_view):
    extinction = EXTINCTION / NZ
    padded = jnp.pad(density, 1)

    def view_image(view):
        step = shear_step[view]
        backward = reverse_view[view]

        def advance(carry, index):
            colour_sum, optical = carry
            plane = jnp.where(backward == 1, NZ - 1 - index, index).astype(jnp.int32)
            block = lax.dynamic_slice_in_dim(padded, plane, 3, 0)
            fields = shade_block(block, light_vector, colour_gain, colour_bias, extinction)[:, 0]
            fields = jnp.pad(fields, ((0, 0), (0, SHEAR_MAX), (0, 0)))
            offset = (plane * step // NZ).astype(jnp.int32)
            sample = lax.dynamic_slice_in_dim(fields, offset, NY, 1)
            colour_sum = colour_sum + sample[:3] * jnp.exp(-optical)[None]
            optical = optical + sample[3]
            return ((colour_sum, optical), None)
        start = (jnp.zeros((3, NY, NX), jnp.float32), jnp.zeros((NY, NX), jnp.float32))
        (colour_sum, optical), _ = lax.scan(advance, start, jnp.arange(NZ, dtype=jnp.int32))
        return jnp.concatenate([colour_sum, -jnp.expm1(-optical)[None]], 0)
    return jnp.stack([view_image(view) for view in range(VIEWS)], 1)
```

```python
import functools

import jax
import jax.numpy as jnp
from jax import lax
from jax.experimental import pallas as pl
from jax.experimental.pallas import tpu as pltpu
from jax.sharding import PartitionSpec as P

EXTINCTION = 2.5
LEAD = 8
TOGETHER = 6
MESH = pl.DeviceIdType.MESH


def spans(low, high, size):
    return [(at, min(size, high - at)) for at in range(low, high, size)]


def line_kernel(
    towers,
    density,
    light_in,
    gain_in,
    bias_in,
    shear_in,
    reverse_in,
    out,
    light,
    gain,
    bias,
    shear,
    reverse,
    volume,
    fields,
    outgoing,
    incoming,
    handed,
    sent_sem,
    halo_sem,
    hand_sem,
    part_sem,
):
    planes, rows, cols = density.shape
    margin = rows // 2
    views = shear.shape[0]
    groups = 4
    share = rows // groups
    total_planes = planes * groups
    extinction = EXTINCTION / total_planes
    d = lax.axis_index("depth")
    h = lax.axis_index("height")
    above, below = (h - 1 >= 0) & (h - 1 < towers), (h + 1 >= 0) & (h + 1 < towers)
    end = LEAD + rows
    own_planes = pl.ds(2, planes)
    images, plane_sent, edge_sent, down_sent, up_sent, relay_sent = range(6)
    pair_in, peer_in, edge_in, down_in, up_in, relay_in = range(6)

    own = pltpu.make_async_copy(
        density, volume.at[own_planes, pl.ds(LEAD, rows)], sent_sem.at[images]
    )
    own.start()
    scalars = [
        pltpu.make_async_copy(source, target, sent_sem.at[1 + index])
        for index, (source, target) in enumerate(
            zip((light_in, gain_in, bias_in, shear_in, reverse_in), (light, gain, bias, shear, reverse))
        )
    ]
    for scalar in scalars:
        scalar.start()

    barrier = pltpu.get_barrier_semaphore()
    expected = jnp.int32(0)
    for step_d, step_h in ((1, 0), (-1, 0), (0, 1), (0, -1)):
        at, count = (d + step_d, groups) if step_d else (h + step_h, towers)
        ok = (at >= 0) & (at < count)
        expected = expected + jnp.where(ok, 1, 0)

        @pl.when(ok)
        def _(target=(d + step_d, h + step_h)):
            pl.semaphore_signal(barrier, inc=1, device_id=target, device_id_type=MESH)

    for scalar in scalars:
        scalar.wait()
    own.wait()

    lz, ly, lx = light[0], light[1], light[2]
    half_gain = [0.5 * gain[c] for c in range(3)]
    half_bias = [0.5 * bias[c] for c in range(3)]
    inside = jnp.where(below, 1.0, 0.0)

    def shade(plane, row, count, keep):
        at = LEAD + row
        centre = volume[plane, at : at + count]
        lane = lax.broadcasted_iota(jnp.int32, (count, cols), 1)
        following = jnp.where(lane == cols - 1, 0.0, pltpu.roll(centre, cols - 1, 1))
        previous = jnp.where(lane == 0, 0.0, pltpu.roll(centre, 1, 1))
        dx = following - previous
        dz = volume[plane + 1, at : at + count] - volume[plane - 1, at : at + count]
        dy = volume[plane, at + 1 : at + 1 + count] - volume[plane, at - 1 : at - 1 + count]
        facing = (lz * dz + ly * dy + lx * dx) * lax.rsqrt(4.0 + dz * dz + dy * dy + dx * dx)
        shading = 0.25 + 1.5 * jnp.maximum(facing, 0.0)
        optical = extinction * (
            jnp.maximum(centre, 0.0) + jnp.log1p(jnp.exp(-jnp.abs(centre)))
        )
        opacity = jnp.tanh(0.5 * optical) * (1.0 + jnp.exp(-optical))
        if keep is not None:
            opacity = opacity * keep
        lit = 0.5 * (opacity * shading)
        to = pl.ds(row, count)
        for c in range(3):
            fields[c, plane, to] = lit + lit * jnp.tanh(half_gain[c] * centre + half_bias[c])
        fields[3, plane, to] = opacity

    def shade_box(low, high, top, bottom):
        tiles = (bottom - top) // 8
        together = max(1, min(high - low, -(-TOGETHER // tiles)))
        looped = (high - low) // together if high - low > together else 0

        def some(plane, count):
            for step in range(count):
                for row, size in spans(top, min(bottom, rows), 16):
                    shade(plane + step, row, size, None)
                for row, size in spans(max(top, rows), bottom, 16):
                    shade(plane + step, row, size, inside)

        if looped:

            def step(index, _):
                some(low + index * together, together)
                return 0

            lax.fori_loop(0, looped, step, 0)
        done = low + looped * together
        if done < high:
            some(done, high - done)

    def copy_to(source, target, sent, received, device):
        return pltpu.make_async_remote_copy(
            src_ref=source,
            dst_ref=target,
            send_sem=sent_sem.at[sent],
            recv_sem=received,
            device_id=device,
            device_id_type=MESH,
        )

    def over(first, second, swap):
        front = [jnp.where(swap, b, a) for a, b in zip(first, second)]
        behind = [jnp.where(swap, a, b) for a, b in zip(first, second)]
        clear = 1.0 - front[3]
        return [f + clear * b for f, b in zip(front, behind)]

    everything = (0, share)

    def load(ref, block, view, part):
        return [ref[block, view, c, pl.ds(*part)] for c in range(4)]

    def store(ref, block, view, part, image):
        for c in range(4):
            ref[block, view, c, pl.ds(*part)] = image[c]

    def each_view(body):
        def step(view, _):
            body(view)
            return 0

        lax.fori_loop(0, views, step, 0)

    def brick(at):
        outer = at in (0, groups - 1)
        lower = at < groups // 2
        mate = at ^ 1
        first = at * planes - 2
        low = {0: 2, 1: 1, 2: 2, 3: 3}[at]
        high = {0: planes + 1, 1: planes + 2, 2: planes + 3, 3: planes + 2}[at]
        reach = (first + high - 1) * margin // total_planes
        extra = -(-reach // 8) * 8
        border = min(margin, -(-(reach + 1) // 8) * 8)
        mate_pair = pl.ds(0, 2) if lower else pl.ds(planes + 2, 2)
        peer_plane = pl.ds(planes + 2, 1) if lower else pl.ds(1, 1)
        edge = {0: planes + 1, 1: 1, 2: planes + 2, 3: 2}[at]
        mate_edge = {0: 1, 3: planes + 2}.get(at, edge)
        others = [2, 3] if lower else [0, 1]
        other = {0: 2, 1: 2, 2: 1, 3: 1}[at]
        peer = {1: 2, 2: 1}.get(at)
        halves = [(share // 2, share // 2), (0, share // 2)]
        parts = {0: halves, 1: [everything], 2: [everything], 3: [everything]}
        hand_at = {
            (block, part): index
            for index, (block, part) in enumerate((block, part) for block in others for part in parts[block])
        }

        def pair_copy():
            source = pl.ds(planes, 2) if lower else pl.ds(2, 2)
            return copy_to(
                volume.at[source, pl.ds(LEAD, rows)],
                volume.at[mate_pair, pl.ds(LEAD, rows)],
                plane_sent,
                halo_sem.at[pair_in],
                (mate, h),
            )

        def peer_copy():
            source = pl.ds(planes + 1, 1) if lower else pl.ds(2, 1)
            target = pl.ds(1, 1) if lower else pl.ds(planes + 2, 1)
            return copy_to(
                volume.at[source, pl.ds(LEAD, rows)],
                volume.at[target, pl.ds(LEAD, rows)],
                plane_sent,
                halo_sem.at[peer_in],
                (peer, h),
            )

        def edge_copy():
            return copy_to(
                volume.at[edge, pl.ds(0, LEAD)],
                volume.at[mate_edge, pl.ds(0, LEAD)],
                edge_sent,
                halo_sem.at[edge_in],
                (mate, h),
            )

        def down_copy(step):
            return copy_to(
                volume.at[own_planes, pl.ds(rows, LEAD)],
                volume.at[own_planes, pl.ds(0, LEAD)],
                down_sent,
                halo_sem.at[down_in],
                (d, h + step),
            )

        def up_copy(step):
            return copy_to(
                volume.at[own_planes, pl.ds(LEAD, border)],
                volume.at[own_planes, pl.ds(end, border)],
                up_sent,
                halo_sem.at[up_in],
                (d, h + step),
            )

        def relay_copy(which, step):
            return copy_to(
                volume.at[which, pl.ds(LEAD, border)],
                volume.at[which, pl.ds(end, border)],
                relay_sent,
                halo_sem.at[relay_in],
                (d, h + step),
            )

        relayed = pl.ds(0, 3)

        def hand(view, block, part):
            index = hand_at[block, part] * views + view
            return copy_to(
                outgoing.at[block, view, :, pl.ds(*part)],
                handed.at[block, view, :, pl.ds(*part)],
                images,
                hand_sem.at[index],
                (mate, h),
            )

        def send(view, block, part):
            slot = 0 if block == mate else views
            return copy_to(
                outgoing.at[block, view, :, pl.ds(*part)],
                incoming.at[at, view, :, pl.ds(*part)],
                images,
                part_sem.at[slot + view],
                (block, h),
            )

        def receive(view, source):
            slot = 0 if source == mate else views
            return copy_to(
                outgoing.at[at, view],
                incoming.at[source, view],
                images,
                part_sem.at[slot + view],
                (source, h),
            )

        def partial(view, block, part):
            step = shear[view]
            backward = reverse[view]
            count = high - low
            size = part[1]
            colour = [jnp.zeros((size, cols), jnp.float32) for _ in range(3)]
            clear = jnp.ones((size, cols), jnp.float32)
            covered = jnp.zeros((size, cols), jnp.float32)
            for i in range(count):
                plane = jnp.where(backward == 1, low + count - 1 - i, low + i)
                offset = lax.div((first + plane) * step, jnp.int32(total_planes))
                offset = jnp.minimum(jnp.maximum(offset, 0), reach)
                rows_at = pl.ds(offset + block * share + part[0], size)
                for c in range(3):
                    colour[c] = colour[c] + clear * fields[c, plane, rows_at]
                covered = covered + clear * fields[3, plane, rows_at]
                clear = 1.0 - covered
            return colour + [covered]

        def send_mate():
            def one(view):
                store(outgoing, mate, view, everything, partial(view, mate, everything))
                send(view, mate, everything).start()

            each_view(one)

        def keep_own():
            each_view(lambda view: store(incoming, at, view, everything, partial(view, at, everything)))

        def hand_over(block, part=everything):
            def one(view):
                store(outgoing, block, view, part, partial(view, block, part))
                hand(view, block, part).start()

            each_view(one)

        def pass_on(block, part=everything):
            def one(view):
                mine = partial(view, block, part)
                hand(view, block, part).wait_recv()
                theirs = load(handed, block, view, part)
                swap = reverse[view] == 1
                merged = over(theirs, mine, swap) if lower else over(mine, theirs, swap)
                store(outgoing, block, view, part, merged)
                send(view, block, part).start()

            each_view(one)

        def begin():
            with jax.named_scope("barrier"):
                pl.semaphore_wait(barrier, expected)
            if outer:
                pair_copy().start()
            else:
                peer_copy().start()

            @pl.when(below)
            def _():
                down_copy(1).start()

            @pl.when(above)
            def _():
                up_copy(-1).start()

        def blank():
            if outer:
                volume[1 if lower else planes + 2] = jnp.zeros(volume.shape[1:], jnp.float32)

            @pl.when(jnp.logical_not(above))
            def _():
                volume[:, :LEAD] = jnp.zeros((planes + 4, LEAD, cols), jnp.float32)

            @pl.when(jnp.logical_not(below))
            def _():
                volume[:, end : end + border] = jnp.zeros((planes + 4, border, cols), jnp.float32)

        def top_landed():
            @pl.when(above)
            def _():
                with jax.named_scope("w_down"):
                    down_copy(-1).wait_recv()

        def bottom_landed():
            @pl.when(below)
            def _():
                with jax.named_scope("w_up"):
                    up_copy(1).wait_recv()

        def edge_landed():
            @pl.when(above)
            def _():
                with jax.named_scope("w_edge"):
                    edge_copy().wait_recv()

        def edge_pass():
            @pl.when(above)
            def _():
                edge_copy().start()

        def relay(which):
            @pl.when(above)
            def _():
                relay_copy(which, -1).start()

        def relay_landed():
            @pl.when(below)
            def _():
                with jax.named_scope("w_relay"):
                    relay_copy(relayed, 1).wait_recv()

        blank()
        if at == 0:
            shade_box(low, high, LEAD, rows - LEAD)
            begin()
            with jax.named_scope("hand2"):
                hand_over(2)
            top_landed()
            edge_pass()
            bottom_landed()
            shade_box(low, high, rows - LEAD, rows + extra)
            with jax.named_scope("hand3"):
                hand_over(3)
            shade_box(low, high, 0, LEAD)
            with jax.named_scope("mate"):
                send_mate()
            keep_own()
        elif at == 3:
            begin()
            shade_box(low, high, LEAD, rows - LEAD)
            with jax.named_scope("hand0b"):
                hand_over(0, halves[0])
            top_landed()
            edge_pass()
            shade_box(low, high, 0, LEAD)
            with jax.named_scope("hand0a"):
                hand_over(0, halves[1])
            bottom_landed()
            shade_box(low, high, rows - LEAD, rows)
            with jax.named_scope("hand1"):
                hand_over(1)
            shade_box(low, high, rows, rows + extra)
            with jax.named_scope("mate"):
                send_mate()
            keep_own()
        else:
            shade_box(3, planes + 1, LEAD, rows - LEAD)
            begin()
            far_edge = planes + 1 if lower else 2
            seam = min(2 if lower else planes + 1, edge)

            def planes_in():
                with jax.named_scope("w_peer"):
                    peer_copy().wait_recv()
                relay(peer_plane)
                shade_box(far_edge, far_edge + 1, LEAD, rows - LEAD)
                with jax.named_scope("w_pair"):
                    pair_copy().wait_recv()
                relay(mate_pair)
                shade_box(seam, seam + 2, LEAD, rows - LEAD)

            def rim():
                top_landed()
                edge_landed()
                shade_box(low, high, 0, LEAD)

            def fringe():
                relay_landed()
                shade_box(seam, seam + 2, rows - LEAD, rows + extra)
                shade_box(far_edge, far_edge + 1, rows - LEAD, rows + extra)

            def bottom():
                bottom_landed()
                shade_box(3, planes + 1, rows - LEAD, rows + extra)

            if lower:
                bottom()
                planes_in()
                shade_box(far_edge, far_edge + 1, rows - LEAD, rows)
                with jax.named_scope("pass2"):
                    pass_on(2)
                rim()
                with jax.named_scope("mate"):
                    send_mate()
                fringe()
                with jax.named_scope("pass3"):
                    pass_on(3)
            else:
                planes_in()
                with jax.named_scope("pass0b"):
                    pass_on(0, halves[0])
                rim()
                with jax.named_scope("pass0a"):
                    pass_on(0, halves[1])
                bottom()
                fringe()
                with jax.named_scope("mate"):
                    send_mate()
                with jax.named_scope("pass1"):
                    pass_on(1)
            keep_own()

        def finish(view):
            swap = reverse[view] == 1
            with jax.named_scope("w_mate"):
                receive(view, mate).wait_recv()
            mine, theirs = (load(incoming, source, view, everything) for source in (at, mate))
            near = over(mine, theirs, swap) if at < mate else over(theirs, mine, swap)
            with jax.named_scope("w_other"):
                receive(view, other).wait_recv()
            far = load(incoming, other, view, everything)
            total = over(near, far, swap) if lower else over(far, near, swap)
            for c in range(4):
                out[c, view] = total[c]

        for view in range(views):
            finish(view)

        if outer:
            pair_copy().wait_send()

            @pl.when(above)
            def _():
                edge_copy().wait_send()
        else:
            peer_copy().wait_send()

            @pl.when(above)
            def _():
                relay_copy(relayed, -1).wait_send()

        @pl.when(below)
        def _():
            down_copy(1).wait_send()

        @pl.when(above)
        def _():
            up_copy(-1).wait_send()

        gone = pl.ds(0, groups - 1)
        copy_to(outgoing.at[gone], handed.at[gone], images, hand_sem.at[0], (mate, h)).wait_send()

    for at in range(groups):

        @pl.when(d == at)
        def _():
            brick(at)


def kernel(
    groups,
    towers,
    density,
    light,
    gain,
    bias,
    shear,
    reverse,
    out,
    volume,
    fields,
    outgoing,
    incoming,
    handed,
    local_sem,
    halo_send,
    halo_recv,
    hand_send,
    hand_recv,
    part_send,
    part_recv,
):
    planes, rows, cols = density.shape
    margin = rows // 2
    views = shear.shape[0]
    share = rows // groups
    total_planes = planes * groups
    extinction = EXTINCTION / total_planes
    d = lax.axis_index("depth")
    h = lax.axis_index("height")
    end = LEAD + rows
    tall = end + margin

    own = pltpu.make_async_copy(
        density, volume.at[pl.ds(1, planes), pl.ds(LEAD, rows)], local_sem
    )
    own.start()

    def near(step_d, step_h):
        ok = None
        for at, step, count in ((d, step_d, groups), (h, step_h, towers)):
            if step:
                test = (at + step >= 0) & (at + step < count)
                ok = test if ok is None else ok & test
        return ok, (d + step_d, h + step_h)

    barrier = pltpu.get_barrier_semaphore()
    beside = [(0, 1), (0, -1), (1, 1), (1, -1), (-1, 1), (-1, -1), (1, 0), (-1, 0)]
    if groups > 4:
        beside += [(step * hop, 0) for hop in range(2, groups) for step in (1, -1)]
    expected = jnp.int32(0)
    for step_d, step_h in beside:
        ok, target = near(step_d, step_h)
        expected = expected + jnp.where(ok, 1, 0)

        @pl.when(ok)
        def _(target=target):
            pl.semaphore_signal(barrier, inc=1, device_id=target, device_id_type=MESH)

    pl.semaphore_wait(barrier, expected)

    whole = pl.ds(0, planes)
    inner = pl.ds(1, planes)
    first, last = pl.ds(0, 1), pl.ds(planes - 1, 1)
    low, high = pl.ds(0, 1), pl.ds(planes + 1, 1)
    routes = [
        ((1, 0), last, (0, rows), low, LEAD),
        ((-1, 0), first, (0, rows), high, LEAD),
        ((0, 1), whole, (rows - LEAD, LEAD), inner, 0),
        ((0, -1), whole, (0, margin), inner, end),
        ((1, -1), last, (0, margin), low, end),
        ((-1, -1), first, (0, margin), high, end),
    ]

    def halo(index, reach):
        step, from_planes, (row, count), to_planes, to_row = routes[index]
        return pltpu.make_async_remote_copy(
            src_ref=density.at[from_planes, pl.ds(row, count)],
            dst_ref=volume.at[to_planes, pl.ds(to_row, count)],
            send_sem=halo_send.at[index],
            recv_sem=halo_recv.at[index],
            device_id=reach,
            device_id_type=MESH,
        )

    for index, route in enumerate(routes):
        ok, target = near(*route[0])

        @pl.when(ok)
        def _(index=index, target=target):
            halo(index, target).start()

    @pl.when(d == 0)
    def _():
        volume[0] = jnp.zeros(volume.shape[1:], jnp.float32)

    @pl.when(d == groups - 1)
    def _():
        volume[planes + 1] = jnp.zeros(volume.shape[1:], jnp.float32)

    @pl.when(h == 0)
    def _():
        volume[1 : planes + 1, :LEAD] = jnp.zeros((planes, LEAD, cols), jnp.float32)

    @pl.when(h == towers - 1)
    def _():
        volume[:, end:tall] = jnp.zeros((planes + 2, margin, cols), jnp.float32)

    own.wait()

    lz, ly, lx = light[0], light[1], light[2]
    half_gain = [0.5 * gain[c] for c in range(3)]
    half_bias = [0.5 * bias[c] for c in range(3)]

    def shade(plane, row, count, keep):
        at = LEAD + row
        centre = volume[plane, at : at + count]
        lane = lax.broadcasted_iota(jnp.int32, (count, cols), 1)
        following = jnp.where(lane == cols - 1, 0.0, pltpu.roll(centre, cols - 1, 1))
        previous = jnp.where(lane == 0, 0.0, pltpu.roll(centre, 1, 1))
        dx = following - previous
        dz = volume[plane + 1, at : at + count] - volume[plane - 1, at : at + count]
        dy = volume[plane, at + 1 : at + 1 + count] - volume[plane, at - 1 : at - 1 + count]
        facing = (lz * dz + ly * dy + lx * dx) * lax.rsqrt(4.0 + dz * dz + dy * dy + dx * dx)
        shading = 0.25 + 1.5 * jnp.maximum(facing, 0.0)
        optical = extinction * (
            jnp.maximum(centre, 0.0) + jnp.log1p(jnp.exp(-jnp.abs(centre)))
        )
        opacity = jnp.tanh(0.5 * optical) * (1.0 + jnp.exp(-optical))
        if keep is not None:
            opacity = opacity * keep
        lit = 0.5 * (opacity * shading)
        to = pl.ds(row, count)
        for c in range(3):
            fields[c, plane - 1, to] = lit + lit * jnp.tanh(half_gain[c] * centre + half_bias[c])
        fields[3, plane - 1, to] = opacity

    inside = jnp.where(h < towers - 1, 1.0, 0.0)

    def early(plane, _):
        for row, count in spans(LEAD, rows - LEAD, 16):
            shade(plane, row, count, None)
        return 0

    lax.fori_loop(2, planes, early, 0)

    def landed(index):
        step_d, step_h = routes[index][0]
        ok, source = near(-step_d, -step_h)

        @pl.when(ok)
        def _():
            halo(index, source).wait_recv()

    def shade_low():
        for index in (0, 1, 2):
            landed(index)
        for plane in range(1, planes + 1):
            shade(plane, 0, LEAD, None)
        for row, count in spans(LEAD, rows - LEAD, 16):
            for plane in (1, planes):
                shade(plane, row, count, None)

    def shade_high():
        for index in (3, 4, 5):
            landed(index)

        def bottom(at, _):
            for plane in (2 * at + 1, 2 * at + 2):
                shade(plane, rows - LEAD, LEAD, None)
                for row, count in spans(rows, rows + margin, 16):
                    shade(plane, row, count, inside)
            return 0

        lax.fori_loop(0, planes // 2, bottom, 0)

    first_plane = d * planes

    def partial(view, block):
        step = shear[view]
        backward = reverse[view]
        colour = [jnp.zeros((share, cols), jnp.float32) for _ in range(3)]
        clear = jnp.ones((share, cols), jnp.float32)
        covered = jnp.zeros((share, cols), jnp.float32)
        for i in range(planes):
            plane = i + backward * (planes - 1 - 2 * i)
            offset = lax.div((first_plane + plane) * step, jnp.int32(total_planes))
            at = pl.ds(offset + block * share, share)
            for c in range(3):
                colour[c] = colour[c] + clear * fields[c, plane, at]
            covered = covered + clear * fields[3, plane, at]
            clear = 1.0 - covered
        return colour + [covered]

    odd = lax.rem(d, 2)
    out_step = 2 * odd - 1
    mate = d - out_step
    pair = lax.div(d, 2)
    beyond = odd * (groups - 1 - d) + (1 - odd) * d
    handing = odd * (d - 1) + (1 - odd) * (groups - 2 - d)

    def over(first, second, swap):
        front = [jnp.where(swap, b, a) for a, b in zip(first, second)]
        behind = [jnp.where(swap, a, b) for a, b in zip(first, second)]
        clear = 1.0 - front[3]
        return [f + clear * b for f, b in zip(front, behind)]

    def load(ref, block, view):
        return [ref[block, view, c] for c in range(4)]

    def store(ref, block, view, image):
        for c in range(4):
            ref[block, view, c] = image[c]

    def hand(view, block):
        return pltpu.make_async_remote_copy(
            src_ref=outgoing.at[block, view],
            dst_ref=handed.at[block, view],
            send_sem=hand_send.at[view, block],
            recv_sem=hand_recv.at[view, block],
            device_id=(mate, h),
            device_id_type=MESH,
        )

    def send(view, block):
        return pltpu.make_async_remote_copy(
            src_ref=outgoing.at[block, view],
            dst_ref=incoming.at[d, view],
            send_sem=part_send.at[view, block],
            recv_sem=part_recv.at[view, d],
            device_id=(block, h),
            device_id_type=MESH,
        )

    def receive(view, source):
        return pltpu.make_async_remote_copy(
            src_ref=outgoing.at[source, view],
            dst_ref=incoming.at[source, view],
            send_sem=part_send.at[view, source],
            recv_sem=part_recv.at[view, source],
            device_id=(source, h),
            device_id_type=MESH,
        )

    def each(count, body):
        def step(k, _):
            body(k)
            return 0

        lax.fori_loop(0, count, step, 0)

    def hand_over(view, k):
        block = odd * k + (1 - odd) * (groups - 1 - k)
        store(outgoing, block, view, partial(view, block))
        hand(view, block).start()

    def prepare(view, k):
        block = d + out_step * (1 + k)
        store(outgoing, block, view, partial(view, block))

    def to_mate(view):
        store(outgoing, mate, view, partial(view, mate))
        send(view, mate).start()

    def pass_on(view, k):
        block = odd * (groups - 1 - k) + (1 - odd) * k
        hand(view, block).wait_recv()
        own_part, other = load(outgoing, block, view), load(handed, block, view)
        swap = reverse[view] != odd
        store(outgoing, block, view, over(own_part, other, swap))
        send(view, block).start()

    reach = lax.div((first_plane + planes - 1) * margin, jnp.int32(total_planes))

    def hand_round(early):
        def one(k):
            block = odd * k + (1 - odd) * (groups - 1 - k)
            ready = ((block + 1) * share + reach <= rows - LEAD) & (odd == 1)

            @pl.when(ready if early else jnp.logical_not(ready))
            def _():
                each(views, lambda view: hand_over(view, k))

        each(handing, one)

    shade_low()
    hand_round(True)
    shade_high()
    hand_round(False)
    each(views, to_mate)
    each(views, lambda view: each(beyond, lambda k: prepare(view, k)))
    each(views, lambda view: store(incoming, d, view, partial(view, d)))
    each(beyond, lambda k: each(views, lambda view: pass_on(view, k)))

    def finish(view):
        swap = reverse[view] == 1
        receive(view, mate).wait_recv()
        both = over(load(incoming, d, view), load(incoming, mate, view), reverse[view] != odd)
        store(incoming, 2 * pair + 1, view, both)
        sources = [jnp.where(j > pair, 2 * j, 2 * j + 1) for j in range(groups // 2)]
        for j, source in enumerate(sources):

            @pl.when(j != pair)
            def _():
                receive(view, source).wait_recv()

        total = load(incoming, sources[0], view)
        for source in sources[1:]:
            total = over(total, load(incoming, source, view), swap)
        for c in range(4):
            out[c, view] = total[c]

    for view in range(views):
        finish(view)

    for index, route in enumerate(routes):
        ok, target = near(*route[0])

        @pl.when(ok)
        def _(index=index, target=target):
            halo(index, target).wait_send()

    def sent(view):
        send(view, mate).wait_send()
        each(handing, lambda k: hand(view, d - out_step * (2 + k)).wait_send())
        each(beyond, lambda k: send(view, d + out_step * (1 + k)).wait_send())

    each(views, sent)


def general(groups, towers, density, light, gain, bias, shear, reverse):
    planes, rows, cols = density.shape
    views = shear.shape[0]
    share = rows // groups
    tall = LEAD + rows + rows // 2
    scalars = pl.BlockSpec(memory_space=pltpu.SMEM)
    return pl.pallas_call(
        functools.partial(kernel, groups, towers),
        name="render",
        out_shape=pltpu.VMEM((4, views, share, cols), jnp.float32),
        in_specs=[pl.BlockSpec(memory_space=pltpu.HBM)] + [scalars] * 5,
        out_specs=pl.BlockSpec(memory_space=pltpu.VMEM),
        scratch_shapes=[
            pltpu.VMEM((planes + 2, tall + LEAD, cols), jnp.float32),
            pltpu.VMEM((4, planes, rows + rows // 2, cols), jnp.float32),
            pltpu.VMEM((groups, views, 4, share, cols), jnp.float32),
            pltpu.VMEM((groups, views, 4, share, cols), jnp.float32),
            pltpu.VMEM((groups, views, 4, share, cols), jnp.float32),
            pltpu.SemaphoreType.DMA,
            pltpu.SemaphoreType.DMA((6,)),
            pltpu.SemaphoreType.DMA((6,)),
            pltpu.SemaphoreType.DMA((views, groups)),
            pltpu.SemaphoreType.DMA((views, groups)),
            pltpu.SemaphoreType.DMA((views, groups)),
            pltpu.SemaphoreType.DMA((views, groups)),
        ],
        compiler_params=pltpu.CompilerParams(collective_id=0, has_side_effects=True, vmem_limit_bytes=60 * 1024 * 1024),
    )(density, light, gain, bias, shear, reverse)


def line(towers, density, light, gain, bias, shear, reverse):
    planes, rows, cols = density.shape
    views = shear.shape[0]
    groups = 4
    share = rows // groups
    whole = pl.BlockSpec(memory_space=pltpu.HBM)
    images = pltpu.VMEM((groups, views, 4, share, cols), jnp.float32)
    return pl.pallas_call(
        functools.partial(line_kernel, towers),
        name="render",
        out_shape=pltpu.VMEM((4, views, share, cols), jnp.float32),
        in_specs=[whole] * 6,
        out_specs=pl.BlockSpec(memory_space=pltpu.VMEM),
        scratch_shapes=[pltpu.SMEM(scalar.shape, scalar.dtype) for scalar in (light, gain, bias, shear, reverse)]
        + [
            pltpu.VMEM((planes + 4, LEAD + rows + rows // 2 + LEAD, cols), jnp.float32),
            pltpu.VMEM((4, planes + 4, rows + rows // 2, cols), jnp.float32),
            images,
            images,
            images,
            pltpu.SemaphoreType.DMA((6,)),
            pltpu.SemaphoreType.DMA((6,)),
            pltpu.SemaphoreType.DMA((3 * views,)),
            pltpu.SemaphoreType.DMA((2 * views,)),
        ],
        compiler_params=pltpu.CompilerParams(collective_id=0, has_side_effects=True, vmem_limit_bytes=60 * 1024 * 1024),
    )(density, light, gain, bias, shear, reverse)


def on_device(groups, towers, density, light, gain, bias, shear, reverse):
    planes, rows, _ = density.shape
    if groups == 4 and planes >= 8 and rows % 64 == 0:
        return line(towers, density, light, gain, bias, shear, reverse)
    return general(groups, towers, density, light, gain, bias, shear, reverse)


def solution(mesh):
    groups, towers = mesh.shape["depth"], mesh.shape["height"]
    placed = (P("depth", "height", None), P(), P(), P(), P(), P())
    return jax.shard_map(
        functools.partial(on_device, groups, towers),
        mesh=mesh,
        in_specs=placed,
        out_specs=P(None, None, ("height", "depth"), None),
        check_vma=False,
    )
```

```python
import functools

import jax
import jax.numpy as jnp
from jax import lax
from jax.experimental import pallas as pl
from jax.experimental.pallas import tpu as pltpu
from jax.sharding import PartitionSpec as P

EXTINCTION = 2.5
LEAD = 8
TOGETHER = 6
MESH = pl.DeviceIdType.MESH


def spans(low, high, size):
    return [(at, min(size, high - at)) for at in range(low, high, size)]


def line_kernel(
    towers,
    density,
    light_in,
    gain_in,
    bias_in,
    shear_in,
    reverse_in,
    out,
    light,
    gain,
    bias,
    shear,
    reverse,
    volume,
    fields,
    outgoing,
    incoming,
    handed,
    sent_sem,
    halo_sem,
    hand_sem,
    part_sem,
):
    planes, rows, cols = density.shape
    margin = rows // 2
    views = shear.shape[0]
    groups = 4
    share = rows // groups
    total_planes = planes * groups
    extinction = EXTINCTION / total_planes
    d = lax.axis_index("depth")
    h = lax.axis_index("height")
    above, below = (h - 1 >= 0) & (h - 1 < towers), (h + 1 >= 0) & (h + 1 < towers)
    end = LEAD + rows
    own_planes = pl.ds(2, planes)
    images, plane_sent, edge_sent, down_sent, up_sent, corner_sent = range(6)
    pair_in, peer_in, edge_in, down_in, up_in, pair_corner_in, peer_corner_in = range(7)

    own = pltpu.make_async_copy(
        density, volume.at[own_planes, pl.ds(LEAD, rows)], sent_sem.at[images]
    )
    own.start()
    scalars = [
        pltpu.make_async_copy(source, target, sent_sem.at[1 + index])
        for index, (source, target) in enumerate(
            zip((light_in, gain_in, bias_in, shear_in, reverse_in), (light, gain, bias, shear, reverse))
        )
    ]
    for scalar in scalars:
        scalar.start()

    def valid(step_d, step_h):
        ok = None
        for at, step, count in ((d, step_d, groups), (h, step_h, towers)):
            if step:
                test = (at + step >= 0) & (at + step < count)
                ok = test if ok is None else ok & test
        return ok

    barrier = pltpu.get_barrier_semaphore()
    expected = jnp.int32(0)
    beside = [(1, 0), (-1, 0), (0, 1), (0, -1)]
    greets = {at: list(beside) for at in range(groups)}
    awaits = {at: list(beside) for at in range(groups)}
    for at in (1, 2):
        mate, peer = at ^ 1, 3 - at
        for step_h in (1, -1):
            greets[at].append((mate - at, step_h))
            awaits[mate].append((at - mate, -step_h))
        greets[at].append((peer - at, 1))
        awaits[peer].append((at - peer, -1))
    for at in range(groups):

        for step in greets[at]:

            @pl.when((d == at) & valid(*step))
            def _(step=step):
                pl.semaphore_signal(
                    barrier, inc=1, device_id=(d + step[0], h + step[1]), device_id_type=MESH
                )

        for step in awaits[at]:
            expected = expected + jnp.where((d == at) & valid(*step), 1, 0)

    for scalar in scalars:
        scalar.wait()
    own.wait()

    lz, ly, lx = light[0], light[1], light[2]
    half_gain = [0.5 * gain[c] for c in range(3)]
    half_bias = [0.5 * bias[c] for c in range(3)]
    inside = jnp.where(below, 1.0, 0.0)

    def shade(plane, row, count, keep):
        at = LEAD + row
        centre = volume[plane, at : at + count]
        lane = lax.broadcasted_iota(jnp.int32, (count, cols), 1)
        following = jnp.where(lane == cols - 1, 0.0, pltpu.roll(centre, cols - 1, 1))
        previous = jnp.where(lane == 0, 0.0, pltpu.roll(centre, 1, 1))
        dx = following - previous
        dz = volume[plane + 1, at : at + count] - volume[plane - 1, at : at + count]
        dy = volume[plane, at + 1 : at + 1 + count] - volume[plane, at - 1 : at - 1 + count]
        facing = (lz * dz + ly * dy + lx * dx) * lax.rsqrt(4.0 + dz * dz + dy * dy + dx * dx)
        shading = 0.25 + 1.5 * jnp.maximum(facing, 0.0)
        optical = extinction * (
            jnp.maximum(centre, 0.0) + jnp.log1p(jnp.exp(-jnp.abs(centre)))
        )
        opacity = jnp.tanh(0.5 * optical) * (1.0 + jnp.exp(-optical))
        if keep is not None:
            opacity = opacity * keep
        lit = 0.5 * (opacity * shading)
        to = pl.ds(row, count)
        for c in range(3):
            fields[c, plane, to] = lit + lit * jnp.tanh(half_gain[c] * centre + half_bias[c])
        fields[3, plane, to] = opacity

    def shade_box(low, high, top, bottom):
        tiles = (bottom - top) // 8
        together = max(1, min(high - low, -(-TOGETHER // tiles)))
        looped = (high - low) // together if high - low > together else 0

        def some(plane, count):
            for step in range(count):
                for row, size in spans(top, min(bottom, rows), 16):
                    shade(plane + step, row, size, None)
                for row, size in spans(max(top, rows), bottom, 16):
                    shade(plane + step, row, size, inside)

        if looped:

            def step(index, _):
                some(low + index * together, together)
                return 0

            lax.fori_loop(0, looped, step, 0)
        done = low + looped * together
        if done < high:
            some(done, high - done)

    def copy_to(source, target, sent, received, device):
        return pltpu.make_async_remote_copy(
            src_ref=source,
            dst_ref=target,
            send_sem=sent_sem.at[sent],
            recv_sem=received,
            device_id=device,
            device_id_type=MESH,
        )

    def over(first, second, swap):
        front = [jnp.where(swap, b, a) for a, b in zip(first, second)]
        behind = [jnp.where(swap, a, b) for a, b in zip(first, second)]
        clear = 1.0 - front[3]
        return [f + clear * b for f, b in zip(front, behind)]

    everything = (0, share)

    def load(ref, block, view, part):
        return [ref[block, view, c, pl.ds(*part)] for c in range(4)]

    def store(ref, block, view, part, image):
        for c in range(4):
            ref[block, view, c, pl.ds(*part)] = image[c]

    def each_view(body):
        def step(view, _):
            body(view)
            return 0

        lax.fori_loop(0, views, step, 0)

    def extent(at):
        low = {0: 2, 1: 1, 2: 2, 3: 3}[at]
        high = {0: planes + 1, 1: planes + 2, 2: planes + 3, 3: planes + 2}[at]
        reach = (at * planes + high - 3) * margin // total_planes
        return low, high, reach, min(margin, -(-(reach + 1) // 8) * 8)

    def brick(at):
        outer = at in (0, groups - 1)
        lower = at < groups // 2
        mate = at ^ 1
        first = at * planes - 2
        low, high, reach, border = extent(at)
        extra = -(-reach // 8) * 8
        mate_pair = pl.ds(0, 2) if lower else pl.ds(planes + 2, 2)
        edge = {0: planes + 1, 1: 1, 2: planes + 2, 3: 2}[at]
        mate_edge = {0: 1, 3: planes + 2}.get(at, edge)
        others = [2, 3] if lower else [0, 1]
        other = {0: 2, 1: 2, 2: 1, 3: 1}[at]
        peer = {1: 2, 2: 1}.get(at)
        halves = [(share // 2, share // 2), (0, share // 2)]
        parts = {0: halves, 1: [everything], 2: [everything], 3: [everything]}
        hand_at = {
            (block, part): index
            for index, (block, part) in enumerate((block, part) for block in others for part in parts[block])
        }

        def plane_copy(source, target, take, put, sent, received, device):
            return copy_to(
                volume.at[source, pl.ds(*take)],
                volume.at[target, pl.ds(*put)],
                sent,
                halo_sem.at[received],
                device,
            )

        own_pair = pl.ds(planes, 2) if lower else pl.ds(2, 2)
        own_peer = pl.ds(planes + 1, 1) if lower else pl.ds(2, 1)
        peer_target = pl.ds(1, 1) if lower else pl.ds(planes + 2, 1)
        peer_border = extent(peer)[3] if peer else None
        pair_border = extent(mate)[3] if outer else border
        whole = (LEAD, rows)

        def pair_copy():
            return plane_copy(own_pair, mate_pair, whole, whole, plane_sent, pair_in, (mate, h))

        def peer_copy():
            return plane_copy(own_peer, peer_target, whole, whole, plane_sent, peer_in, (peer, h))

        def pair_corner(step):
            take, put = (LEAD, pair_border), (end, pair_border)
            return plane_copy(own_pair, mate_pair, take, put, corner_sent, pair_corner_in, (d + mate - at, h + step))

        def peer_corner(step, count):
            take, put = (LEAD, count), (end, count)
            return plane_copy(own_peer, peer_target, take, put, corner_sent, peer_corner_in, (d + peer - at, h + step))

        def edge_copy(step):
            take, put = (rows, LEAD), (0, LEAD)
            return plane_copy(edge, mate_edge, take, put, edge_sent, edge_in, (d + mate - at, h + step))

        def down_copy(step):
            return copy_to(
                volume.at[own_planes, pl.ds(rows, LEAD)],
                volume.at[own_planes, pl.ds(0, LEAD)],
                down_sent,
                halo_sem.at[down_in],
                (d, h + step),
            )

        def up_copy(step):
            return copy_to(
                volume.at[own_planes, pl.ds(LEAD, border)],
                volume.at[own_planes, pl.ds(end, border)],
                up_sent,
                halo_sem.at[up_in],
                (d, h + step),
            )

        def hand(view, block, part):
            index = hand_at[block, part] * views + view
            return copy_to(
                outgoing.at[block, view, :, pl.ds(*part)],
                handed.at[block, view, :, pl.ds(*part)],
                images,
                hand_sem.at[index],
                (mate, h),
            )

        def send(view, block, part):
            slot = 0 if block == mate else views
            return copy_to(
                outgoing.at[block, view, :, pl.ds(*part)],
                incoming.at[at, view, :, pl.ds(*part)],
                images,
                part_sem.at[slot + view],
                (block, h),
            )

        def receive(view, source):
            slot = 0 if source == mate else views
            return copy_to(
                outgoing.at[at, view],
                incoming.at[source, view],
                images,
                part_sem.at[slot + view],
                (source, h),
            )

        def partial(view, block, part):
            step = shear[view]
            backward = reverse[view]
            count = high - low
            size = part[1]
            colour = [jnp.zeros((size, cols), jnp.float32) for _ in range(3)]
            clear = jnp.ones((size, cols), jnp.float32)
            covered = jnp.zeros((size, cols), jnp.float32)
            for i in range(count):
                plane = jnp.where(backward == 1, low + count - 1 - i, low + i)
                offset = lax.div((first + plane) * step, jnp.int32(total_planes))
                offset = jnp.minimum(jnp.maximum(offset, 0), reach)
                rows_at = pl.ds(offset + block * share + part[0], size)
                for c in range(3):
                    colour[c] = colour[c] + clear * fields[c, plane, rows_at]
                covered = covered + clear * fields[3, plane, rows_at]
                clear = 1.0 - covered
            return colour + [covered]

        def send_mate():
            def one(view):
                store(outgoing, mate, view, everything, partial(view, mate, everything))
                send(view, mate, everything).start()

            each_view(one)

        def keep_own():
            each_view(lambda view: store(incoming, at, view, everything, partial(view, at, everything)))

        def hand_over(block, part=everything):
            def one(view):
                store(outgoing, block, view, part, partial(view, block, part))
                hand(view, block, part).start()

            each_view(one)

        def pass_on(block, part=everything):
            def one(view):
                mine = partial(view, block, part)
                hand(view, block, part).wait_recv()
                theirs = load(handed, block, view, part)
                swap = reverse[view] == 1
                merged = over(theirs, mine, swap) if lower else over(mine, theirs, swap)
                store(outgoing, block, view, part, merged)
                send(view, block, part).start()

            each_view(one)

        def begin():
            with jax.named_scope("barrier"):
                pl.semaphore_wait(barrier, expected)
            if outer:
                pair_copy().start()
            else:
                peer_copy().start()

            @pl.when(below)
            def _():
                down_copy(1).start()
                if outer:
                    edge_copy(1).start()

            @pl.when(above)
            def _():
                if outer:
                    pair_corner(-1).start()
                else:
                    peer_corner(-1, peer_border).start()
                up_copy(-1).start()

        def blank():
            if outer:
                volume[1 if lower else planes + 2] = jnp.zeros(volume.shape[1:], jnp.float32)

            @pl.when(jnp.logical_not(above))
            def _():
                volume[:, :LEAD] = jnp.zeros((planes + 4, LEAD, cols), jnp.float32)

            @pl.when(jnp.logical_not(below))
            def _():
                volume[:, end : end + border] = jnp.zeros((planes + 4, border, cols), jnp.float32)

        def top_landed():
            @pl.when(above)
            def _():
                with jax.named_scope("w_down"):
                    down_copy(-1).wait_recv()

        def bottom_landed():
            @pl.when(below)
            def _():
                with jax.named_scope("w_up"):
                    up_copy(1).wait_recv()

        def corners_landed():
            @pl.when(below)
            def _():
                with jax.named_scope("w_corner"):
                    peer_corner(1, border).wait_recv()
                    pair_corner(1).wait_recv()

        def edge_landed():
            @pl.when(above)
            def _():
                with jax.named_scope("w_edge"):
                    edge_copy(-1).wait_recv()

        blank()
        if at == 0:
            shade_box(low, high, LEAD, rows - LEAD)
            begin()
            with jax.named_scope("hand2"):
                hand_over(2)
            top_landed()
            bottom_landed()
            shade_box(low, high, rows - LEAD, rows + extra)
            with jax.named_scope("hand3"):
                hand_over(3)
            shade_box(low, high, 0, LEAD)
            with jax.named_scope("mate"):
                send_mate()
            keep_own()
        elif at == 3:
            begin()
            shade_box(low, high, LEAD, rows - LEAD)
            with jax.named_scope("hand0b"):
                hand_over(0, halves[0])
            top_landed()
            shade_box(low, high, 0, LEAD)
            with jax.named_scope("hand0a"):
                hand_over(0, halves[1])
            bottom_landed()
            shade_box(low, high, rows - LEAD, rows)
            with jax.named_scope("hand1"):
                hand_over(1)
            shade_box(low, high, rows, rows + extra)
            with jax.named_scope("mate"):
                send_mate()
            keep_own()
        else:
            shade_box(3, planes + 1, LEAD, rows - LEAD)
            begin()
            far_edge = planes + 1 if lower else 2
            seam = min(2 if lower else planes + 1, edge)

            top_landed()
            shade_box(3, planes + 1, 0, LEAD)
            bottom_landed()
            shade_box(3, planes + 1, rows - LEAD, rows + extra)
            with jax.named_scope("w_peer"):
                peer_copy().wait_recv()
            shade_box(far_edge, far_edge + 1, 0, rows)
            with jax.named_scope("w_pair"):
                pair_copy().wait_recv()
            shade_box(seam, seam + 2, LEAD, rows - LEAD)

            def rim():
                edge_landed()
                shade_box(seam, seam + 2, 0, LEAD)

            def fringe():
                corners_landed()
                shade_box(seam, seam + 2, rows - LEAD, rows + extra)
                shade_box(far_edge, far_edge + 1, rows, rows + extra)

            if lower:
                rim()
                with jax.named_scope("mate"):
                    send_mate()
                with jax.named_scope("pass2"):
                    pass_on(2)
                fringe()
                with jax.named_scope("pass3"):
                    pass_on(3)
            else:
                with jax.named_scope("pass0b"):
                    pass_on(0, halves[0])
                rim()
                fringe()
                with jax.named_scope("mate"):
                    send_mate()
                with jax.named_scope("pass0a"):
                    pass_on(0, halves[1])
                with jax.named_scope("pass1"):
                    pass_on(1)
            keep_own()

        def finish(view):
            swap = reverse[view] == 1
            with jax.named_scope("w_mate"):
                receive(view, mate).wait_recv()
            mine, theirs = (load(incoming, source, view, everything) for source in (at, mate))
            near = over(mine, theirs, swap) if at < mate else over(theirs, mine, swap)
            with jax.named_scope("w_other"):
                receive(view, other).wait_recv()
            far = load(incoming, other, view, everything)
            total = over(near, far, swap) if lower else over(far, near, swap)
            for c in range(4):
                out[c, view] = total[c]

        for view in range(views):
            finish(view)

        if outer:
            pair_copy().wait_send()
        else:
            peer_copy().wait_send()

        @pl.when(below)
        def _():
            down_copy(1).wait_send()
            if outer:
                edge_copy(1).wait_send()

        @pl.when(above)
        def _():
            up_copy(-1).wait_send()
            if outer:
                pair_corner(-1).wait_send()
            else:
                peer_corner(-1, peer_border).wait_send()

        gone = pl.ds(0, groups - 1)
        copy_to(outgoing.at[gone], handed.at[gone], images, hand_sem.at[0], (mate, h)).wait_send()

    for at in range(groups):

        @pl.when(d == at)
        def _():
            brick(at)


def kernel(
    groups,
    towers,
    density,
    light,
    gain,
    bias,
    shear,
    reverse,
    out,
    volume,
    fields,
    outgoing,
    incoming,
    handed,
    local_sem,
    halo_send,
    halo_recv,
    hand_send,
    hand_recv,
    part_send,
    part_recv,
):
    planes, rows, cols = density.shape
    margin = rows // 2
    views = shear.shape[0]
    share = rows // groups
    total_planes = planes * groups
    extinction = EXTINCTION / total_planes
    d = lax.axis_index("depth")
    h = lax.axis_index("height")
    end = LEAD + rows
    tall = end + margin

    own = pltpu.make_async_copy(
        density, volume.at[pl.ds(1, planes), pl.ds(LEAD, rows)], local_sem
    )
    own.start()

    def near(step_d, step_h):
        ok = None
        for at, step, count in ((d, step_d, groups), (h, step_h, towers)):
            if step:
                test = (at + step >= 0) & (at + step < count)
                ok = test if ok is None else ok & test
        return ok, (d + step_d, h + step_h)

    barrier = pltpu.get_barrier_semaphore()
    beside = [(0, 1), (0, -1), (1, 1), (1, -1), (-1, 1), (-1, -1), (1, 0), (-1, 0)]
    if groups > 4:
        beside += [(step * hop, 0) for hop in range(2, groups) for step in (1, -1)]
    expected = jnp.int32(0)
    for step_d, step_h in beside:
        ok, target = near(step_d, step_h)
        expected = expected + jnp.where(ok, 1, 0)

        @pl.when(ok)
        def _(target=target):
            pl.semaphore_signal(barrier, inc=1, device_id=target, device_id_type=MESH)

    pl.semaphore_wait(barrier, expected)

    whole = pl.ds(0, planes)
    inner = pl.ds(1, planes)
    first, last = pl.ds(0, 1), pl.ds(planes - 1, 1)
    low, high = pl.ds(0, 1), pl.ds(planes + 1, 1)
    routes = [
        ((1, 0), last, (0, rows), low, LEAD),
        ((-1, 0), first, (0, rows), high, LEAD),
        ((0, 1), whole, (rows - LEAD, LEAD), inner, 0),
        ((0, -1), whole, (0, margin), inner, end),
        ((1, -1), last, (0, margin), low, end),
        ((-1, -1), first, (0, margin), high, end),
    ]

    def halo(index, reach):
        step, from_planes, (row, count), to_planes, to_row = routes[index]
        return pltpu.make_async_remote_copy(
            src_ref=density.at[from_planes, pl.ds(row, count)],
            dst_ref=volume.at[to_planes, pl.ds(to_row, count)],
            send_sem=halo_send.at[index],
            recv_sem=halo_recv.at[index],
            device_id=reach,
            device_id_type=MESH,
        )

    for index, route in enumerate(routes):
        ok, target = near(*route[0])

        @pl.when(ok)
        def _(index=index, target=target):
            halo(index, target).start()

    @pl.when(d == 0)
    def _():
        volume[0] = jnp.zeros(volume.shape[1:], jnp.float32)

    @pl.when(d == groups - 1)
    def _():
        volume[planes + 1] = jnp.zeros(volume.shape[1:], jnp.float32)

    @pl.when(h == 0)
    def _():
        volume[1 : planes + 1, :LEAD] = jnp.zeros((planes, LEAD, cols), jnp.float32)

    @pl.when(h == towers - 1)
    def _():
        volume[:, end:tall] = jnp.zeros((planes + 2, margin, cols), jnp.float32)

    own.wait()

    lz, ly, lx = light[0], light[1], light[2]
    half_gain = [0.5 * gain[c] for c in range(3)]
    half_bias = [0.5 * bias[c] for c in range(3)]

    def shade(plane, row, count, keep):
        at = LEAD + row
        centre = volume[plane, at : at + count]
        lane = lax.broadcasted_iota(jnp.int32, (count, cols), 1)
        following = jnp.where(lane == cols - 1, 0.0, pltpu.roll(centre, cols - 1, 1))
        previous = jnp.where(lane == 0, 0.0, pltpu.roll(centre, 1, 1))
        dx = following - previous
        dz = volume[plane + 1, at : at + count] - volume[plane - 1, at : at + count]
        dy = volume[plane, at + 1 : at + 1 + count] - volume[plane, at - 1 : at - 1 + count]
        facing = (lz * dz + ly * dy + lx * dx) * lax.rsqrt(4.0 + dz * dz + dy * dy + dx * dx)
        shading = 0.25 + 1.5 * jnp.maximum(facing, 0.0)
        optical = extinction * (
            jnp.maximum(centre, 0.0) + jnp.log1p(jnp.exp(-jnp.abs(centre)))
        )
        opacity = jnp.tanh(0.5 * optical) * (1.0 + jnp.exp(-optical))
        if keep is not None:
            opacity = opacity * keep
        lit = 0.5 * (opacity * shading)
        to = pl.ds(row, count)
        for c in range(3):
            fields[c, plane - 1, to] = lit + lit * jnp.tanh(half_gain[c] * centre + half_bias[c])
        fields[3, plane - 1, to] = opacity

    inside = jnp.where(h < towers - 1, 1.0, 0.0)

    def early(plane, _):
        for row, count in spans(LEAD, rows - LEAD, 16):
            shade(plane, row, count, None)
        return 0

    lax.fori_loop(2, planes, early, 0)

    def landed(index):
        step_d, step_h = routes[index][0]
        ok, source = near(-step_d, -step_h)

        @pl.when(ok)
        def _():
            halo(index, source).wait_recv()

    def shade_low():
        for index in (0, 1, 2):
            landed(index)
        for plane in range(1, planes + 1):
            shade(plane, 0, LEAD, None)
        for row, count in spans(LEAD, rows - LEAD, 16):
            for plane in (1, planes):
                shade(plane, row, count, None)

    def shade_high():
        for index in (3, 4, 5):
            landed(index)

        def bottom(at, _):
            for plane in (2 * at + 1, 2 * at + 2):
                shade(plane, rows - LEAD, LEAD, None)
                for row, count in spans(rows, rows + margin, 16):
                    shade(plane, row, count, inside)
            return 0

        lax.fori_loop(0, planes // 2, bottom, 0)

    first_plane = d * planes

    def partial(view, block):
        step = shear[view]
        backward = reverse[view]
        colour = [jnp.zeros((share, cols), jnp.float32) for _ in range(3)]
        clear = jnp.ones((share, cols), jnp.float32)
        covered = jnp.zeros((share, cols), jnp.float32)
        for i in range(planes):
            plane = i + backward * (planes - 1 - 2 * i)
            offset = lax.div((first_plane + plane) * step, jnp.int32(total_planes))
            at = pl.ds(offset + block * share, share)
            for c in range(3):
                colour[c] = colour[c] + clear * fields[c, plane, at]
            covered = covered + clear * fields[3, plane, at]
            clear = 1.0 - covered
        return colour + [covered]

    odd = lax.rem(d, 2)
    out_step = 2 * odd - 1
    mate = d - out_step
    pair = lax.div(d, 2)
    beyond = odd * (groups - 1 - d) + (1 - odd) * d
    handing = odd * (d - 1) + (1 - odd) * (groups - 2 - d)

    def over(first, second, swap):
        front = [jnp.where(swap, b, a) for a, b in zip(first, second)]
        behind = [jnp.where(swap, a, b) for a, b in zip(first, second)]
        clear = 1.0 - front[3]
        return [f + clear * b for f, b in zip(front, behind)]

    def load(ref, block, view):
        return [ref[block, view, c] for c in range(4)]

    def store(ref, block, view, image):
        for c in range(4):
            ref[block, view, c] = image[c]

    def hand(view, block):
        return pltpu.make_async_remote_copy(
            src_ref=outgoing.at[block, view],
            dst_ref=handed.at[block, view],
            send_sem=hand_send.at[view, block],
            recv_sem=hand_recv.at[view, block],
            device_id=(mate, h),
            device_id_type=MESH,
        )

    def send(view, block):
        return pltpu.make_async_remote_copy(
            src_ref=outgoing.at[block, view],
            dst_ref=incoming.at[d, view],
            send_sem=part_send.at[view, block],
            recv_sem=part_recv.at[view, d],
            device_id=(block, h),
            device_id_type=MESH,
        )

    def receive(view, source):
        return pltpu.make_async_remote_copy(
            src_ref=outgoing.at[source, view],
            dst_ref=incoming.at[source, view],
            send_sem=part_send.at[view, source],
            recv_sem=part_recv.at[view, source],
            device_id=(source, h),
            device_id_type=MESH,
        )

    def each(count, body):
        def step(k, _):
            body(k)
            return 0

        lax.fori_loop(0, count, step, 0)

    def hand_over(view, k):
        block = odd * k + (1 - odd) * (groups - 1 - k)
        store(outgoing, block, view, partial(view, block))
        hand(view, block).start()

    def prepare(view, k):
        block = d + out_step * (1 + k)
        store(outgoing, block, view, partial(view, block))

    def to_mate(view):
        store(outgoing, mate, view, partial(view, mate))
        send(view, mate).start()

    def pass_on(view, k):
        block = odd * (groups - 1 - k) + (1 - odd) * k
        hand(view, block).wait_recv()
        own_part, other = load(outgoing, block, view), load(handed, block, view)
        swap = reverse[view] != odd
        store(outgoing, block, view, over(own_part, other, swap))
        send(view, block).start()

    reach = lax.div((first_plane + planes - 1) * margin, jnp.int32(total_planes))

    def hand_round(early):
        def one(k):
            block = odd * k + (1 - odd) * (groups - 1 - k)
            ready = ((block + 1) * share + reach <= rows - LEAD) & (odd == 1)

            @pl.when(ready if early else jnp.logical_not(ready))
            def _():
                each(views, lambda view: hand_over(view, k))

        each(handing, one)

    shade_low()
    hand_round(True)
    shade_high()
    hand_round(False)
    each(views, to_mate)
    each(views, lambda view: each(beyond, lambda k: prepare(view, k)))
    each(views, lambda view: store(incoming, d, view, partial(view, d)))
    each(beyond, lambda k: each(views, lambda view: pass_on(view, k)))

    def finish(view):
        swap = reverse[view] == 1
        receive(view, mate).wait_recv()
        both = over(load(incoming, d, view), load(incoming, mate, view), reverse[view] != odd)
        store(incoming, 2 * pair + 1, view, both)
        sources = [jnp.where(j > pair, 2 * j, 2 * j + 1) for j in range(groups // 2)]
        for j, source in enumerate(sources):

            @pl.when(j != pair)
            def _():
                receive(view, source).wait_recv()

        total = load(incoming, sources[0], view)
        for source in sources[1:]:
            total = over(total, load(incoming, source, view), swap)
        for c in range(4):
            out[c, view] = total[c]

    for view in range(views):
        finish(view)

    for index, route in enumerate(routes):
        ok, target = near(*route[0])

        @pl.when(ok)
        def _(index=index, target=target):
            halo(index, target).wait_send()

    def sent(view):
        send(view, mate).wait_send()
        each(handing, lambda k: hand(view, d - out_step * (2 + k)).wait_send())
        each(beyond, lambda k: send(view, d + out_step * (1 + k)).wait_send())

    each(views, sent)


def general(groups, towers, density, light, gain, bias, shear, reverse):
    planes, rows, cols = density.shape
    views = shear.shape[0]
    share = rows // groups
    tall = LEAD + rows + rows // 2
    scalars = pl.BlockSpec(memory_space=pltpu.SMEM)
    return pl.pallas_call(
        functools.partial(kernel, groups, towers),
        name="render",
        out_shape=pltpu.VMEM((4, views, share, cols), jnp.float32),
        in_specs=[pl.BlockSpec(memory_space=pltpu.HBM)] + [scalars] * 5,
        out_specs=pl.BlockSpec(memory_space=pltpu.VMEM),
        scratch_shapes=[
            pltpu.VMEM((planes + 2, tall + LEAD, cols), jnp.float32),
            pltpu.VMEM((4, planes, rows + rows // 2, cols), jnp.float32),
            pltpu.VMEM((groups, views, 4, share, cols), jnp.float32),
            pltpu.VMEM((groups, views, 4, share, cols), jnp.float32),
            pltpu.VMEM((groups, views, 4, share, cols), jnp.float32),
            pltpu.SemaphoreType.DMA,
            pltpu.SemaphoreType.DMA((6,)),
            pltpu.SemaphoreType.DMA((6,)),
            pltpu.SemaphoreType.DMA((views, groups)),
            pltpu.SemaphoreType.DMA((views, groups)),
            pltpu.SemaphoreType.DMA((views, groups)),
            pltpu.SemaphoreType.DMA((views, groups)),
        ],
        compiler_params=pltpu.CompilerParams(collective_id=0, has_side_effects=True, vmem_limit_bytes=60 * 1024 * 1024),
    )(density, light, gain, bias, shear, reverse)


def line(towers, density, light, gain, bias, shear, reverse):
    planes, rows, cols = density.shape
    views = shear.shape[0]
    groups = 4
    share = rows // groups
    whole = pl.BlockSpec(memory_space=pltpu.HBM)
    images = pltpu.VMEM((groups, views, 4, share, cols), jnp.float32)
    return pl.pallas_call(
        functools.partial(line_kernel, towers),
        name="render",
        out_shape=pltpu.VMEM((4, views, share, cols), jnp.float32),
        in_specs=[whole] * 6,
        out_specs=pl.BlockSpec(memory_space=pltpu.VMEM),
        scratch_shapes=[pltpu.SMEM(scalar.shape, scalar.dtype) for scalar in (light, gain, bias, shear, reverse)]
        + [
            pltpu.VMEM((planes + 4, LEAD + rows + rows // 2 + LEAD, cols), jnp.float32),
            pltpu.VMEM((4, planes + 4, rows + rows // 2, cols), jnp.float32),
            images,
            images,
            images,
            pltpu.SemaphoreType.DMA((6,)),
            pltpu.SemaphoreType.DMA((7,)),
            pltpu.SemaphoreType.DMA((3 * views,)),
            pltpu.SemaphoreType.DMA((2 * views,)),
        ],
        compiler_params=pltpu.CompilerParams(collective_id=0, has_side_effects=True, vmem_limit_bytes=60 * 1024 * 1024),
    )(density, light, gain, bias, shear, reverse)


def on_device(groups, towers, density, light, gain, bias, shear, reverse):
    planes, rows, _ = density.shape
    if groups == 4 and planes >= 8 and rows % 64 == 0:
        return line(towers, density, light, gain, bias, shear, reverse)
    return general(groups, towers, density, light, gain, bias, shear, reverse)


def solution(mesh):
    groups, towers = mesh.shape["depth"], mesh.shape["height"]
    placed = (P("depth", "height", None), P(), P(), P(), P(), P())
    return jax.shard_map(
        functools.partial(on_device, groups, towers),
        mesh=mesh,
        in_specs=placed,
        out_specs=P(None, None, ("height", "depth"), None),
        check_vma=False,
    )
```

```python
import functools

import jax
import jax.numpy as jnp
from jax import lax
from jax.experimental import pallas as pl
from jax.experimental.pallas import tpu as pltpu
from jax.sharding import PartitionSpec as P

EXTINCTION = 2.5
LEAD = 8
TOGETHER = 6
MESH = pl.DeviceIdType.MESH


def spans(low, high, size):
    return [(at, min(size, high - at)) for at in range(low, high, size)]


def line_kernel(
    towers,
    density,
    light_in,
    gain_in,
    bias_in,
    shear_in,
    reverse_in,
    out,
    light,
    gain,
    bias,
    shear,
    reverse,
    volume,
    fields,
    outgoing,
    incoming,
    handed,
    sent_sem,
    halo_sem,
    hand_sem,
    part_sem,
):
    planes, rows, cols = density.shape
    margin = rows // 2
    views = shear.shape[0]
    groups = 4
    share = rows // groups
    total_planes = planes * groups
    extinction = EXTINCTION / total_planes
    d = lax.axis_index("depth")
    h = lax.axis_index("height")
    above, below = (h - 1 >= 0) & (h - 1 < towers), (h + 1 >= 0) & (h + 1 < towers)
    end = LEAD + rows
    own_planes = pl.ds(2, planes)
    images, plane_sent, edge_sent, down_sent, up_sent, corner_sent, rest_sent = range(7)
    slab_sent, slab_edge_sent = edge_sent, rest_sent
    pair_in, peer_in, edge_in, down_in, up_in, pair_corner_in, peer_corner_in, rest_in = range(8)
    slab_in, slab_edge_in, slab_end_in = pair_in, edge_in, peer_in

    own = pltpu.make_async_copy(
        density, volume.at[own_planes, pl.ds(LEAD, rows)], sent_sem.at[images]
    )
    own.start()
    scalars = [
        pltpu.make_async_copy(source, target, sent_sem.at[1 + index])
        for index, (source, target) in enumerate(
            zip((light_in, gain_in, bias_in, shear_in, reverse_in), (light, gain, bias, shear, reverse))
        )
    ]
    for scalar in scalars:
        scalar.start()

    def valid(step_d, step_h):
        ok = None
        for at, step, count in ((d, step_d, groups), (h, step_h, towers)):
            if step:
                test = (at + step >= 0) & (at + step < count)
                ok = test if ok is None else ok & test
        return ok

    barrier = pltpu.get_barrier_semaphore()
    expected = jnp.int32(0)
    beside = [(1, 0), (-1, 0), (0, 1), (0, -1)]
    greets = {at: list(beside) for at in range(groups)}
    awaits = {at: list(beside) for at in range(groups)}
    for at in (1, 2):
        mate, peer = at ^ 1, 3 - at
        for step_h in (1, -1):
            greets[at].append((mate - at, step_h))
            awaits[mate].append((at - mate, -step_h))
        greets[at].append((peer - at, 1))
        awaits[peer].append((at - peer, -1))
    for at, *step in ((0, 1, -1), (0, 2, 0)):
        greets[at].append(tuple(step))
        awaits[at + step[0]].append((-step[0], -step[1]))
    for at in range(groups):

        for step in greets[at]:

            @pl.when((d == at) & valid(*step))
            def _(step=step):
                pl.semaphore_signal(
                    barrier, inc=1, device_id=(d + step[0], h + step[1]), device_id_type=MESH
                )

        for step in awaits[at]:
            expected = expected + jnp.where((d == at) & valid(*step), 1, 0)

    for scalar in scalars:
        scalar.wait()
    own.wait()

    lz, ly, lx = light[0], light[1], light[2]
    half_gain = [0.5 * gain[c] for c in range(3)]
    half_bias = [0.5 * bias[c] for c in range(3)]
    inside = jnp.where(below, 1.0, 0.0)

    def shade(plane, row, count, keep):
        at = LEAD + row
        centre = volume[plane, at : at + count]
        lane = lax.broadcasted_iota(jnp.int32, (count, cols), 1)
        following = jnp.where(lane == cols - 1, 0.0, pltpu.roll(centre, cols - 1, 1))
        previous = jnp.where(lane == 0, 0.0, pltpu.roll(centre, 1, 1))
        dx = following - previous
        dz = volume[plane + 1, at : at + count] - volume[plane - 1, at : at + count]
        dy = volume[plane, at + 1 : at + 1 + count] - volume[plane, at - 1 : at - 1 + count]
        facing = (lz * dz + ly * dy + lx * dx) * lax.rsqrt(4.0 + dz * dz + dy * dy + dx * dx)
        shading = 0.25 + 1.5 * jnp.maximum(facing, 0.0)
        optical = extinction * (
            jnp.maximum(centre, 0.0) + jnp.log1p(jnp.exp(-jnp.abs(centre)))
        )
        opacity = jnp.tanh(0.5 * optical) * (1.0 + jnp.exp(-optical))
        if keep is not None:
            opacity = opacity * keep
        lit = 0.5 * (opacity * shading)
        to = pl.ds(row, count)
        for c in range(3):
            fields[c, plane, to] = lit + lit * jnp.tanh(half_gain[c] * centre + half_bias[c])
        fields[3, plane, to] = opacity

    def shade_box(low, high, top, bottom):
        tiles = (bottom - top) // 8
        together = max(1, min(high - low, -(-TOGETHER // tiles)))
        looped = (high - low) // together if high - low > together else 0

        def some(plane, count):
            for step in range(count):
                for row, size in spans(top, min(bottom, rows), 16):
                    shade(plane + step, row, size, None)
                for row, size in spans(max(top, rows), bottom, 16):
                    shade(plane + step, row, size, inside)

        if looped:

            def step(index, _):
                some(low + index * together, together)
                return 0

            lax.fori_loop(0, looped, step, 0)
        done = low + looped * together
        if done < high:
            some(done, high - done)

    def copy_to(source, target, sent, received, device):
        return pltpu.make_async_remote_copy(
            src_ref=source,
            dst_ref=target,
            send_sem=sent_sem.at[sent],
            recv_sem=received,
            device_id=device,
            device_id_type=MESH,
        )

    def over(first, second, swap):
        front = [jnp.where(swap, b, a) for a, b in zip(first, second)]
        behind = [jnp.where(swap, a, b) for a, b in zip(first, second)]
        clear = 1.0 - front[3]
        return [f + clear * b for f, b in zip(front, behind)]

    everything = (0, share)
    distant = (lax.rem(h, max(towers // 2, 1)) == 0) & (h > 0)
    some, rest = (0, views // 2), (views // 2, views)

    def load(ref, block, view, part):
        return [ref[block, view, c, pl.ds(*part)] for c in range(4)]

    def store(ref, block, view, part, image):
        for c in range(4):
            ref[block, view, c, pl.ds(*part)] = image[c]

    def each_view(body, start=0, stop=views):
        def step(view, _):
            body(view)
            return 0

        lax.fori_loop(start, stop, step, 0)

    def extent(at):
        low = {0: 2, 1: 1, 2: 2, 3: 3}[at]
        high = {0: planes + 1, 1: planes + 2, 2: planes + 3, 3: planes + 2}[at]
        reach = (at * planes + high - 3) * margin // total_planes
        return low, high, reach, min(margin, -(-(reach + 1) // 8) * 8)

    def brick(at):
        outer = at in (0, groups - 1)
        lower = at < groups // 2
        mate = at ^ 1
        first = at * planes - 2
        low, high, reach, border = extent(at)
        extra = -(-reach // 8) * 8
        mate_pair = pl.ds(0, 2) if lower else pl.ds(planes + 2, 2)
        edge = {0: planes + 1, 1: 1, 2: planes + 2, 3: 2}[at]
        mate_edge = {0: 1, 3: planes + 2}.get(at, edge)
        others = [2, 3] if lower else [0, 1]
        other = {0: 2, 1: 2, 2: 1, 3: 1}[at]
        peer = {1: 2, 2: 1}.get(at)
        halves = [(share // 2, share // 2), (0, share // 2)]
        parts = {0: halves, 1: [everything], 2: [everything], 3: [everything]}
        hand_at = {
            (block, part): index
            for index, (block, part) in enumerate((block, part) for block in others for part in parts[block])
        }

        def plane_copy(source, target, take, put, sent, received, device):
            return copy_to(
                volume.at[source, pl.ds(*take)],
                volume.at[target, pl.ds(*put)],
                sent,
                halo_sem.at[received],
                device,
            )

        own_pair = pl.ds(planes, 2) if lower else pl.ds(2, 2)
        own_peer = pl.ds(planes + 1, 1) if lower else pl.ds(2, 1)
        peer_target = pl.ds(1, 1) if lower else pl.ds(planes + 2, 1)
        peer_border = extent(peer)[3] if peer else None
        pair_border = extent(mate)[3] if outer else border
        whole = (LEAD, rows)

        cut = rows - share
        soon, after = ((LEAD + share, cut), (LEAD, share)) if lower else ((LEAD, cut), (LEAD + cut, share))

        def pair_copy():
            return plane_copy(own_pair, mate_pair, soon, soon, plane_sent, pair_in, (mate, h))

        def pair_rest():
            return plane_copy(own_pair, mate_pair, after, after, rest_sent, rest_in, (mate, h))

        def peer_copy():
            return plane_copy(own_peer, peer_target, whole, whole, plane_sent, peer_in, (peer, h))

        def pair_corner(step):
            take, put = (LEAD, pair_border), (end, pair_border)
            return plane_copy(own_pair, mate_pair, take, put, corner_sent, pair_corner_in, (d + mate - at, h + step))

        def peer_corner(step, count):
            take, put = (LEAD, count), (end, count)
            return plane_copy(own_peer, peer_target, take, put, corner_sent, peer_corner_in, (d + peer - at, h + step))

        def edge_copy(step):
            take, put = (rows, LEAD), (0, LEAD)
            return plane_copy(edge, mate_edge, take, put, edge_sent, edge_in, (d + mate - at, h + step))

        span_high = 2 * planes + 2
        span_reach = extent(1)[2]
        span_rows = share + extent(1)[3]
        slab = pl.ds(planes + 2, planes)
        slab_end = pl.ds(2 * planes + 2, 1)

        def slab_copy():
            take = (LEAD, span_rows)
            return plane_copy(own_planes, slab, take, take, slab_sent, slab_in, (0 if at else 1, h))

        def slab_edge_copy(step):
            take, put = (rows, LEAD), (0, LEAD)
            return plane_copy(own_planes, slab, take, put, slab_edge_sent, slab_edge_in, (d + (-1 if at else 1), h + step))

        def slab_end_copy():
            take = (LEAD, span_rows)
            return plane_copy(pl.ds(2, 1), slab_end, take, take, slab_sent, slab_end_in, (0 if at else 2, h))

        def down_copy(step):
            return copy_to(
                volume.at[own_planes, pl.ds(rows, LEAD)],
                volume.at[own_planes, pl.ds(0, LEAD)],
                down_sent,
                halo_sem.at[down_in],
                (d, h + step),
            )

        def up_copy(step):
            return copy_to(
                volume.at[own_planes, pl.ds(LEAD, border)],
                volume.at[own_planes, pl.ds(end, border)],
                up_sent,
                halo_sem.at[up_in],
                (d, h + step),
            )

        def hand(view, block, part):
            index = hand_at[block, part] * views + view
            return copy_to(
                outgoing.at[block, view, :, pl.ds(*part)],
                handed.at[block, view, :, pl.ds(*part)],
                images,
                hand_sem.at[index],
                (mate, h),
            )

        def send(view, block, part):
            slot = 0 if block == mate else views
            return copy_to(
                outgoing.at[block, view, :, pl.ds(*part)],
                incoming.at[at, view, :, pl.ds(*part)],
                images,
                part_sem.at[slot + view],
                (block, h),
            )

        def receive(view, source):
            slot = 0 if source == mate else views
            return copy_to(
                outgoing.at[at, view],
                incoming.at[source, view],
                images,
                part_sem.at[slot + view],
                (source, h),
            )

        def partial(view, block, part, high=high, reach=reach):
            step = shear[view]
            backward = reverse[view]
            count = high - low
            size = part[1]
            colour = [jnp.zeros((size, cols), jnp.float32) for _ in range(3)]
            clear = jnp.ones((size, cols), jnp.float32)
            covered = jnp.zeros((size, cols), jnp.float32)
            for i in range(count):
                plane = jnp.where(backward == 1, low + count - 1 - i, low + i)
                offset = lax.div((first + plane) * step, jnp.int32(total_planes))
                offset = jnp.minimum(jnp.maximum(offset, 0), reach)
                rows_at = pl.ds(offset + block * share + part[0], size)
                for c in range(3):
                    colour[c] = colour[c] + clear * fields[c, plane, rows_at]
                covered = covered + clear * fields[3, plane, rows_at]
                clear = 1.0 - covered
            return colour + [covered]

        def send_mate():
            def one(view):
                store(outgoing, mate, view, everything, partial(view, mate, everything))
                send(view, mate, everything).start()

            each_view(one)

        def keep_own():
            span = (span_high, span_reach) if at == 0 else (high, reach)
            each_view(lambda view: store(incoming, at, view, everything, partial(view, at, everything, *span)))

        def hand_over(block, part=everything, which=(0, views)):
            def one(view):
                store(outgoing, block, view, part, partial(view, block, part))
                hand(view, block, part).start()

            each_view(one, *which)

        def pass_on(block, part=everything, which=(0, views)):
            def one(view):
                mine = partial(view, block, part)
                hand(view, block, part).wait_recv()
                theirs = load(handed, block, view, part)
                swap = reverse[view] == 1
                merged = over(theirs, mine, swap) if lower else over(mine, theirs, swap)
                store(outgoing, block, view, part, merged)
                send(view, block, part).start()

            each_view(one, *which)

        def begin():
            with jax.named_scope("barrier"):
                pl.semaphore_wait(barrier, expected)
            if outer:
                pair_copy().start()
            else:
                peer_copy().start()
                (slab_copy if lower else slab_end_copy)().start()

            @pl.when(below)
            def _():
                down_copy(1).start()
                if outer:
                    edge_copy(1).start()
                if at == 1:
                    slab_edge_copy(1).start()

            @pl.when(above)
            def _():
                if outer:
                    pair_corner(-1).start()
                else:
                    peer_corner(-1, peer_border).start()
                up_copy(-1).start()

        def blank():
            if outer:
                volume[1 if lower else planes + 2] = jnp.zeros(volume.shape[1:], jnp.float32)

            @pl.when(jnp.logical_not(above))
            def _():
                volume[:, :LEAD] = jnp.zeros((2 * planes + 3, LEAD, cols), jnp.float32)

            @pl.when(jnp.logical_not(below))
            def _():
                volume[:, end : end + border] = jnp.zeros((2 * planes + 3, border, cols), jnp.float32)

        def top_landed():
            @pl.when(above)
            def _():
                with jax.named_scope("w_down"):
                    down_copy(-1).wait_recv()

        def bottom_landed():
            @pl.when(below)
            def _():
                with jax.named_scope("w_up"):
                    up_copy(1).wait_recv()

        def corners_landed():
            @pl.when(below)
            def _():
                with jax.named_scope("w_corner"):
                    peer_corner(1, border).wait_recv()
                    pair_corner(1).wait_recv()

        def edge_landed():
            @pl.when(above)
            def _():
                with jax.named_scope("w_edge"):
                    edge_copy(-1).wait_recv()

        blank()
        if at == 0:
            shade_box(low, high, LEAD, rows - LEAD)
            begin()
            with jax.named_scope("hand2"):
                hand_over(2)
            pair_rest().start()
            top_landed()
            bottom_landed()
            shade_box(low, high, rows - LEAD, rows + extra)
            with jax.named_scope("hand3"):
                hand_over(3)
            shade_box(low, high, 0, LEAD)
            with jax.named_scope("mate"):
                send_mate()
            with jax.named_scope("w_slab"):
                slab_copy().wait_recv()

                @pl.when(above)
                def _():
                    slab_edge_copy(-1).wait_recv()

                slab_end_copy().wait_recv()
            shade_box(high, span_high, 0, -(-(share + span_reach) // 8) * 8)
            keep_own()
        elif at == 3:
            begin()
            shade_box(low, high, LEAD, rows - LEAD)
            with jax.named_scope("hand0b"):
                hand_over(0, halves[0])
            pair_rest().start()
            def early():
                top_landed()
                shade_box(low, high, 0, LEAD)
                with jax.named_scope("hand0a"):
                    hand_over(0, halves[1])

            def late(which):
                with jax.named_scope("hand1"):
                    hand_over(1, everything, which)

            def bottom():
                bottom_landed()
                shade_box(low, high, rows - LEAD, rows)

            @pl.when(distant)
            def _():
                bottom()
                late(some)
                early()
                late(rest)

            @pl.when(jnp.logical_not(distant))
            def _():
                early()
                bottom()
                late((0, views))

            shade_box(low, high, rows, rows + extra)
            with jax.named_scope("mate"):
                send_mate()
            keep_own()
        else:
            shade_box(3, planes + 1, LEAD, rows - LEAD)
            begin()
            far_edge = planes + 1 if lower else 2
            seam = min(2 if lower else planes + 1, edge)

            top_landed()
            shade_box(3, planes + 1, 0, LEAD)
            bottom_landed()
            shade_box(3, planes + 1, rows - LEAD, rows + extra)
            with jax.named_scope("w_peer"):
                peer_copy().wait_recv()
            shade_box(far_edge, far_edge + 1, 0, rows)
            with jax.named_scope("w_pair"):
                pair_copy().wait_recv()
            if lower:
                shade_box(seam, seam + 2, share + LEAD, rows - LEAD)
            else:
                shade_box(seam, seam + 2, LEAD, rows - share - LEAD)

            def rim():
                with jax.named_scope("w_rest"):
                    pair_rest().wait_recv()
                edge_landed()
                if lower:
                    shade_box(seam, seam + 2, 0, share + LEAD)
                else:
                    shade_box(seam, seam + 2, 0, LEAD)
                    shade_box(seam, seam + 2, rows - share - LEAD, rows - LEAD)

            def fringe():
                corners_landed()
                shade_box(seam, seam + 2, rows - LEAD, rows + extra)
                shade_box(far_edge, far_edge + 1, rows, rows + extra)

            if lower:
                with jax.named_scope("pass2"):
                    pass_on(2)
                rim()
                fringe()
                with jax.named_scope("pass3"):
                    pass_on(3)
            else:
                with jax.named_scope("pass0b"):
                    pass_on(0, halves[0])
                rim()
                fringe()
                with jax.named_scope("mate"):
                    send_mate()

                @pl.when(distant)
                def _():
                    pass_on(1, everything, some)
                    with jax.named_scope("pass0a"):
                        pass_on(0, halves[1])
                    with jax.named_scope("pass1"):
                        pass_on(1, everything, rest)

                @pl.when(jnp.logical_not(distant))
                def _():
                    with jax.named_scope("pass0a"):
                        pass_on(0, halves[1])
                    with jax.named_scope("pass1"):
                        pass_on(1)

            keep_own()

        def finish(view):
            swap = reverse[view] == 1
            near = load(incoming, at, view, everything)
            if at != 0:
                with jax.named_scope("w_mate"):
                    receive(view, mate).wait_recv()
                theirs = load(incoming, mate, view, everything)
                near = over(near, theirs, swap) if at < mate else over(theirs, near, swap)
            with jax.named_scope("w_other"):
                receive(view, other).wait_recv()
            far = load(incoming, other, view, everything)
            total = over(near, far, swap) if lower else over(far, near, swap)
            for c in range(4):
                out[c, view] = total[c]

        for view in range(views):
            finish(view)

        if outer:
            pair_copy().wait_send()
            pair_rest().wait_send()
        else:
            peer_copy().wait_send()
            (slab_copy if lower else slab_end_copy)().wait_send()

        @pl.when(below)
        def _():
            down_copy(1).wait_send()
            if outer:
                edge_copy(1).wait_send()
            if at == 1:
                slab_edge_copy(1).wait_send()

        @pl.when(above)
        def _():
            up_copy(-1).wait_send()
            if outer:
                pair_corner(-1).wait_send()
            else:
                peer_corner(-1, peer_border).wait_send()

        gone = pl.ds(0, groups - 2 if at == 1 else groups - 1)
        copy_to(outgoing.at[gone], handed.at[gone], images, hand_sem.at[0], (mate, h)).wait_send()

    for at in range(groups):

        @pl.when(d == at)
        def _():
            brick(at)


def kernel(
    groups,
    towers,
    density,
    light,
    gain,
    bias,
    shear,
    reverse,
    out,
    volume,
    fields,
    outgoing,
    incoming,
    handed,
    local_sem,
    halo_send,
    halo_recv,
    hand_send,
    hand_recv,
    part_send,
    part_recv,
):
    planes, rows, cols = density.shape
    margin = rows // 2
    views = shear.shape[0]
    share = rows // groups
    total_planes = planes * groups
    extinction = EXTINCTION / total_planes
    d = lax.axis_index("depth")
    h = lax.axis_index("height")
    end = LEAD + rows
    tall = end + margin

    own = pltpu.make_async_copy(
        density, volume.at[pl.ds(1, planes), pl.ds(LEAD, rows)], local_sem
    )
    own.start()

    def near(step_d, step_h):
        ok = None
        for at, step, count in ((d, step_d, groups), (h, step_h, towers)):
            if step:
                test = (at + step >= 0) & (at + step < count)
                ok = test if ok is None else ok & test
        return ok, (d + step_d, h + step_h)

    barrier = pltpu.get_barrier_semaphore()
    beside = [(0, 1), (0, -1), (1, 1), (1, -1), (-1, 1), (-1, -1), (1, 0), (-1, 0)]
    if groups > 4:
        beside += [(step * hop, 0) for hop in range(2, groups) for step in (1, -1)]
    expected = jnp.int32(0)
    for step_d, step_h in beside:
        ok, target = near(step_d, step_h)
        expected = expected + jnp.where(ok, 1, 0)

        @pl.when(ok)
        def _(target=target):
            pl.semaphore_signal(barrier, inc=1, device_id=target, device_id_type=MESH)

    pl.semaphore_wait(barrier, expected)

    whole = pl.ds(0, planes)
    inner = pl.ds(1, planes)
    first, last = pl.ds(0, 1), pl.ds(planes - 1, 1)
    low, high = pl.ds(0, 1), pl.ds(planes + 1, 1)
    routes = [
        ((1, 0), last, (0, rows), low, LEAD),
        ((-1, 0), first, (0, rows), high, LEAD),
        ((0, 1), whole, (rows - LEAD, LEAD), inner, 0),
        ((0, -1), whole, (0, margin), inner, end),
        ((1, -1), last, (0, margin), low, end),
        ((-1, -1), first, (0, margin), high, end),
    ]

    def halo(index, reach):
        step, from_planes, (row, count), to_planes, to_row = routes[index]
        return pltpu.make_async_remote_copy(
            src_ref=density.at[from_planes, pl.ds(row, count)],
            dst_ref=volume.at[to_planes, pl.ds(to_row, count)],
            send_sem=halo_send.at[index],
            recv_sem=halo_recv.at[index],
            device_id=reach,
            device_id_type=MESH,
        )

    for index, route in enumerate(routes):
        ok, target = near(*route[0])

        @pl.when(ok)
        def _(index=index, target=target):
            halo(index, target).start()

    @pl.when(d == 0)
    def _():
        volume[0] = jnp.zeros(volume.shape[1:], jnp.float32)

    @pl.when(d == groups - 1)
    def _():
        volume[planes + 1] = jnp.zeros(volume.shape[1:], jnp.float32)

    @pl.when(h == 0)
    def _():
        volume[1 : planes + 1, :LEAD] = jnp.zeros((planes, LEAD, cols), jnp.float32)

    @pl.when(h == towers - 1)
    def _():
        volume[:, end:tall] = jnp.zeros((planes + 2, margin, cols), jnp.float32)

    own.wait()

    lz, ly, lx = light[0], light[1], light[2]
    half_gain = [0.5 * gain[c] for c in range(3)]
    half_bias = [0.5 * bias[c] for c in range(3)]

    def shade(plane, row, count, keep):
        at = LEAD + row
        centre = volume[plane, at : at + count]
        lane = lax.broadcasted_iota(jnp.int32, (count, cols), 1)
        following = jnp.where(lane == cols - 1, 0.0, pltpu.roll(centre, cols - 1, 1))
        previous = jnp.where(lane == 0, 0.0, pltpu.roll(centre, 1, 1))
        dx = following - previous
        dz = volume[plane + 1, at : at + count] - volume[plane - 1, at : at + count]
        dy = volume[plane, at + 1 : at + 1 + count] - volume[plane, at - 1 : at - 1 + count]
        facing = (lz * dz + ly * dy + lx * dx) * lax.rsqrt(4.0 + dz * dz + dy * dy + dx * dx)
        shading = 0.25 + 1.5 * jnp.maximum(facing, 0.0)
        optical = extinction * (
            jnp.maximum(centre, 0.0) + jnp.log1p(jnp.exp(-jnp.abs(centre)))
        )
        opacity = jnp.tanh(0.5 * optical) * (1.0 + jnp.exp(-optical))
        if keep is not None:
            opacity = opacity * keep
        lit = 0.5 * (opacity * shading)
        to = pl.ds(row, count)
        for c in range(3):
            fields[c, plane - 1, to] = lit + lit * jnp.tanh(half_gain[c] * centre + half_bias[c])
        fields[3, plane - 1, to] = opacity

    inside = jnp.where(h < towers - 1, 1.0, 0.0)

    def early(plane, _):
        for row, count in spans(LEAD, rows - LEAD, 16):
            shade(plane, row, count, None)
        return 0

    lax.fori_loop(2, planes, early, 0)

    def landed(index):
        step_d, step_h = routes[index][0]
        ok, source = near(-step_d, -step_h)

        @pl.when(ok)
        def _():
            halo(index, source).wait_recv()

    def shade_low():
        for index in (0, 1, 2):
            landed(index)
        for plane in range(1, planes + 1):
            shade(plane, 0, LEAD, None)
        for row, count in spans(LEAD, rows - LEAD, 16):
            for plane in (1, planes):
                shade(plane, row, count, None)

    def shade_high():
        for index in (3, 4, 5):
            landed(index)

        def bottom(at, _):
            for plane in (2 * at + 1, 2 * at + 2):
                shade(plane, rows - LEAD, LEAD, None)
                for row, count in spans(rows, rows + margin, 16):
                    shade(plane, row, count, inside)
            return 0

        lax.fori_loop(0, planes // 2, bottom, 0)

    first_plane = d * planes

    def partial(view, block):
        step = shear[view]
        backward = reverse[view]
        colour = [jnp.zeros((share, cols), jnp.float32) for _ in range(3)]
        clear = jnp.ones((share, cols), jnp.float32)
        covered = jnp.zeros((share, cols), jnp.float32)
        for i in range(planes):
            plane = i + backward * (planes - 1 - 2 * i)
            offset = lax.div((first_plane + plane) * step, jnp.int32(total_planes))
            at = pl.ds(offset + block * share, share)
            for c in range(3):
                colour[c] = colour[c] + clear * fields[c, plane, at]
            covered = covered + clear * fields[3, plane, at]
            clear = 1.0 - covered
        return colour + [covered]

    odd = lax.rem(d, 2)
    out_step = 2 * odd - 1
    mate = d - out_step
    pair = lax.div(d, 2)
    beyond = odd * (groups - 1 - d) + (1 - odd) * d
    handing = odd * (d - 1) + (1 - odd) * (groups - 2 - d)

    def over(first, second, swap):
        front = [jnp.where(swap, b, a) for a, b in zip(first, second)]
        behind = [jnp.where(swap, a, b) for a, b in zip(first, second)]
        clear = 1.0 - front[3]
        return [f + clear * b for f, b in zip(front, behind)]

    def load(ref, block, view):
        return [ref[block, view, c] for c in range(4)]

    def store(ref, block, view, image):
        for c in range(4):
            ref[block, view, c] = image[c]

    def hand(view, block):
        return pltpu.make_async_remote_copy(
            src_ref=outgoing.at[block, view],
            dst_ref=handed.at[block, view],
            send_sem=hand_send.at[view, block],
            recv_sem=hand_recv.at[view, block],
            device_id=(mate, h),
            device_id_type=MESH,
        )

    def send(view, block):
        return pltpu.make_async_remote_copy(
            src_ref=outgoing.at[block, view],
            dst_ref=incoming.at[d, view],
            send_sem=part_send.at[view, block],
            recv_sem=part_recv.at[view, d],
            device_id=(block, h),
            device_id_type=MESH,
        )

    def receive(view, source):
        return pltpu.make_async_remote_copy(
            src_ref=outgoing.at[source, view],
            dst_ref=incoming.at[source, view],
            send_sem=part_send.at[view, source],
            recv_sem=part_recv.at[view, source],
            device_id=(source, h),
            device_id_type=MESH,
        )

    def each(count, body):
        def step(k, _):
            body(k)
            return 0

        lax.fori_loop(0, count, step, 0)

    def hand_over(view, k):
        block = odd * k + (1 - odd) * (groups - 1 - k)
        store(outgoing, block, view, partial(view, block))
        hand(view, block).start()

    def prepare(view, k):
        block = d + out_step * (1 + k)
        store(outgoing, block, view, partial(view, block))

    def to_mate(view):
        store(outgoing, mate, view, partial(view, mate))
        send(view, mate).start()

    def pass_on(view, k):
        block = odd * (groups - 1 - k) + (1 - odd) * k
        hand(view, block).wait_recv()
        own_part, other = load(outgoing, block, view), load(handed, block, view)
        swap = reverse[view] != odd
        store(outgoing, block, view, over(own_part, other, swap))
        send(view, block).start()

    reach = lax.div((first_plane + planes - 1) * margin, jnp.int32(total_planes))

    def hand_round(early):
        def one(k):
            block = odd * k + (1 - odd) * (groups - 1 - k)
            ready = ((block + 1) * share + reach <= rows - LEAD) & (odd == 1)

            @pl.when(ready if early else jnp.logical_not(ready))
            def _():
                each(views, lambda view: hand_over(view, k))

        each(handing, one)

    shade_low()
    hand_round(True)
    shade_high()
    hand_round(False)
    each(views, to_mate)
    each(views, lambda view: each(beyond, lambda k: prepare(view, k)))
    each(views, lambda view: store(incoming, d, view, partial(view, d)))
    each(beyond, lambda k: each(views, lambda view: pass_on(view, k)))

    def finish(view):
        swap = reverse[view] == 1
        receive(view, mate).wait_recv()
        both = over(load(incoming, d, view), load(incoming, mate, view), reverse[view] != odd)
        store(incoming, 2 * pair + 1, view, both)
        sources = [jnp.where(j > pair, 2 * j, 2 * j + 1) for j in range(groups // 2)]
        for j, source in enumerate(sources):

            @pl.when(j != pair)
            def _():
                receive(view, source).wait_recv()

        total = load(incoming, sources[0], view)
        for source in sources[1:]:
            total = over(total, load(incoming, source, view), swap)
        for c in range(4):
            out[c, view] = total[c]

    for view in range(views):
        finish(view)

    for index, route in enumerate(routes):
        ok, target = near(*route[0])

        @pl.when(ok)
        def _(index=index, target=target):
            halo(index, target).wait_send()

    def sent(view):
        send(view, mate).wait_send()
        each(handing, lambda k: hand(view, d - out_step * (2 + k)).wait_send())
        each(beyond, lambda k: send(view, d + out_step * (1 + k)).wait_send())

    each(views, sent)


def general(groups, towers, density, light, gain, bias, shear, reverse):
    planes, rows, cols = density.shape
    views = shear.shape[0]
    share = rows // groups
    tall = LEAD + rows + rows // 2
    scalars = pl.BlockSpec(memory_space=pltpu.SMEM)
    return pl.pallas_call(
        functools.partial(kernel, groups, towers),
        name="render",
        out_shape=pltpu.VMEM((4, views, share, cols), jnp.float32),
        in_specs=[pl.BlockSpec(memory_space=pltpu.HBM)] + [scalars] * 5,
        out_specs=pl.BlockSpec(memory_space=pltpu.VMEM),
        scratch_shapes=[
            pltpu.VMEM((planes + 2, tall + LEAD, cols), jnp.float32),
            pltpu.VMEM((4, planes, rows + rows // 2, cols), jnp.float32),
            pltpu.VMEM((groups, views, 4, share, cols), jnp.float32),
            pltpu.VMEM((groups, views, 4, share, cols), jnp.float32),
            pltpu.VMEM((groups, views, 4, share, cols), jnp.float32),
            pltpu.SemaphoreType.DMA,
            pltpu.SemaphoreType.DMA((6,)),
            pltpu.SemaphoreType.DMA((6,)),
            pltpu.SemaphoreType.DMA((views, groups)),
            pltpu.SemaphoreType.DMA((views, groups)),
            pltpu.SemaphoreType.DMA((views, groups)),
            pltpu.SemaphoreType.DMA((views, groups)),
        ],
        compiler_params=pltpu.CompilerParams(collective_id=0, has_side_effects=True, vmem_limit_bytes=60 * 1024 * 1024),
    )(density, light, gain, bias, shear, reverse)


def line(towers, density, light, gain, bias, shear, reverse):
    planes, rows, cols = density.shape
    views = shear.shape[0]
    groups = 4
    share = rows // groups
    whole = pl.BlockSpec(memory_space=pltpu.HBM)
    images = pltpu.VMEM((groups, views, 4, share, cols), jnp.float32)
    return pl.pallas_call(
        functools.partial(line_kernel, towers),
        name="render",
        out_shape=pltpu.VMEM((4, views, share, cols), jnp.float32),
        in_specs=[whole] * 6,
        out_specs=pl.BlockSpec(memory_space=pltpu.VMEM),
        scratch_shapes=[pltpu.SMEM(scalar.shape, scalar.dtype) for scalar in (light, gain, bias, shear, reverse)]
        + [
            pltpu.VMEM((2 * planes + 3, LEAD + rows + rows // 2 + LEAD, cols), jnp.float32),
            pltpu.VMEM((4, 2 * planes + 2, rows + rows // 2, cols), jnp.float32),
            images,
            images,
            images,
            pltpu.SemaphoreType.DMA((7,)),
            pltpu.SemaphoreType.DMA((8,)),
            pltpu.SemaphoreType.DMA((3 * views,)),
            pltpu.SemaphoreType.DMA((2 * views,)),
        ],
        compiler_params=pltpu.CompilerParams(collective_id=0, has_side_effects=True, vmem_limit_bytes=60 * 1024 * 1024),
    )(density, light, gain, bias, shear, reverse)


def on_device(groups, towers, density, light, gain, bias, shear, reverse):
    planes, rows, _ = density.shape
    if groups == 4 and planes >= 8 and rows % 64 == 0:
        return line(towers, density, light, gain, bias, shear, reverse)
    return general(groups, towers, density, light, gain, bias, shear, reverse)


def solution(mesh):
    groups, towers = mesh.shape["depth"], mesh.shape["height"]
    placed = (P("depth", "height", None), P(), P(), P(), P(), P())
    return jax.shard_map(
        functools.partial(on_device, groups, towers),
        mesh=mesh,
        in_specs=placed,
        out_specs=P(None, None, ("height", "depth"), None),
        check_vma=False,
    )
```

```python
import functools

import jax
import jax.numpy as jnp
from jax import lax
from jax.experimental import pallas as pl
from jax.experimental.pallas import tpu as pltpu
from jax.sharding import PartitionSpec as P

EXTINCTION = 2.5
LEAD = 8
TOGETHER = 6
MESH = pl.DeviceIdType.MESH


def spans(low, high, size):
    return [(at, min(size, high - at)) for at in range(low, high, size)]


def line_kernel(
    towers,
    density,
    light_in,
    gain_in,
    bias_in,
    shear_in,
    reverse_in,
    out,
    light,
    gain,
    bias,
    shear,
    reverse,
    volume,
    fields,
    outgoing,
    incoming,
    handed,
    sent_sem,
    halo_sem,
    hand_sem,
    part_sem,
    go_sem,
):
    planes, rows, cols = density.shape
    margin = rows // 2
    views = shear.shape[0]
    groups = 4
    share = rows // groups
    total_planes = planes * groups
    extinction = EXTINCTION / total_planes
    d = lax.axis_index("depth")
    h = lax.axis_index("height")
    above, below = (h - 1 >= 0) & (h - 1 < towers), (h + 1 >= 0) & (h + 1 < towers)
    end = LEAD + rows
    own_planes = pl.ds(2, planes)
    images, plane_sent, edge_sent, down_sent, up_sent, corner_sent, rest_sent, relay_sent = range(8)
    slab_sent, slab_edge_sent = edge_sent, rest_sent
    pair_in, peer_in, edge_in, down_in, up_in, pair_corner_in, peer_corner_in, rest_in = range(8)
    slab_in, slab_edge_in, slab_end_in = pair_in, edge_in, peer_in

    own = pltpu.make_async_copy(
        density, volume.at[own_planes, pl.ds(LEAD, rows)], sent_sem.at[images]
    )
    own.start()
    scalars = [
        pltpu.make_async_copy(source, target, sent_sem.at[1 + index])
        for index, (source, target) in enumerate(
            zip((light_in, gain_in, bias_in, shear_in, reverse_in), (light, gain, bias, shear, reverse))
        )
    ]
    for scalar in scalars:
        scalar.start()

    def valid(step_d, step_h):
        ok = None
        for at, step, count in ((d, step_d, groups), (h, step_h, towers)):
            if step:
                test = (at + step >= 0) & (at + step < count)
                ok = test if ok is None else ok & test
        return ok

    barrier = pltpu.get_barrier_semaphore()
    expected = jnp.int32(0)
    greets = {at: [] for at in range(groups)}
    awaits = {at: [] for at in range(groups)}

    def greet(at, step_d, step_h, parity=None):
        greets[at].append((step_d, step_h, parity))
        awaits[at + step_d].append((-step_d, -step_h, parity if parity is None else (parity + step_h) % 2))

    for at in range(groups):
        mate = (at ^ 1) - at
        outer = at in (0, 3)
        for step_h in (1, -1):
            greet(at, mate if outer else 0, step_h)
            greet(at, 0 if outer else mate, step_h, 0)
        greet(at, mate, 0)
        if not outer:
            greet(at, -mate, 0)
            greet(at, -mate, 1)
    greet(0, 2, 0)

    def meets(at, step_d, step_h, parity):
        ok = (d == at) & valid(step_d, step_h)
        return ok if parity is None else ok & (lax.rem(h, 2) == parity)

    for at in range(groups):

        for step_d, step_h, parity in greets[at]:

            @pl.when(meets(at, step_d, step_h, parity))
            def _(target=(d + step_d, h + step_h)):
                pl.semaphore_signal(barrier, inc=1, device_id=target, device_id_type=MESH)

        for step in awaits[at]:
            expected = expected + jnp.where(meets(at, *step), 1, 0)

    for scalar in scalars:
        scalar.wait()
    own.wait()

    lz, ly, lx = light[0], light[1], light[2]
    half_gain = [0.5 * gain[c] for c in range(3)]
    half_bias = [0.5 * bias[c] for c in range(3)]
    inside = jnp.where(below, 1.0, 0.0)

    def shade(plane, row, count, keep, loose=False):
        at = LEAD + row
        centre = volume[plane, at : at + count]
        lane = lax.broadcasted_iota(jnp.int32, (count, cols), 1)
        following = jnp.where(lane == cols - 1, 0.0, pltpu.roll(centre, cols - 1, 1))
        previous = jnp.where(lane == 0, 0.0, pltpu.roll(centre, 1, 1))
        dx = following - previous
        dz = volume[plane + 1, at : at + count] - volume[plane - 1, at : at + count]
        below_it = pltpu.roll(centre, count - 1, 0) if loose else volume[plane, at + 1 : at + 1 + count]
        dy = below_it - volume[plane, at - 1 : at - 1 + count]
        facing = (lz * dz + ly * dy + lx * dx) * lax.rsqrt(4.0 + dz * dz + dy * dy + dx * dx)
        shading = 0.25 + 1.5 * jnp.maximum(facing, 0.0)
        optical = extinction * (
            jnp.maximum(centre, 0.0) + jnp.log1p(jnp.exp(-jnp.abs(centre)))
        )
        opacity = jnp.tanh(0.5 * optical) * (1.0 + jnp.exp(-optical))
        if keep is not None:
            opacity = opacity * keep
        lit = 0.5 * (opacity * shading)
        to = pl.ds(row, count)
        for c in range(3):
            fields[c, plane, to] = lit + lit * jnp.tanh(half_gain[c] * centre + half_bias[c])
        fields[3, plane, to] = opacity

    def shade_box(low, high, top, bottom, loose=False):
        tiles = (bottom - top) // 8
        together = max(1, min(high - low, -(-TOGETHER // tiles)))
        looped = (high - low) // together if high - low > together else 0

        def some(plane, count):
            for step in range(count):
                for row, size in spans(top, min(bottom, rows), 16):
                    shade(plane + step, row, size, None, loose)
                for row, size in spans(max(top, rows), bottom, 16):
                    shade(plane + step, row, size, inside)

        if looped:

            def step(index, _):
                some(low + index * together, together)
                return 0

            lax.fori_loop(0, looped, step, 0)
        done = low + looped * together
        if done < high:
            some(done, high - done)

    def copy_to(source, target, sent, received, device):
        return pltpu.make_async_remote_copy(
            src_ref=source,
            dst_ref=target,
            send_sem=sent_sem.at[sent],
            recv_sem=received,
            device_id=device,
            device_id_type=MESH,
        )

    def over(first, second, swap):
        front = [jnp.where(swap, b, a) for a, b in zip(first, second)]
        behind = [jnp.where(swap, a, b) for a, b in zip(first, second)]
        clear = 1.0 - front[3]
        return [f + clear * b for f, b in zip(front, behind)]

    everything = (0, share)
    odd = lax.rem(h, 2) == 1
    distant = (lax.rem(h, 2) == 0) & (h > 0)
    ahead = jnp.where(h == towers // 2, views // 2, 1)
    some, rest = (0, ahead), (ahead, views)

    def load(ref, block, view, part):
        return [ref[block, view, c, pl.ds(*part)] for c in range(4)]

    def store(ref, block, view, part, image):
        for c in range(4):
            ref[block, view, c, pl.ds(*part)] = image[c]

    def each_view(body, start=0, stop=views):
        def step(view, _):
            body(view)
            return 0

        lax.fori_loop(start, stop, step, 0)

    def extent(at):
        low = {0: 2, 1: 1, 2: 2, 3: 3}[at]
        high = {0: planes + 1, 1: planes + 2, 2: planes + 3, 3: planes + 2}[at]
        reach = (at * planes + high - 3) * margin // total_planes
        return low, high, reach, min(margin, -(-(reach + 1) // 8) * 8)

    def brick(at):
        outer = at in (0, groups - 1)
        lower = at < groups // 2
        mate = at ^ 1
        first = at * planes - 2
        low, high, reach, border = extent(at)
        extra = -(-reach // 8) * 8
        mate_pair = pl.ds(0, 2) if lower else pl.ds(planes + 2, 2)
        edge = {0: planes + 1, 1: 1, 2: planes + 2, 3: 2}[at]
        mate_edge = {0: 1, 3: planes + 2}.get(at, edge)
        others = [2, 3] if lower else [0, 1]
        other = {0: 2, 1: 2, 2: 1, 3: 1}[at]
        peer = {1: 2, 2: 1}.get(at)
        halves = [(share // 2, share // 2), (0, share // 2)]
        parts = {0: halves, 1: [everything], 2: [everything], 3: [everything]}
        hand_at = {
            (block, part): index
            for index, (block, part) in enumerate((block, part) for block in others for part in parts[block])
        }

        def plane_copy(source, target, take, put, sent, received, device):
            return copy_to(
                volume.at[source, pl.ds(*take)],
                volume.at[target, pl.ds(*put)],
                sent,
                halo_sem.at[received],
                device,
            )

        own_pair = pl.ds(planes, 2) if lower else pl.ds(2, 2)
        own_peer = pl.ds(planes + 1, 1) if lower else pl.ds(2, 1)
        peer_target = pl.ds(1, 1) if lower else pl.ds(planes + 2, 1)
        peer_border = extent(peer)[3] if peer else None
        whole = (LEAD, rows)

        cut = rows - share
        soon, after = ((LEAD + share, cut), (LEAD, share)) if lower else ((LEAD, cut), (LEAD + cut, share))

        def pair_copy():
            return plane_copy(own_pair, mate_pair, soon, soon, plane_sent, pair_in, (mate, h))

        def pair_rest():
            return plane_copy(own_pair, mate_pair, after, after, rest_sent, rest_in, (mate, h))

        def peer_copy():
            return plane_copy(own_peer, peer_target, whole, whole, plane_sent, peer_in, (peer, h))

        def pair_relay(step):
            take, put = (LEAD, border), (end, border)
            return plane_copy(mate_pair, mate_pair, take, put, relay_sent, pair_corner_in, (d, h + step))

        def peer_corner(step, count):
            take, put = (LEAD, count), (end, count)
            return plane_copy(own_peer, peer_target, take, put, corner_sent, peer_corner_in, (d + peer - at, h + step))

        def edge_copy(step):
            take, put = (rows, LEAD), (0, LEAD)
            return plane_copy(edge, mate_edge, take, put, edge_sent, edge_in, (d + mate - at, h + step))

        span_high = 2 * planes + 2
        span_reach = extent(1)[2]
        span_rows = share + extent(1)[3]
        slab = pl.ds(planes + 2, planes)
        slab_end = pl.ds(2 * planes + 2, 1)

        def slab_copy():
            take = (LEAD, span_rows)
            return plane_copy(own_planes, slab, take, take, slab_sent, slab_in, (0 if at else 1, h))

        def slab_edge_copy(step):
            take, put = (rows, LEAD), (0, LEAD)
            return plane_copy(own_planes, slab, take, put, slab_edge_sent, slab_edge_in, (d + (-1 if at else 1), h + step))

        def slab_end_copy():
            take = (LEAD, span_rows)
            return plane_copy(pl.ds(2, 1), slab_end, take, take, slab_sent, slab_end_in, (0 if at else 2, h))

        def down_copy(step):
            return copy_to(
                volume.at[own_planes, pl.ds(rows, LEAD)],
                volume.at[own_planes, pl.ds(0, LEAD)],
                down_sent,
                halo_sem.at[down_in],
                (d, h + step),
            )

        def up_copy(step):
            return copy_to(
                volume.at[own_planes, pl.ds(LEAD, border)],
                volume.at[own_planes, pl.ds(end, border)],
                up_sent,
                halo_sem.at[up_in],
                (d, h + step),
            )

        def hand(view, block, part):
            index = hand_at[block, part] * views + view
            return copy_to(
                outgoing.at[block, view, :, pl.ds(*part)],
                handed.at[block, view, :, pl.ds(*part)],
                images,
                hand_sem.at[index],
                (mate, h),
            )

        def send(view, block, part):
            slot = 0 if block == mate else views
            return copy_to(
                outgoing.at[block, view, :, pl.ds(*part)],
                incoming.at[at, view, :, pl.ds(*part)],
                images,
                part_sem.at[slot + view],
                (block, h),
            )

        def receive(view, source):
            slot = 0 if source == mate else views
            return copy_to(
                outgoing.at[at, view],
                incoming.at[source, view],
                images,
                part_sem.at[slot + view],
                (source, h),
            )

        def partial(view, block, part, high=high, reach=reach):
            step = shear[view]
            backward = reverse[view]
            count = high - low
            size = part[1]
            colour = [jnp.zeros((size, cols), jnp.float32) for _ in range(3)]
            clear = jnp.ones((size, cols), jnp.float32)
            covered = jnp.zeros((size, cols), jnp.float32)
            for i in range(count):
                plane = jnp.where(backward == 1, low + count - 1 - i, low + i)
                offset = lax.div((first + plane) * step, jnp.int32(total_planes))
                offset = jnp.minimum(jnp.maximum(offset, 0), reach)
                rows_at = pl.ds(offset + block * share + part[0], size)
                for c in range(3):
                    colour[c] = colour[c] + clear * fields[c, plane, rows_at]
                covered = covered + clear * fields[3, plane, rows_at]
                clear = 1.0 - covered
            return colour + [covered]

        def send_mate():
            def one(view):
                store(outgoing, mate, view, everything, partial(view, mate, everything))
                send(view, mate, everything).start()

            each_view(one)

        def keep_own():
            span = (span_high, span_reach) if at == 0 else (high, reach)
            each_view(lambda view: store(incoming, at, view, everything, partial(view, at, everything, *span)))

        def hand_over(block, part=everything, which=(0, views)):
            def one(view):
                store(outgoing, block, view, part, partial(view, block, part))
                hand(view, block, part).start()

            each_view(one, *which)

        def pass_on(block, part=everything, which=(0, views)):
            def one(view):
                mine = partial(view, block, part)
                hand(view, block, part).wait_recv()
                theirs = load(handed, block, view, part)
                swap = reverse[view] == 1
                merged = over(theirs, mine, swap) if lower else over(mine, theirs, swap)
                store(outgoing, block, view, part, merged)
                send(view, block, part).start()

            each_view(one, *which)

        def images_gone(blocks):
            gone = pl.ds(0, blocks)
            copy_to(outgoing.at[gone], handed.at[gone], images, hand_sem.at[0], (mate, h)).wait_send()

        def begin():
            with jax.named_scope("barrier"):
                pl.semaphore_wait(barrier, expected)
            if outer:
                pair_copy().start()
            else:

                @pl.when(jnp.logical_not(odd))
                def _():
                    pl.semaphore_signal(go_sem, inc=1, device_id=(mate, h), device_id_type=MESH)

                peer_copy().start()
                (slab_copy if lower else slab_end_copy)().start()
                columns()

        def columns():
            if outer:

                @pl.when(jnp.logical_not(odd))
                def _():
                    with jax.named_scope("w_go"):
                        pl.semaphore_wait(go_sem, 1)

            @pl.when(below)
            def _():
                down_copy(1).start()
                if outer:
                    edge_copy(1).start()
                if at == 1:
                    slab_edge_copy(1).start()

            @pl.when(above)
            def _():
                if not outer:
                    peer_corner(-1, peer_border).start()
                up_copy(-1).start()

        def blank():
            if outer:
                volume[1 if lower else planes + 2] = jnp.zeros(volume.shape[1:], jnp.float32)

            @pl.when(jnp.logical_not(above))
            def _():
                volume[:, :LEAD] = jnp.zeros((2 * planes + 3, LEAD, cols), jnp.float32)

            @pl.when(jnp.logical_not(below))
            def _():
                volume[:, end : end + border] = jnp.zeros((2 * planes + 3, border, cols), jnp.float32)

        def top_landed():
            @pl.when(above)
            def _():
                with jax.named_scope("w_down"):
                    down_copy(-1).wait_recv()

        def bottom_landed():
            @pl.when(below)
            def _():
                with jax.named_scope("w_up"):
                    up_copy(1).wait_recv()

        def corners_landed():
            @pl.when(below)
            def _():
                with jax.named_scope("w_corner"):
                    peer_corner(1, border).wait_recv()
                    pair_relay(1).wait_recv()

        def edge_landed():
            @pl.when(above)
            def _():
                with jax.named_scope("w_edge"):
                    edge_copy(-1).wait_recv()

        blank()
        if at == 0:
            shade_box(low, high, LEAD, rows - LEAD)
            begin()
            with jax.named_scope("hand2"):
                hand_over(2)
            pair_rest().start()
            columns()
            top_landed()
            bottom_landed()
            shade_box(low, high, rows - LEAD, rows + extra)
            with jax.named_scope("hand3"):
                hand_over(3)
            shade_box(low, high, 0, LEAD)
            with jax.named_scope("mate"):
                send_mate()
            with jax.named_scope("w_slab"):
                slab_copy().wait_recv()

                @pl.when(above)
                def _():
                    slab_edge_copy(-1).wait_recv()

                slab_end_copy().wait_recv()
            shade_box(high, span_high, 0, -(-(share + span_reach) // 8) * 8)
            keep_own()
        elif at == 3:
            begin()
            shade_box(low, high, LEAD, rows - LEAD)
            with jax.named_scope("hand0b"):
                hand_over(0, halves[0])
            pair_rest().start()
            columns()
            shade_box(low, high, rows - LEAD, rows, True)

            def early():
                top_landed()
                shade_box(low, high, 0, LEAD)
                with jax.named_scope("hand0a"):
                    hand_over(0, halves[1])

            def late(which):
                with jax.named_scope("hand1"):
                    hand_over(1, everything, which)

            @pl.when(distant)
            def _():
                late(some)
                early()
                late(rest)

            @pl.when(h == 0)
            def _():
                early()
                late((0, views))

            @pl.when(odd)
            def _():
                early()
                late((0, views))

            bottom_landed()
            shade_box(low, high, rows - LEAD, rows)
            shade_box(low, high, rows, rows + extra)
            with jax.named_scope("mate"):
                send_mate()
            keep_own()
        else:
            shade_box(3, planes + 1, LEAD, rows - LEAD)
            begin()
            far_edge = planes + 1 if lower else 2
            seam = min(2 if lower else planes + 1, edge)


            def top():
                top_landed()
                edge_landed()
                shade_box(low, high, 0, LEAD)

            def relay():
                @pl.when(above)
                def _():
                    pair_relay(-1).start()

            def rest_landed():
                with jax.named_scope("w_rest"):
                    pair_rest().wait_recv()
                if lower:
                    relay()
                    shade_box(seam, seam + 2, LEAD, share + LEAD)
                else:
                    shade_box(seam, seam + 2, rows - share - LEAD, rows - LEAD)

            def bottom():
                bottom_landed()
                corners_landed()
                shade_box(low, high, rows - LEAD, rows + extra)

            with jax.named_scope("w_peer"):
                peer_copy().wait_recv()
            shade_box(far_edge, far_edge + 1, LEAD, rows - LEAD)
            if lower:
                shade_box(3, planes + 2, rows - LEAD, rows, True)
            with jax.named_scope("w_pair"):
                pair_copy().wait_recv()
            if lower:
                shade_box(seam, seam + 2, share + LEAD, rows - LEAD)
                with jax.named_scope("pass2"):
                    pass_on(2)
                rest_landed()
                top()
                bottom()
                with jax.named_scope("pass3"):
                    pass_on(3)
            else:
                relay()
                shade_box(seam, seam + 2, LEAD, rows - share - LEAD)
                with jax.named_scope("pass0b"):
                    pass_on(0, halves[0])
                rest_landed()

                def mate_part():
                    bottom()
                    with jax.named_scope("mate"):
                        send_mate()

                def early():
                    top()
                    with jax.named_scope("pass0a"):
                        pass_on(0, halves[1])

                @pl.when(distant)
                def _():
                    mate_part()
                    with jax.named_scope("pass1"):
                        pass_on(1, everything, some)
                    early()
                    pass_on(1, everything, rest)

                @pl.when(h == 0)
                def _():
                    mate_part()
                    early()
                    pass_on(1)

                @pl.when(odd)
                def _():
                    early()
                    mate_part()
                    with jax.named_scope("pass1"):
                        pass_on(1)

            keep_own()

        def finish(view):
            swap = reverse[view] == 1
            near = load(incoming, at, view, everything)
            if at != 0:
                with jax.named_scope("w_mate"):
                    receive(view, mate).wait_recv()
                theirs = load(incoming, mate, view, everything)
                near = over(near, theirs, swap) if at < mate else over(theirs, near, swap)
            with jax.named_scope("w_other"):
                receive(view, other).wait_recv()
            far = load(incoming, other, view, everything)
            total = over(near, far, swap) if lower else over(far, near, swap)
            for c in range(4):
                out[c, view] = total[c]

        for view in range(views):
            finish(view)

        if outer:
            pair_copy().wait_send()
            pair_rest().wait_send()
        else:
            peer_copy().wait_send()
            (slab_copy if lower else slab_end_copy)().wait_send()

        @pl.when(below)
        def _():
            down_copy(1).wait_send()
            if outer:
                edge_copy(1).wait_send()
            if at == 1:
                slab_edge_copy(1).wait_send()

        @pl.when(above)
        def _():
            up_copy(-1).wait_send()
            if not outer:
                peer_corner(-1, peer_border).wait_send()
                pair_relay(-1).wait_send()

        images_gone(2 if at == 1 else 3)
    for at in range(groups):

        @pl.when(d == at)
        def _():
            brick(at)


def kernel(
    groups,
    towers,
    density,
    light,
    gain,
    bias,
    shear,
    reverse,
    out,
    volume,
    fields,
    outgoing,
    incoming,
    handed,
    local_sem,
    halo_send,
    halo_recv,
    hand_send,
    hand_recv,
    part_send,
    part_recv,
):
    planes, rows, cols = density.shape
    margin = rows // 2
    views = shear.shape[0]
    share = rows // groups
    total_planes = planes * groups
    extinction = EXTINCTION / total_planes
    d = lax.axis_index("depth")
    h = lax.axis_index("height")
    end = LEAD + rows
    tall = end + margin

    own = pltpu.make_async_copy(
        density, volume.at[pl.ds(1, planes), pl.ds(LEAD, rows)], local_sem
    )
    own.start()

    def near(step_d, step_h):
        ok = None
        for at, step, count in ((d, step_d, groups), (h, step_h, towers)):
            if step:
                test = (at + step >= 0) & (at + step < count)
                ok = test if ok is None else ok & test
        return ok, (d + step_d, h + step_h)

    barrier = pltpu.get_barrier_semaphore()
    beside = [(0, 1), (0, -1), (1, 1), (1, -1), (-1, 1), (-1, -1), (1, 0), (-1, 0)]
    if groups > 4:
        beside += [(step * hop, 0) for hop in range(2, groups) for step in (1, -1)]
    expected = jnp.int32(0)
    for step_d, step_h in beside:
        ok, target = near(step_d, step_h)
        expected = expected + jnp.where(ok, 1, 0)

        @pl.when(ok)
        def _(target=target):
            pl.semaphore_signal(barrier, inc=1, device_id=target, device_id_type=MESH)

    pl.semaphore_wait(barrier, expected)

    whole = pl.ds(0, planes)
    inner = pl.ds(1, planes)
    first, last = pl.ds(0, 1), pl.ds(planes - 1, 1)
    low, high = pl.ds(0, 1), pl.ds(planes + 1, 1)
    routes = [
        ((1, 0), last, (0, rows), low, LEAD),
        ((-1, 0), first, (0, rows), high, LEAD),
        ((0, 1), whole, (rows - LEAD, LEAD), inner, 0),
        ((0, -1), whole, (0, margin), inner, end),
        ((1, -1), last, (0, margin), low, end),
        ((-1, -1), first, (0, margin), high, end),
    ]

    def halo(index, reach):
        step, from_planes, (row, count), to_planes, to_row = routes[index]
        return pltpu.make_async_remote_copy(
            src_ref=density.at[from_planes, pl.ds(row, count)],
            dst_ref=volume.at[to_planes, pl.ds(to_row, count)],
            send_sem=halo_send.at[index],
            recv_sem=halo_recv.at[index],
            device_id=reach,
            device_id_type=MESH,
        )

    for index, route in enumerate(routes):
        ok, target = near(*route[0])

        @pl.when(ok)
        def _(index=index, target=target):
            halo(index, target).start()

    @pl.when(d == 0)
    def _():
        volume[0] = jnp.zeros(volume.shape[1:], jnp.float32)

    @pl.when(d == groups - 1)
    def _():
        volume[planes + 1] = jnp.zeros(volume.shape[1:], jnp.float32)

    @pl.when(h == 0)
    def _():
        volume[1 : planes + 1, :LEAD] = jnp.zeros((planes, LEAD, cols), jnp.float32)

    @pl.when(h == towers - 1)
    def _():
        volume[:, end:tall] = jnp.zeros((planes + 2, margin, cols), jnp.float32)

    own.wait()

    lz, ly, lx = light[0], light[1], light[2]
    half_gain = [0.5 * gain[c] for c in range(3)]
    half_bias = [0.5 * bias[c] for c in range(3)]

    def shade(plane, row, count, keep):
        at = LEAD + row
        centre = volume[plane, at : at + count]
        lane = lax.broadcasted_iota(jnp.int32, (count, cols), 1)
        following = jnp.where(lane == cols - 1, 0.0, pltpu.roll(centre, cols - 1, 1))
        previous = jnp.where(lane == 0, 0.0, pltpu.roll(centre, 1, 1))
        dx = following - previous
        dz = volume[plane + 1, at : at + count] - volume[plane - 1, at : at + count]
        dy = volume[plane, at + 1 : at + 1 + count] - volume[plane, at - 1 : at - 1 + count]
        facing = (lz * dz + ly * dy + lx * dx) * lax.rsqrt(4.0 + dz * dz + dy * dy + dx * dx)
        shading = 0.25 + 1.5 * jnp.maximum(facing, 0.0)
        optical = extinction * (
            jnp.maximum(centre, 0.0) + jnp.log1p(jnp.exp(-jnp.abs(centre)))
        )
        opacity = jnp.tanh(0.5 * optical) * (1.0 + jnp.exp(-optical))
        if keep is not None:
            opacity = opacity * keep
        lit = 0.5 * (opacity * shading)
        to = pl.ds(row, count)
        for c in range(3):
            fields[c, plane - 1, to] = lit + lit * jnp.tanh(half_gain[c] * centre + half_bias[c])
        fields[3, plane - 1, to] = opacity

    inside = jnp.where(h < towers - 1, 1.0, 0.0)

    def early(plane, _):
        for row, count in spans(LEAD, rows - LEAD, 16):
            shade(plane, row, count, None)
        return 0

    lax.fori_loop(2, planes, early, 0)

    def landed(index):
        step_d, step_h = routes[index][0]
        ok, source = near(-step_d, -step_h)

        @pl.when(ok)
        def _():
            halo(index, source).wait_recv()

    def shade_low():
        for index in (0, 1, 2):
            landed(index)
        for plane in range(1, planes + 1):
            shade(plane, 0, LEAD, None)
        for row, count in spans(LEAD, rows - LEAD, 16):
            for plane in (1, planes):
                shade(plane, row, count, None)

    def shade_high():
        for index in (3, 4, 5):
            landed(index)

        def bottom(at, _):
            for plane in (2 * at + 1, 2 * at + 2):
                shade(plane, rows - LEAD, LEAD, None)
                for row, count in spans(rows, rows + margin, 16):
                    shade(plane, row, count, inside)
            return 0

        lax.fori_loop(0, planes // 2, bottom, 0)

    first_plane = d * planes

    def partial(view, block):
        step = shear[view]
        backward = reverse[view]
        colour = [jnp.zeros((share, cols), jnp.float32) for _ in range(3)]
        clear = jnp.ones((share, cols), jnp.float32)
        covered = jnp.zeros((share, cols), jnp.float32)
        for i in range(planes):
            plane = i + backward * (planes - 1 - 2 * i)
            offset = lax.div((first_plane + plane) * step, jnp.int32(total_planes))
            at = pl.ds(offset + block * share, share)
            for c in range(3):
                colour[c] = colour[c] + clear * fields[c, plane, at]
            covered = covered + clear * fields[3, plane, at]
            clear = 1.0 - covered
        return colour + [covered]

    odd = lax.rem(d, 2)
    out_step = 2 * odd - 1
    mate = d - out_step
    pair = lax.div(d, 2)
    beyond = odd * (groups - 1 - d) + (1 - odd) * d
    handing = odd * (d - 1) + (1 - odd) * (groups - 2 - d)

    def over(first, second, swap):
        front = [jnp.where(swap, b, a) for a, b in zip(first, second)]
        behind = [jnp.where(swap, a, b) for a, b in zip(first, second)]
        clear = 1.0 - front[3]
        return [f + clear * b for f, b in zip(front, behind)]

    def load(ref, block, view):
        return [ref[block, view, c] for c in range(4)]

    def store(ref, block, view, image):
        for c in range(4):
            ref[block, view, c] = image[c]

    def hand(view, block):
        return pltpu.make_async_remote_copy(
            src_ref=outgoing.at[block, view],
            dst_ref=handed.at[block, view],
            send_sem=hand_send.at[view, block],
            recv_sem=hand_recv.at[view, block],
            device_id=(mate, h),
            device_id_type=MESH,
        )

    def send(view, block):
        return pltpu.make_async_remote_copy(
            src_ref=outgoing.at[block, view],
            dst_ref=incoming.at[d, view],
            send_sem=part_send.at[view, block],
            recv_sem=part_recv.at[view, d],
            device_id=(block, h),
            device_id_type=MESH,
        )

    def receive(view, source):
        return pltpu.make_async_remote_copy(
            src_ref=outgoing.at[source, view],
            dst_ref=incoming.at[source, view],
            send_sem=part_send.at[view, source],
            recv_sem=part_recv.at[view, source],
            device_id=(source, h),
            device_id_type=MESH,
        )

    def each(count, body):
        def step(k, _):
            body(k)
            return 0

        lax.fori_loop(0, count, step, 0)

    def hand_over(view, k):
        block = odd * k + (1 - odd) * (groups - 1 - k)
        store(outgoing, block, view, partial(view, block))
        hand(view, block).start()

    def prepare(view, k):
        block = d + out_step * (1 + k)
        store(outgoing, block, view, partial(view, block))

    def to_mate(view):
        store(outgoing, mate, view, partial(view, mate))
        send(view, mate).start()

    def pass_on(view, k):
        block = odd * (groups - 1 - k) + (1 - odd) * k
        hand(view, block).wait_recv()
        own_part, other = load(outgoing, block, view), load(handed, block, view)
        swap = reverse[view] != odd
        store(outgoing, block, view, over(own_part, other, swap))
        send(view, block).start()

    reach = lax.div((first_plane + planes - 1) * margin, jnp.int32(total_planes))

    def hand_round(early):
        def one(k):
            block = odd * k + (1 - odd) * (groups - 1 - k)
            ready = ((block + 1) * share + reach <= rows - LEAD) & (odd == 1)

            @pl.when(ready if early else jnp.logical_not(ready))
            def _():
                each(views, lambda view: hand_over(view, k))

        each(handing, one)

    shade_low()
    hand_round(True)
    shade_high()
    hand_round(False)
    each(views, to_mate)
    each(views, lambda view: each(beyond, lambda k: prepare(view, k)))
    each(views, lambda view: store(incoming, d, view, partial(view, d)))
    each(beyond, lambda k: each(views, lambda view: pass_on(view, k)))

    def finish(view):
        swap = reverse[view] == 1
        receive(view, mate).wait_recv()
        both = over(load(incoming, d, view), load(incoming, mate, view), reverse[view] != odd)
        store(incoming, 2 * pair + 1, view, both)
        sources = [jnp.where(j > pair, 2 * j, 2 * j + 1) for j in range(groups // 2)]
        for j, source in enumerate(sources):

            @pl.when(j != pair)
            def _():
                receive(view, source).wait_recv()

        total = load(incoming, sources[0], view)
        for source in sources[1:]:
            total = over(total, load(incoming, source, view), swap)
        for c in range(4):
            out[c, view] = total[c]

    for view in range(views):
        finish(view)

    for index, route in enumerate(routes):
        ok, target = near(*route[0])

        @pl.when(ok)
        def _(index=index, target=target):
            halo(index, target).wait_send()

    def sent(view):
        send(view, mate).wait_send()
        each(handing, lambda k: hand(view, d - out_step * (2 + k)).wait_send())
        each(beyond, lambda k: send(view, d + out_step * (1 + k)).wait_send())

    each(views, sent)


def general(groups, towers, density, light, gain, bias, shear, reverse):
    planes, rows, cols = density.shape
    views = shear.shape[0]
    share = rows // groups
    tall = LEAD + rows + rows // 2
    scalars = pl.BlockSpec(memory_space=pltpu.SMEM)
    return pl.pallas_call(
        functools.partial(kernel, groups, towers),
        name="render",
        out_shape=pltpu.VMEM((4, views, share, cols), jnp.float32),
        in_specs=[pl.BlockSpec(memory_space=pltpu.HBM)] + [scalars] * 5,
        out_specs=pl.BlockSpec(memory_space=pltpu.VMEM),
        scratch_shapes=[
            pltpu.VMEM((planes + 2, tall + LEAD, cols), jnp.float32),
            pltpu.VMEM((4, planes, rows + rows // 2, cols), jnp.float32),
            pltpu.VMEM((groups, views, 4, share, cols), jnp.float32),
            pltpu.VMEM((groups, views, 4, share, cols), jnp.float32),
            pltpu.VMEM((groups, views, 4, share, cols), jnp.float32),
            pltpu.SemaphoreType.DMA,
            pltpu.SemaphoreType.DMA((6,)),
            pltpu.SemaphoreType.DMA((6,)),
            pltpu.SemaphoreType.DMA((views, groups)),
            pltpu.SemaphoreType.DMA((views, groups)),
            pltpu.SemaphoreType.DMA((views, groups)),
            pltpu.SemaphoreType.DMA((views, groups)),
        ],
        compiler_params=pltpu.CompilerParams(collective_id=0, has_side_effects=True, vmem_limit_bytes=60 * 1024 * 1024),
    )(density, light, gain, bias, shear, reverse)


def line(towers, density, light, gain, bias, shear, reverse):
    planes, rows, cols = density.shape
    views = shear.shape[0]
    groups = 4
    share = rows // groups
    whole = pl.BlockSpec(memory_space=pltpu.HBM)
    images = pltpu.VMEM((groups, views, 4, share, cols), jnp.float32)
    return pl.pallas_call(
        functools.partial(line_kernel, towers),
        name="render",
        out_shape=pltpu.VMEM((4, views, share, cols), jnp.float32),
        in_specs=[whole] * 6,
        out_specs=pl.BlockSpec(memory_space=pltpu.VMEM),
        scratch_shapes=[pltpu.SMEM(scalar.shape, scalar.dtype) for scalar in (light, gain, bias, shear, reverse)]
        + [
            pltpu.VMEM((2 * planes + 3, LEAD + rows + rows // 2 + LEAD, cols), jnp.float32),
            pltpu.VMEM((4, 2 * planes + 2, rows + rows // 2, cols), jnp.float32),
            images,
            images,
            images,
            pltpu.SemaphoreType.DMA((8,)),
            pltpu.SemaphoreType.DMA((8,)),
            pltpu.SemaphoreType.DMA((3 * views,)),
            pltpu.SemaphoreType.DMA((2 * views,)),
            pltpu.SemaphoreType.REGULAR,
        ],
        compiler_params=pltpu.CompilerParams(collective_id=0, has_side_effects=True, vmem_limit_bytes=60 * 1024 * 1024),
    )(density, light, gain, bias, shear, reverse)


def on_device(groups, towers, density, light, gain, bias, shear, reverse):
    planes, rows, _ = density.shape
    if groups == 4 and planes >= 8 and rows % 64 == 0:
        return line(towers, density, light, gain, bias, shear, reverse)
    return general(groups, towers, density, light, gain, bias, shear, reverse)


def solution(mesh):
    groups, towers = mesh.shape["depth"], mesh.shape["height"]
    placed = (P("depth", "height", None), P(), P(), P(), P(), P())
    return jax.shard_map(
        functools.partial(on_device, groups, towers),
        mesh=mesh,
        in_specs=placed,
        out_specs=P(None, None, ("height", "depth"), None),
        check_vma=False,
    )
```

```python
import functools

import jax
import jax.numpy as jnp
from jax import lax
from jax.experimental import pallas as pl
from jax.experimental.pallas import tpu as pltpu
from jax.sharding import PartitionSpec as P

EXTINCTION = 2.5
LEAD = 8
TOGETHER = 6
MESH = pl.DeviceIdType.MESH


def spans(low, high, size):
    return [(at, min(size, high - at)) for at in range(low, high, size)]


def line_kernel(
    towers,
    density,
    light_in,
    gain_in,
    bias_in,
    shear_in,
    reverse_in,
    out,
    light,
    gain,
    bias,
    shear,
    reverse,
    volume,
    fields,
    outgoing,
    incoming,
    handed,
    sent_sem,
    halo_sem,
    hand_sem,
    part_sem,
    go_sem,
):
    planes, rows, cols = density.shape
    margin = rows // 2
    views = shear.shape[0]
    groups = 4
    share = rows // groups
    total_planes = planes * groups
    extinction = EXTINCTION / total_planes
    d = lax.axis_index("depth")
    h = lax.axis_index("height")
    above, below = (h - 1 >= 0) & (h - 1 < towers), (h + 1 >= 0) & (h + 1 < towers)
    end = LEAD + rows
    own_planes = pl.ds(2, planes)
    images, plane_sent, edge_sent, down_sent, up_sent, corner_sent, rest_sent, relay_sent, flank_edge_sent, flank_end_sent = range(10)
    slab_sent, slab_edge_sent, flank_sent = edge_sent, rest_sent, rest_sent
    pair_in, peer_in, edge_in, down_in, up_in, pair_corner_in, peer_corner_in, rest_in = range(8)
    slab_in, slab_edge_in, slab_end_in = pair_in, edge_in, peer_in
    flank_in, flank_edge_in, flank_end_in = pair_in, edge_in, peer_in

    own = pltpu.make_async_copy(
        density, volume.at[own_planes, pl.ds(LEAD, rows)], sent_sem.at[images]
    )
    own.start()

    scalars = [
        pltpu.make_async_copy(source, target, sent_sem.at[1 + index])
        for index, (source, target) in enumerate(
            zip((light_in, gain_in, bias_in, shear_in, reverse_in), (light, gain, bias, shear, reverse))
        )
    ]
    for scalar in scalars:
        scalar.start()

    def valid(step_d, step_h):
        ok = None
        for at, step, count in ((d, step_d, groups), (h, step_h, towers)):
            if step:
                test = (at + step >= 0) & (at + step < count)
                ok = test if ok is None else ok & test
        return ok

    barrier = pltpu.get_barrier_semaphore()
    expected = jnp.int32(0)
    greets = {at: [] for at in range(groups)}
    awaits = {at: [] for at in range(groups)}

    def greet(at, step_d, step_h, parity=None):
        greets[at].append((step_d, step_h, parity))
        awaits[at + step_d].append((-step_d, -step_h, parity if parity is None else (parity + step_h) % 2))

    for at in range(groups):
        mate = (at ^ 1) - at
        outer = at in (0, 3)
        for step_h in (1, -1):
            greet(at, mate if outer else 0, step_h)
            greet(at, 0 if outer else mate, step_h, 0)
        greet(at, mate, 0)
        if not outer:
            greet(at, -mate, 0)
            greet(at, -mate, 1)
    greet(0, 2, 0)

    def meets(at, step_d, step_h, parity):
        ok = (d == at) & valid(step_d, step_h)
        return ok if parity is None else ok & (lax.rem(h, 2) == parity)

    for at in range(groups):

        for step_d, step_h, parity in greets[at]:

            @pl.when(meets(at, step_d, step_h, parity))
            def _(target=(d + step_d, h + step_h)):
                pl.semaphore_signal(barrier, inc=1, device_id=target, device_id_type=MESH)

        for step in awaits[at]:
            expected = expected + jnp.where(meets(at, *step), 1, 0)

    for scalar in scalars:
        scalar.wait()
    own.wait()

    lz, ly, lx = light[0], light[1], light[2]
    half_gain = [0.5 * gain[c] for c in range(3)]
    half_bias = [0.5 * bias[c] for c in range(3)]
    inside = jnp.where(below, 1.0, 0.0)

    def shade(plane, row, count, keep, loose=False):
        at = LEAD + row
        centre = volume[plane, at : at + count]
        lane = lax.broadcasted_iota(jnp.int32, (count, cols), 1)
        following = jnp.where(lane == cols - 1, 0.0, pltpu.roll(centre, cols - 1, 1))
        previous = jnp.where(lane == 0, 0.0, pltpu.roll(centre, 1, 1))
        dx = following - previous
        dz = volume[plane + 1, at : at + count] - volume[plane - 1, at : at + count]
        below_it = pltpu.roll(centre, count - 1, 0) if loose else volume[plane, at + 1 : at + 1 + count]
        dy = below_it - volume[plane, at - 1 : at - 1 + count]
        facing = (lz * dz + ly * dy + lx * dx) * lax.rsqrt(4.0 + dz * dz + dy * dy + dx * dx)
        shading = 0.25 + 1.5 * jnp.maximum(facing, 0.0)
        optical = extinction * (
            jnp.maximum(centre, 0.0) + jnp.log1p(jnp.exp(-jnp.abs(centre)))
        )
        opacity = jnp.tanh(0.5 * optical) * (1.0 + jnp.exp(-optical))
        if keep is not None:
            opacity = opacity * keep
        lit = 0.5 * (opacity * shading)
        to = pl.ds(row, count)
        for c in range(3):
            fields[c, plane, to] = lit + lit * jnp.tanh(half_gain[c] * centre + half_bias[c])
        fields[3, plane, to] = opacity

    def shade_box(low, high, top, bottom, loose=False):
        tiles = (bottom - top) // 8
        together = max(1, min(high - low, -(-TOGETHER // tiles)))
        looped = (high - low) // together if high - low > together else 0

        def some(plane, count):
            for step in range(count):
                for row, size in spans(top, min(bottom, rows), 16):
                    shade(plane + step, row, size, None, loose)
                for row, size in spans(max(top, rows), bottom, 16):
                    shade(plane + step, row, size, inside)

        if looped:

            def step(index, _):
                some(low + index * together, together)
                return 0

            lax.fori_loop(0, looped, step, 0)
        done = low + looped * together
        if done < high:
            some(done, high - done)

    def copy_to(source, target, sent, received, device):
        return pltpu.make_async_remote_copy(
            src_ref=source,
            dst_ref=target,
            send_sem=sent_sem.at[sent],
            recv_sem=received,
            device_id=device,
            device_id_type=MESH,
        )

    def over(first, second, swap):
        front = [jnp.where(swap, b, a) for a, b in zip(first, second)]
        behind = [jnp.where(swap, a, b) for a, b in zip(first, second)]
        clear = 1.0 - front[3]
        return [f + clear * b for f, b in zip(front, behind)]

    everything = (0, share)
    odd = lax.rem(h, 2) == 1
    distant = (lax.rem(h, 2) == 0) & (h > 0)
    ahead = jnp.where(h == towers // 2, views // 2, 1)
    some, rest = (0, ahead), (ahead, views)

    def load(ref, block, view, part):
        return [ref[block, view, c, pl.ds(*part)] for c in range(4)]

    def store(ref, block, view, part, image):
        for c in range(4):
            ref[block, view, c, pl.ds(*part)] = image[c]

    def each_view(body, start=0, stop=views):
        def step(view, _):
            body(view)
            return 0

        lax.fori_loop(start, stop, step, 0)

    def extent(at):
        low = {0: 2, 1: 1, 2: 2, 3: 3}[at]
        high = {0: planes + 1, 1: planes + 2, 2: planes + 3, 3: planes + 2}[at]
        reach = (at * planes + high - 3) * margin // total_planes
        return low, high, reach, min(margin, -(-(reach + 1) // 8) * 8)

    def brick(at):
        outer = at in (0, groups - 1)
        lower = at < groups // 2
        mate = at ^ 1
        first = at * planes - 2
        low, high, reach, border = extent(at)
        extra = -(-reach // 8) * 8
        mate_pair = pl.ds(0, 2) if lower else pl.ds(planes + 2, 2)
        edge = {0: planes + 1, 1: 1, 2: planes + 2, 3: 2}[at]
        mate_edge = {0: 1, 3: planes + 2}.get(at, edge)
        others = [2, 3] if lower else [0, 1]
        other = {0: 2, 1: 2, 2: 1, 3: 1}[at]
        peer = {1: 2, 2: 1}.get(at)
        halves = [(share // 2, share // 2), (0, share // 2)]
        parts = {0: halves, 1: [everything], 2: [everything], 3: [everything]}
        hand_at = {
            (block, part): index
            for index, (block, part) in enumerate((block, part) for block in others for part in parts[block])
        }

        def plane_copy(source, target, take, put, sent, received, device):
            return copy_to(
                volume.at[source, pl.ds(*take)],
                volume.at[target, pl.ds(*put)],
                sent,
                halo_sem.at[received],
                device,
            )

        own_pair = pl.ds(planes, 2) if lower else pl.ds(2, 2)
        own_peer = pl.ds(planes + 1, 1) if lower else pl.ds(2, 1)
        peer_target = pl.ds(1, 1) if lower else pl.ds(planes + 2, 1)
        peer_border = extent(peer)[3] if peer else None
        whole = (LEAD, rows)

        cut = rows - share
        soon, after = ((LEAD + share, cut), (LEAD, share)) if lower else ((LEAD, cut), (LEAD + cut, share))

        def pair_copy():
            return plane_copy(own_pair, mate_pair, soon, soon, plane_sent, pair_in, (mate, h))

        def pair_rest():
            return plane_copy(own_pair, mate_pair, after, after, rest_sent, rest_in, (mate, h))

        def peer_copy():
            return plane_copy(own_peer, peer_target, whole, whole, plane_sent, peer_in, (peer, h))

        def pair_relay(step):
            take, put = (LEAD, border), (end, border)
            return plane_copy(mate_pair, mate_pair, take, put, relay_sent, pair_corner_in, (d, h + step))

        def peer_corner(step, count):
            take, put = (LEAD, count), (end, count)
            return plane_copy(own_peer, peer_target, take, put, corner_sent, peer_corner_in, (d + peer - at, h + step))

        def edge_copy(step):
            take, put = (rows, LEAD), (0, LEAD)
            return plane_copy(edge, mate_edge, take, put, edge_sent, edge_in, (d + mate - at, h + step))

        span_high = 2 * planes + 2
        span_reach = extent(1)[2]
        span_rows = share + extent(1)[3]
        slab = pl.ds(planes + 2, planes)
        slab_end = pl.ds(2 * planes + 2, 1)

        def slab_copy():
            take = (LEAD, span_rows)
            return plane_copy(own_planes, slab, take, take, slab_sent, slab_in, (0 if at else 1, h))

        def slab_edge_copy(step):
            take, put = (rows, LEAD), (0, LEAD)
            return plane_copy(own_planes, slab, take, put, slab_edge_sent, slab_edge_in, (d + (-1 if at else 1), h + step))

        def slab_end_copy():
            take = (LEAD, span_rows)
            return plane_copy(pl.ds(2, 1), slab_end, take, take, slab_sent, slab_end_in, (0 if at else 2, h))

        flank = planes + 4
        flank_top = rows - share - LEAD
        flank_reach = (3 * planes - 1) * margin // total_planes
        flank_rows = min(extent(2)[3], -(-(flank_reach + 1) // 8) * 8)
        flank_planes = pl.ds(flank, planes)

        def flank_copy():
            take = (LEAD + flank_top, share + LEAD)
            return plane_copy(own_planes, flank_planes, take, take, flank_sent, flank_in, (3 if at == 2 else 2, h))

        def flank_edge_copy(step):
            take, put = (LEAD, flank_rows), (end, flank_rows)
            return plane_copy(own_planes, flank_planes, take, put, flank_edge_sent, flank_edge_in, (d + (1 if at == 2 else -1), h + step))

        def flank_end_copy():
            take = (LEAD + flank_top, share + LEAD + flank_rows)
            return plane_copy(pl.ds(1, 1), pl.ds(flank - 1, 1), take, take, flank_end_sent, flank_end_in, (3 if at == 2 else 2, h))

        def down_copy(step):
            return copy_to(
                volume.at[own_planes, pl.ds(rows, LEAD)],
                volume.at[own_planes, pl.ds(0, LEAD)],
                down_sent,
                halo_sem.at[down_in],
                (d, h + step),
            )

        def up_copy(step):
            return copy_to(
                volume.at[own_planes, pl.ds(LEAD, border)],
                volume.at[own_planes, pl.ds(end, border)],
                up_sent,
                halo_sem.at[up_in],
                (d, h + step),
            )

        def hand(view, block, part):
            index = hand_at[block, part] * views + view
            return copy_to(
                outgoing.at[block, view, :, pl.ds(*part)],
                handed.at[block, view, :, pl.ds(*part)],
                images,
                hand_sem.at[index],
                (mate, h),
            )

        def send(view, block, part):
            slot = 0 if block == mate else views
            return copy_to(
                outgoing.at[block, view, :, pl.ds(*part)],
                incoming.at[at, view, :, pl.ds(*part)],
                images,
                part_sem.at[slot + view],
                (block, h),
            )

        def receive(view, source):
            slot = 0 if source == mate else views
            return copy_to(
                outgoing.at[at, view],
                incoming.at[source, view],
                images,
                part_sem.at[slot + view],
                (source, h),
            )

        def partial(view, block, part, span=None):
            step = shear[view]
            backward = reverse[view]
            count = high - low if span is None else 2 * planes
            size = part[1]
            colour = [jnp.zeros((size, cols), jnp.float32) for _ in range(3)]
            clear = jnp.ones((size, cols), jnp.float32)
            covered = jnp.zeros((size, cols), jnp.float32)
            for i in range(count):
                index = jnp.where(backward == 1, count - 1 - i, i)
                if span is None:
                    plane, depth, limit = low + index, first + low + index, reach
                else:
                    plane, depth, limit = span(index)
                offset = lax.div(depth * step, jnp.int32(total_planes))
                offset = jnp.minimum(jnp.maximum(offset, 0), limit)
                rows_at = pl.ds(offset + block * share + part[0], size)
                for c in range(3):
                    colour[c] = colour[c] + clear * fields[c, plane, rows_at]
                covered = covered + clear * fields[3, plane, rows_at]
                clear = 1.0 - covered
            return colour + [covered]

        def send_mate():
            def one(view):
                store(outgoing, mate, view, everything, partial(view, mate, everything))
                send(view, mate, everything).start()

            each_view(one)

        def keep_own():
            def front_pair(index):
                return 2 + index, index, span_reach

            def back_pair(index):
                return jnp.where(index < planes, flank + index, index - planes + 2), 2 * planes + index, reach

            span = {0: front_pair, 3: back_pair}.get(at)
            each_view(lambda view: store(incoming, at, view, everything, partial(view, at, everything, span)))

        def hand_over(block, part=everything, which=(0, views)):
            def one(view):
                store(outgoing, block, view, part, partial(view, block, part))
                hand(view, block, part).start()

            each_view(one, *which)

        def pass_on(block, part=everything, which=(0, views)):
            def one(view):
                mine = partial(view, block, part)
                hand(view, block, part).wait_recv()
                theirs = load(handed, block, view, part)
                swap = reverse[view] == 1
                merged = over(theirs, mine, swap) if lower else over(mine, theirs, swap)
                store(outgoing, block, view, part, merged)
                send(view, block, part).start()

            each_view(one, *which)

        def images_gone(blocks):
            gone = pl.ds(0, blocks)
            copy_to(outgoing.at[gone], handed.at[gone], images, hand_sem.at[0], (mate, h)).wait_send()

        def begin():
            with jax.named_scope("barrier"):
                pl.semaphore_wait(barrier, expected)
            if outer:
                pair_copy().start()
                if lower:
                    pair_rest().start()
            else:

                @pl.when(jnp.logical_not(odd))
                def _():
                    pl.semaphore_signal(go_sem, inc=1, device_id=(mate, h), device_id_type=MESH)

                peer_copy().start()
                (slab_copy if lower else slab_end_copy)().start()
                if not lower:
                    flank_copy().start()
                columns()

        def columns():
            if outer:

                @pl.when(jnp.logical_not(odd))
                def _():
                    with jax.named_scope("w_go"):
                        pl.semaphore_wait(go_sem, 1)

            @pl.when(below)
            def _():
                down_copy(1).start()
                if outer:
                    edge_copy(1).start()
                if at == 1:
                    slab_edge_copy(1).start()

            @pl.when(above)
            def _():
                if not outer:
                    peer_corner(-1, peer_border).start()
                if at == 2:
                    flank_edge_copy(-1).start()
                up_copy(-1).start()

        def blank():
            if outer:
                volume[1 if lower else planes + 2] = jnp.zeros(volume.shape[1:], jnp.float32)

            @pl.when(jnp.logical_not(above))
            def _():
                volume[:, :LEAD] = jnp.zeros((2 * planes + 5, LEAD, cols), jnp.float32)

            @pl.when(jnp.logical_not(below))
            def _():
                volume[:, end : end + border] = jnp.zeros((2 * planes + 5, border, cols), jnp.float32)

        def top_landed():
            @pl.when(above)
            def _():
                with jax.named_scope("w_down"):
                    down_copy(-1).wait_recv()

        def bottom_landed():
            @pl.when(below)
            def _():
                with jax.named_scope("w_up"):
                    up_copy(1).wait_recv()

        def peer_corner_landed():
            @pl.when(below)
            def _():
                with jax.named_scope("w_pcorner"):
                    peer_corner(1, border).wait_recv()

        def pair_corner_landed():
            @pl.when(below)
            def _():
                with jax.named_scope("w_corner"):
                    pair_relay(1).wait_recv()

        def edge_landed():
            @pl.when(above)
            def _():
                with jax.named_scope("w_edge"):
                    edge_copy(-1).wait_recv()

        blank()
        if at == 0:
            shade_box(low, high, LEAD, rows - LEAD)
            begin()
            with jax.named_scope("hand2"):
                hand_over(2)
            columns()
            top_landed()
            bottom_landed()
            shade_box(low, high, rows - LEAD, rows + extra)
            with jax.named_scope("hand3"):
                hand_over(3)
            shade_box(low, high, 0, LEAD)
            with jax.named_scope("mate"):
                send_mate()
            with jax.named_scope("w_slab"):
                slab_copy().wait_recv()

                @pl.when(above)
                def _():
                    slab_edge_copy(-1).wait_recv()

                slab_end_copy().wait_recv()
            shade_box(high, span_high, 0, -(-(share + span_reach) // 8) * 8)
            keep_own()
        elif at == 3:
            begin()
            shade_box(low, high, LEAD, rows - LEAD)
            with jax.named_scope("hand0b"):
                hand_over(0, halves[0])
            pair_rest().start()
            columns()
            shade_box(low, high, rows - LEAD, rows, True)

            def early():
                top_landed()
                shade_box(low, high, 0, LEAD)
                with jax.named_scope("hand0a"):
                    hand_over(0, halves[1])

            def late(which):
                with jax.named_scope("hand1"):
                    hand_over(1, everything, which)

            @pl.when(distant)
            def _():
                late(some)
                early()
                late(rest)

            @pl.when(h == 0)
            def _():
                early()
                late((0, views))

            @pl.when(odd)
            def _():
                early()
                late((0, views))

            bottom_landed()
            shade_box(low, high, rows - LEAD, rows)
            shade_box(low, high, rows, rows + extra)
            with jax.named_scope("mate"):
                send_mate()
            with jax.named_scope("w_flank"):
                flank_copy().wait_recv()

                @pl.when(below)
                def _():
                    flank_edge_copy(1).wait_recv()

                flank_end_copy().wait_recv()
            top_row, bottom_row = rows - share, rows + flank_rows
            there = pl.ds(LEAD + top_row, bottom_row - top_row)
            volume[1, there] = volume[flank + planes - 1, there]
            volume[flank + planes, there] = volume[2, there]
            shade_box(flank, flank + planes, top_row, bottom_row)
            shade_box(2, 3, top_row, bottom_row)
            keep_own()
        else:
            shade_box(3, planes + 1, LEAD, rows - LEAD)
            begin()
            far_edge = planes + 1 if lower else 2
            seam = min(2 if lower else planes + 1, edge)


            def top():
                top_landed()
                edge_landed()
                shade_box(low, high, 0, LEAD)

            def relay():
                @pl.when(above)
                def _():
                    pair_relay(-1).start()

            def rest_landed():
                with jax.named_scope("w_rest"):
                    pair_rest().wait_recv()
                if lower:
                    relay()
                    shade_box(seam, seam + 2, LEAD, share + LEAD)
                else:
                    shade_box(seam, seam + 2, rows - share - LEAD, rows - LEAD)

            def bottom():
                bottom_landed()
                pair_corner_landed()
                if lower:
                    peer_corner_landed()
                shade_box(low, high, rows - LEAD, rows + extra)

            with jax.named_scope("w_peer"):
                peer_copy().wait_recv()
            shade_box(far_edge, far_edge + 1, LEAD, rows - LEAD)
            if lower:
                shade_box(3, planes + 2, rows - LEAD, rows, True)
            with jax.named_scope("w_pair"):
                pair_copy().wait_recv()
            if lower:
                shade_box(seam, seam + 2, share + LEAD, rows - LEAD)
                rest_landed()
                with jax.named_scope("pass2"):
                    pass_on(2)
                top()
                bottom()
                with jax.named_scope("pass3"):
                    pass_on(3)
            else:
                relay()
                shade_box(seam, seam + 2, LEAD, rows - share - LEAD)
                with jax.named_scope("pass0b"):
                    pass_on(0, halves[0])
                peer_corner_landed()
                flank_end_copy().start()
                rest_landed()

                def early():
                    top()
                    with jax.named_scope("pass0a"):
                        pass_on(0, halves[1])

                @pl.when(distant)
                def _():
                    with jax.named_scope("pass1"):
                        pass_on(1, everything, some)
                    early()
                    pass_on(1, everything, rest)

                @pl.when(jnp.logical_not(distant))
                def _():
                    early()
                    with jax.named_scope("pass1"):
                        pass_on(1)

                bottom()
            keep_own()

        def finish(view):
            swap = reverse[view] == 1
            near = load(incoming, at, view, everything)
            if not outer:
                with jax.named_scope("w_mate"):
                    receive(view, mate).wait_recv()
                theirs = load(incoming, mate, view, everything)
                near = over(near, theirs, swap) if at < mate else over(theirs, near, swap)
            with jax.named_scope("w_other"):
                receive(view, other).wait_recv()
            far = load(incoming, other, view, everything)
            total = over(near, far, swap) if lower else over(far, near, swap)
            for c in range(4):
                out[c, view] = total[c]

        for view in range(views):
            finish(view)

        if outer:
            pair_copy().wait_send()
            pair_rest().wait_send()
        else:
            peer_copy().wait_send()
            (slab_copy if lower else slab_end_copy)().wait_send()
            if not lower:
                flank_copy().wait_send()
                flank_end_copy().wait_send()

        @pl.when(below)
        def _():
            down_copy(1).wait_send()
            if outer:
                edge_copy(1).wait_send()
            if at == 1:
                slab_edge_copy(1).wait_send()

        @pl.when(above)
        def _():
            up_copy(-1).wait_send()
            if not outer:
                peer_corner(-1, peer_border).wait_send()
                pair_relay(-1).wait_send()
            if at == 2:
                flank_edge_copy(-1).wait_send()

        images_gone(3 if outer else 2)
    for at in range(groups):

        @pl.when(d == at)
        def _():
            brick(at)


def kernel(
    groups,
    towers,
    density,
    light,
    gain,
    bias,
    shear,
    reverse,
    out,
    volume,
    fields,
    outgoing,
    incoming,
    handed,
    local_sem,
    halo_send,
    halo_recv,
    hand_send,
    hand_recv,
    part_send,
    part_recv,
):
    planes, rows, cols = density.shape
    margin = rows // 2
    views = shear.shape[0]
    share = rows // groups
    total_planes = planes * groups
    extinction = EXTINCTION / total_planes
    d = lax.axis_index("depth")
    h = lax.axis_index("height")
    end = LEAD + rows
    tall = end + margin

    own = pltpu.make_async_copy(
        density, volume.at[pl.ds(1, planes), pl.ds(LEAD, rows)], local_sem
    )
    own.start()

    def near(step_d, step_h):
        ok = None
        for at, step, count in ((d, step_d, groups), (h, step_h, towers)):
            if step:
                test = (at + step >= 0) & (at + step < count)
                ok = test if ok is None else ok & test
        return ok, (d + step_d, h + step_h)

    barrier = pltpu.get_barrier_semaphore()
    beside = [(0, 1), (0, -1), (1, 1), (1, -1), (-1, 1), (-1, -1), (1, 0), (-1, 0)]
    if groups > 4:
        beside += [(step * hop, 0) for hop in range(2, groups) for step in (1, -1)]
    expected = jnp.int32(0)
    for step_d, step_h in beside:
        ok, target = near(step_d, step_h)
        expected = expected + jnp.where(ok, 1, 0)

        @pl.when(ok)
        def _(target=target):
            pl.semaphore_signal(barrier, inc=1, device_id=target, device_id_type=MESH)

    pl.semaphore_wait(barrier, expected)

    whole = pl.ds(0, planes)
    inner = pl.ds(1, planes)
    first, last = pl.ds(0, 1), pl.ds(planes - 1, 1)
    low, high = pl.ds(0, 1), pl.ds(planes + 1, 1)
    routes = [
        ((1, 0), last, (0, rows), low, LEAD),
        ((-1, 0), first, (0, rows), high, LEAD),
        ((0, 1), whole, (rows - LEAD, LEAD), inner, 0),
        ((0, -1), whole, (0, margin), inner, end),
        ((1, -1), last, (0, margin), low, end),
        ((-1, -1), first, (0, margin), high, end),
    ]

    def halo(index, reach):
        step, from_planes, (row, count), to_planes, to_row = routes[index]
        return pltpu.make_async_remote_copy(
            src_ref=density.at[from_planes, pl.ds(row, count)],
            dst_ref=volume.at[to_planes, pl.ds(to_row, count)],
            send_sem=halo_send.at[index],
            recv_sem=halo_recv.at[index],
            device_id=reach,
            device_id_type=MESH,
        )

    for index, route in enumerate(routes):
        ok, target = near(*route[0])

        @pl.when(ok)
        def _(index=index, target=target):
            halo(index, target).start()

    @pl.when(d == 0)
    def _():
        volume[0] = jnp.zeros(volume.shape[1:], jnp.float32)

    @pl.when(d == groups - 1)
    def _():
        volume[planes + 1] = jnp.zeros(volume.shape[1:], jnp.float32)

    @pl.when(h == 0)
    def _():
        volume[1 : planes + 1, :LEAD] = jnp.zeros((planes, LEAD, cols), jnp.float32)

    @pl.when(h == towers - 1)
    def _():
        volume[:, end:tall] = jnp.zeros((planes + 2, margin, cols), jnp.float32)

    own.wait()

    lz, ly, lx = light[0], light[1], light[2]
    half_gain = [0.5 * gain[c] for c in range(3)]
    half_bias = [0.5 * bias[c] for c in range(3)]

    def shade(plane, row, count, keep):
        at = LEAD + row
        centre = volume[plane, at : at + count]
        lane = lax.broadcasted_iota(jnp.int32, (count, cols), 1)
        following = jnp.where(lane == cols - 1, 0.0, pltpu.roll(centre, cols - 1, 1))
        previous = jnp.where(lane == 0, 0.0, pltpu.roll(centre, 1, 1))
        dx = following - previous
        dz = volume[plane + 1, at : at + count] - volume[plane - 1, at : at + count]
        dy = volume[plane, at + 1 : at + 1 + count] - volume[plane, at - 1 : at - 1 + count]
        facing = (lz * dz + ly * dy + lx * dx) * lax.rsqrt(4.0 + dz * dz + dy * dy + dx * dx)
        shading = 0.25 + 1.5 * jnp.maximum(facing, 0.0)
        optical = extinction * (
            jnp.maximum(centre, 0.0) + jnp.log1p(jnp.exp(-jnp.abs(centre)))
        )
        opacity = jnp.tanh(0.5 * optical) * (1.0 + jnp.exp(-optical))
        if keep is not None:
            opacity = opacity * keep
        lit = 0.5 * (opacity * shading)
        to = pl.ds(row, count)
        for c in range(3):
            fields[c, plane - 1, to] = lit + lit * jnp.tanh(half_gain[c] * centre + half_bias[c])
        fields[3, plane - 1, to] = opacity

    inside = jnp.where(h < towers - 1, 1.0, 0.0)

    def early(plane, _):
        for row, count in spans(LEAD, rows - LEAD, 16):
            shade(plane, row, count, None)
        return 0

    lax.fori_loop(2, planes, early, 0)

    def landed(index):
        step_d, step_h = routes[index][0]
        ok, source = near(-step_d, -step_h)

        @pl.when(ok)
        def _():
            halo(index, source).wait_recv()

    def shade_low():
        for index in (0, 1, 2):
            landed(index)
        for plane in range(1, planes + 1):
            shade(plane, 0, LEAD, None)
        for row, count in spans(LEAD, rows - LEAD, 16):
            for plane in (1, planes):
                shade(plane, row, count, None)

    def shade_high():
        for index in (3, 4, 5):
            landed(index)

        def bottom(at, _):
            for plane in (2 * at + 1, 2 * at + 2):
                shade(plane, rows - LEAD, LEAD, None)
                for row, count in spans(rows, rows + margin, 16):
                    shade(plane, row, count, inside)
            return 0

        lax.fori_loop(0, planes // 2, bottom, 0)

    first_plane = d * planes

    def partial(view, block):
        step = shear[view]
        backward = reverse[view]
        colour = [jnp.zeros((share, cols), jnp.float32) for _ in range(3)]
        clear = jnp.ones((share, cols), jnp.float32)
        covered = jnp.zeros((share, cols), jnp.float32)
        for i in range(planes):
            plane = i + backward * (planes - 1 - 2 * i)
            offset = lax.div((first_plane + plane) * step, jnp.int32(total_planes))
            at = pl.ds(offset + block * share, share)
            for c in range(3):
                colour[c] = colour[c] + clear * fields[c, plane, at]
            covered = covered + clear * fields[3, plane, at]
            clear = 1.0 - covered
        return colour + [covered]

    odd = lax.rem(d, 2)
    out_step = 2 * odd - 1
    mate = d - out_step
    pair = lax.div(d, 2)
    beyond = odd * (groups - 1 - d) + (1 - odd) * d
    handing = odd * (d - 1) + (1 - odd) * (groups - 2 - d)

    def over(first, second, swap):
        front = [jnp.where(swap, b, a) for a, b in zip(first, second)]
        behind = [jnp.where(swap, a, b) for a, b in zip(first, second)]
        clear = 1.0 - front[3]
        return [f + clear * b for f, b in zip(front, behind)]

    def load(ref, block, view):
        return [ref[block, view, c] for c in range(4)]

    def store(ref, block, view, image):
        for c in range(4):
            ref[block, view, c] = image[c]

    def hand(view, block):
        return pltpu.make_async_remote_copy(
            src_ref=outgoing.at[block, view],
            dst_ref=handed.at[block, view],
            send_sem=hand_send.at[view, block],
            recv_sem=hand_recv.at[view, block],
            device_id=(mate, h),
            device_id_type=MESH,
        )

    def send(view, block):
        return pltpu.make_async_remote_copy(
            src_ref=outgoing.at[block, view],
            dst_ref=incoming.at[d, view],
            send_sem=part_send.at[view, block],
            recv_sem=part_recv.at[view, d],
            device_id=(block, h),
            device_id_type=MESH,
        )

    def receive(view, source):
        return pltpu.make_async_remote_copy(
            src_ref=outgoing.at[source, view],
            dst_ref=incoming.at[source, view],
            send_sem=part_send.at[view, source],
            recv_sem=part_recv.at[view, source],
            device_id=(source, h),
            device_id_type=MESH,
        )

    def each(count, body):
        def step(k, _):
            body(k)
            return 0

        lax.fori_loop(0, count, step, 0)

    def hand_over(view, k):
        block = odd * k + (1 - odd) * (groups - 1 - k)
        store(outgoing, block, view, partial(view, block))
        hand(view, block).start()

    def prepare(view, k):
        block = d + out_step * (1 + k)
        store(outgoing, block, view, partial(view, block))

    def to_mate(view):
        store(outgoing, mate, view, partial(view, mate))
        send(view, mate).start()

    def pass_on(view, k):
        block = odd * (groups - 1 - k) + (1 - odd) * k
        hand(view, block).wait_recv()
        own_part, other = load(outgoing, block, view), load(handed, block, view)
        swap = reverse[view] != odd
        store(outgoing, block, view, over(own_part, other, swap))
        send(view, block).start()

    reach = lax.div((first_plane + planes - 1) * margin, jnp.int32(total_planes))

    def hand_round(early):
        def one(k):
            block = odd * k + (1 - odd) * (groups - 1 - k)
            ready = ((block + 1) * share + reach <= rows - LEAD) & (odd == 1)

            @pl.when(ready if early else jnp.logical_not(ready))
            def _():
                each(views, lambda view: hand_over(view, k))

        each(handing, one)

    shade_low()
    hand_round(True)
    shade_high()
    hand_round(False)
    each(views, to_mate)
    each(views, lambda view: each(beyond, lambda k: prepare(view, k)))
    each(views, lambda view: store(incoming, d, view, partial(view, d)))
    each(beyond, lambda k: each(views, lambda view: pass_on(view, k)))

    def finish(view):
        swap = reverse[view] == 1
        receive(view, mate).wait_recv()
        both = over(load(incoming, d, view), load(incoming, mate, view), reverse[view] != odd)
        store(incoming, 2 * pair + 1, view, both)
        sources = [jnp.where(j > pair, 2 * j, 2 * j + 1) for j in range(groups // 2)]
        for j, source in enumerate(sources):

            @pl.when(j != pair)
            def _():
                receive(view, source).wait_recv()

        total = load(incoming, sources[0], view)
        for source in sources[1:]:
            total = over(total, load(incoming, source, view), swap)
        for c in range(4):
            out[c, view] = total[c]

    for view in range(views):
        finish(view)

    for index, route in enumerate(routes):
        ok, target = near(*route[0])

        @pl.when(ok)
        def _(index=index, target=target):
            halo(index, target).wait_send()

    def sent(view):
        send(view, mate).wait_send()
        each(handing, lambda k: hand(view, d - out_step * (2 + k)).wait_send())
        each(beyond, lambda k: send(view, d + out_step * (1 + k)).wait_send())

    each(views, sent)


def general(groups, towers, density, light, gain, bias, shear, reverse):
    planes, rows, cols = density.shape
    views = shear.shape[0]
    share = rows // groups
    tall = LEAD + rows + rows // 2
    scalars = pl.BlockSpec(memory_space=pltpu.SMEM)
    return pl.pallas_call(
        functools.partial(kernel, groups, towers),
        name="render",
        out_shape=pltpu.VMEM((4, views, share, cols), jnp.float32),
        in_specs=[pl.BlockSpec(memory_space=pltpu.HBM)] + [scalars] * 5,
        out_specs=pl.BlockSpec(memory_space=pltpu.VMEM),
        scratch_shapes=[
            pltpu.VMEM((planes + 2, tall + LEAD, cols), jnp.float32),
            pltpu.VMEM((4, planes, rows + rows // 2, cols), jnp.float32),
            pltpu.VMEM((groups, views, 4, share, cols), jnp.float32),
            pltpu.VMEM((groups, views, 4, share, cols), jnp.float32),
            pltpu.VMEM((groups, views, 4, share, cols), jnp.float32),
            pltpu.SemaphoreType.DMA,
            pltpu.SemaphoreType.DMA((6,)),
            pltpu.SemaphoreType.DMA((6,)),
            pltpu.SemaphoreType.DMA((views, groups)),
            pltpu.SemaphoreType.DMA((views, groups)),
            pltpu.SemaphoreType.DMA((views, groups)),
            pltpu.SemaphoreType.DMA((views, groups)),
        ],
        compiler_params=pltpu.CompilerParams(collective_id=0, has_side_effects=True, vmem_limit_bytes=60 * 1024 * 1024),
    )(density, light, gain, bias, shear, reverse)


def line(towers, density, light, gain, bias, shear, reverse):
    planes, rows, cols = density.shape
    views = shear.shape[0]
    groups = 4
    share = rows // groups
    whole = pl.BlockSpec(memory_space=pltpu.HBM)
    images = pltpu.VMEM((groups, views, 4, share, cols), jnp.float32)
    return pl.pallas_call(
        functools.partial(line_kernel, towers),
        name="render",
        out_shape=pltpu.VMEM((4, views, share, cols), jnp.float32),
        in_specs=[whole] * 6,
        out_specs=pl.BlockSpec(memory_space=pltpu.VMEM),
        scratch_shapes=[pltpu.SMEM(scalar.shape, scalar.dtype) for scalar in (light, gain, bias, shear, reverse)]
        + [
            pltpu.VMEM((2 * planes + 5, LEAD + rows + rows // 2 + LEAD, cols), jnp.float32),
            pltpu.VMEM((4, 2 * planes + 4, rows + rows // 2, cols), jnp.float32),
            images,
            images,
            images,
            pltpu.SemaphoreType.DMA((10,)),
            pltpu.SemaphoreType.DMA((8,)),
            pltpu.SemaphoreType.DMA((3 * views,)),
            pltpu.SemaphoreType.DMA((2 * views,)),
            pltpu.SemaphoreType.REGULAR,
        ],
        compiler_params=pltpu.CompilerParams(collective_id=0, has_side_effects=True, vmem_limit_bytes=60 * 1024 * 1024),
    )(density, light, gain, bias, shear, reverse)


def on_device(groups, towers, density, light, gain, bias, shear, reverse):
    planes, rows, _ = density.shape
    if groups == 4 and planes >= 8 and rows % 64 == 0:
        return line(towers, density, light, gain, bias, shear, reverse)
    return general(groups, towers, density, light, gain, bias, shear, reverse)


def solution(mesh):
    groups, towers = mesh.shape["depth"], mesh.shape["height"]
    placed = (P("depth", "height", None), P(), P(), P(), P(), P())
    return jax.shard_map(
        functools.partial(on_device, groups, towers),
        mesh=mesh,
        in_specs=placed,
        out_specs=P(None, None, ("height", "depth"), None),
        check_vma=False,
    )
```

```python
import functools

import jax
import jax.numpy as jnp
from jax import lax
from jax.experimental import pallas as pl
from jax.experimental.pallas import tpu as pltpu
from jax.sharding import PartitionSpec as P

EXTINCTION = 2.5
LEAD = 8
TOGETHER = 6
MESH = pl.DeviceIdType.MESH


def spans(low, high, size):
    return [(at, min(size, high - at)) for at in range(low, high, size)]


def line_kernel(
    towers,
    density,
    light_in,
    gain_in,
    bias_in,
    shear_in,
    reverse_in,
    out,
    light,
    gain,
    bias,
    shear,
    reverse,
    volume,
    fields,
    outgoing,
    incoming,
    handed,
    sent_sem,
    halo_sem,
    hand_sem,
    part_sem,
    go_sem,
):
    planes, rows, cols = density.shape
    margin = rows // 2
    views = shear.shape[0]
    groups = 4
    share = rows // groups
    total_planes = planes * groups
    extinction = EXTINCTION / total_planes
    d = lax.axis_index("depth")
    h = lax.axis_index("height")
    above, below = (h - 1 >= 0) & (h - 1 < towers), (h + 1 >= 0) & (h + 1 < towers)
    end = LEAD + rows
    own_planes = pl.ds(2, planes)
    images, plane_sent, edge_sent, down_sent, up_sent, corner_sent, rest_sent, relay_sent, flank_edge_sent, flank_end_sent = range(10)
    slab_sent, slab_edge_sent, flank_sent = edge_sent, rest_sent, rest_sent
    pair_in, peer_in, edge_in, down_in, up_in, pair_corner_in, peer_corner_in, rest_in = range(8)
    slab_in, slab_edge_in, slab_end_in = pair_in, edge_in, peer_in
    flank_in, flank_edge_in, flank_end_in = pair_in, edge_in, peer_in

    early_planes = jnp.where(d < groups // 2, planes - 2, 0)
    later_planes = jnp.where(d < groups // 2, 0, 2)
    own, own_rest = (
        pltpu.make_async_copy(
            density.at[pl.ds(start, count)],
            volume.at[pl.ds(2 + start, count), pl.ds(LEAD, rows)],
            sent_sem.at[index],
        )
        for start, count, index in ((early_planes, 2, images), (later_planes, planes - 2, relay_sent))
    )
    own.start()
    own_rest.start()

    scalars = [
        pltpu.make_async_copy(source, target, sent_sem.at[(edge_sent, down_sent, up_sent, corner_sent, rest_sent)[index]])
        for index, (source, target) in enumerate(
            zip((light_in, gain_in, bias_in, shear_in, reverse_in), (light, gain, bias, shear, reverse))
        )
    ]
    for scalar in scalars:
        scalar.start()

    def valid(step_d, step_h):
        ok = None
        for at, step, count in ((d, step_d, groups), (h, step_h, towers)):
            if step:
                test = (at + step >= 0) & (at + step < count)
                ok = test if ok is None else ok & test
        return ok

    barrier = pltpu.get_barrier_semaphore()
    expected = jnp.int32(0)
    greets = {at: [] for at in range(groups)}
    awaits = {at: [] for at in range(groups)}

    def greet(at, step_d, step_h, parity=None):
        greets[at].append((step_d, step_h, parity))
        awaits[at + step_d].append((-step_d, -step_h, parity if parity is None else (parity + step_h) % 2))

    for at in range(groups):
        mate = (at ^ 1) - at
        outer = at in (0, 3)
        for step_h in (1, -1):
            greet(at, mate if outer else 0, step_h)
            greet(at, 0 if outer else mate, step_h, 0)
        greet(at, mate, 0)
        if not outer:
            greet(at, -mate, 0)
            greet(at, -mate, 1)
    greet(0, 2, 0)

    def meets(at, step_d, step_h, parity):
        ok = (d == at) & valid(step_d, step_h)
        return ok if parity is None else ok & (lax.rem(h, 2) == parity)

    for at in range(groups):

        for step_d, step_h, parity in greets[at]:

            @pl.when(meets(at, step_d, step_h, parity))
            def _(target=(d + step_d, h + step_h)):
                pl.semaphore_signal(barrier, inc=1, device_id=target, device_id_type=MESH)

        for step in awaits[at]:
            expected = expected + jnp.where(meets(at, *step), 1, 0)

    own.wait()

    @pl.when(d == groups - 1)
    def _():
        with jax.named_scope("barrier"):
            pl.semaphore_wait(barrier, expected)
        first_pair = volume.at[pl.ds(2, 2), pl.ds(LEAD, rows - share)]
        first_target = volume.at[pl.ds(planes + 2, 2), pl.ds(LEAD, rows - share)]
        pltpu.make_async_remote_copy(
            src_ref=first_pair,
            dst_ref=first_target,
            send_sem=sent_sem.at[plane_sent],
            recv_sem=halo_sem.at[pair_in],
            device_id=(d - 1, h),
            device_id_type=MESH,
        ).start()

    for scalar in scalars:
        scalar.wait()
    own_rest.wait()

    lz, ly, lx = light[0], light[1], light[2]
    half_gain = [0.5 * gain[c] for c in range(3)]
    half_bias = [0.5 * bias[c] for c in range(3)]
    inside = jnp.where(below, 1.0, 0.0)

    def shade(plane, row, count, keep, loose=False):
        at = LEAD + row
        centre = volume[plane, at : at + count]
        lane = lax.broadcasted_iota(jnp.int32, (count, cols), 1)
        following = jnp.where(lane == cols - 1, 0.0, pltpu.roll(centre, cols - 1, 1))
        previous = jnp.where(lane == 0, 0.0, pltpu.roll(centre, 1, 1))
        dx = following - previous
        dz = volume[plane + 1, at : at + count] - volume[plane - 1, at : at + count]
        below_it = pltpu.roll(centre, count - 1, 0) if loose else volume[plane, at + 1 : at + 1 + count]
        dy = below_it - volume[plane, at - 1 : at - 1 + count]
        facing = (lz * dz + ly * dy + lx * dx) * lax.rsqrt(4.0 + dz * dz + dy * dy + dx * dx)
        shading = 0.25 + 1.5 * jnp.maximum(facing, 0.0)
        optical = extinction * (
            jnp.maximum(centre, 0.0) + jnp.log1p(jnp.exp(-jnp.abs(centre)))
        )
        opacity = jnp.tanh(0.5 * optical) * (1.0 + jnp.exp(-optical))
        if keep is not None:
            opacity = opacity * keep
        lit = 0.5 * (opacity * shading)
        to = pl.ds(row, count)
        for c in range(3):
            fields[c, plane, to] = lit + lit * jnp.tanh(half_gain[c] * centre + half_bias[c])
        fields[3, plane, to] = opacity

    def shade_box(low, high, top, bottom, loose=False):
        tiles = (bottom - top) // 8
        together = max(1, min(high - low, -(-TOGETHER // tiles)))
        looped = (high - low) // together if high - low > together else 0

        def some(plane, count):
            for step in range(count):
                for row, size in spans(top, min(bottom, rows), 16):
                    shade(plane + step, row, size, None, loose)
                for row, size in spans(max(top, rows), bottom, 16):
                    shade(plane + step, row, size, inside)

        if looped:

            def step(index, _):
                some(low + index * together, together)
                return 0

            lax.fori_loop(0, looped, step, 0)
        done = low + looped * together
        if done < high:
            some(done, high - done)

    def copy_to(source, target, sent, received, device):
        return pltpu.make_async_remote_copy(
            src_ref=source,
            dst_ref=target,
            send_sem=sent_sem.at[sent],
            recv_sem=received,
            device_id=device,
            device_id_type=MESH,
        )

    def over(first, second, swap):
        front = [jnp.where(swap, b, a) for a, b in zip(first, second)]
        behind = [jnp.where(swap, a, b) for a, b in zip(first, second)]
        clear = 1.0 - front[3]
        return [f + clear * b for f, b in zip(front, behind)]

    everything = (0, share)
    odd = lax.rem(h, 2) == 1
    distant = (lax.rem(h, 2) == 0) & (h > 0)
    ahead = jnp.where(h == towers // 2, views // 2, 1)
    some, rest = (0, ahead), (ahead, views - 1)

    def load(ref, block, view, part):
        return [ref[block, view, c, pl.ds(*part)] for c in range(4)]

    def store(ref, block, view, part, image):
        for c in range(4):
            ref[block, view, c, pl.ds(*part)] = image[c]

    def each_view(body, start=0, stop=views):
        def step(view, _):
            body(view)
            return 0

        lax.fori_loop(start, stop, step, 0)

    def extent(at):
        low = {0: 2, 1: 1, 2: 2, 3: 3}[at]
        high = {0: planes + 1, 1: planes + 2, 2: planes + 3, 3: planes + 2}[at]
        reach = (at * planes + high - 3) * margin // total_planes
        return low, high, reach, min(margin, -(-(reach + 1) // 8) * 8)

    def brick(at):
        outer = at in (0, groups - 1)
        lower = at < groups // 2
        mate = at ^ 1
        first = at * planes - 2
        low, high, reach, border = extent(at)
        extra = -(-reach // 8) * 8
        mate_pair = pl.ds(0, 2) if lower else pl.ds(planes + 2, 2)
        edge = {0: planes + 1, 1: 1, 2: planes + 2, 3: 2}[at]
        mate_edge = {0: 1, 3: planes + 2}.get(at, edge)
        others = [2, 3] if lower else [0, 1]
        other = {0: 2, 1: 2, 2: 1, 3: 1}[at]
        peer = {1: 2, 2: 1}.get(at)
        halves = [(share // 2, share // 2), (0, share // 2)]
        parts = {0: halves, 1: [everything], 2: [everything], 3: [everything]}
        hand_at = {
            (block, part): index
            for index, (block, part) in enumerate((block, part) for block in others for part in parts[block])
        }

        def plane_copy(source, target, take, put, sent, received, device):
            return copy_to(
                volume.at[source, pl.ds(*take)],
                volume.at[target, pl.ds(*put)],
                sent,
                halo_sem.at[received],
                device,
            )

        own_pair = pl.ds(planes, 2) if lower else pl.ds(2, 2)
        own_peer = pl.ds(planes + 1, 1) if lower else pl.ds(2, 1)
        peer_target = pl.ds(1, 1) if lower else pl.ds(planes + 2, 1)
        peer_border = extent(peer)[3] if peer else None
        whole = (LEAD, rows)

        cut = rows - share
        soon, after = ((LEAD + share, cut), (LEAD, share)) if lower else ((LEAD, cut), (LEAD + cut, share))

        def pair_copy():
            return plane_copy(own_pair, mate_pair, soon, soon, plane_sent, pair_in, (mate, h))

        def pair_rest():
            return plane_copy(own_pair, mate_pair, after, after, rest_sent, rest_in, (mate, h))

        def peer_copy():
            return plane_copy(own_peer, peer_target, whole, whole, plane_sent, peer_in, (peer, h))

        def pair_relay(step):
            take, put = (LEAD, border), (end, border)
            return plane_copy(mate_pair, mate_pair, take, put, relay_sent, pair_corner_in, (d, h + step))

        def peer_corner(step, count):
            take, put = (LEAD, count), (end, count)
            return plane_copy(own_peer, peer_target, take, put, corner_sent, peer_corner_in, (d + peer - at, h + step))

        def edge_copy(step):
            take, put = (rows, LEAD), (0, LEAD)
            return plane_copy(edge, mate_edge, take, put, edge_sent, edge_in, (d + mate - at, h + step))

        span_high = 2 * planes + 2
        span_reach = extent(1)[2]
        span_rows = share + extent(1)[3]
        slab = pl.ds(planes + 2, planes)
        slab_end = pl.ds(2 * planes + 2, 1)

        def slab_copy():
            take = (LEAD, span_rows)
            return plane_copy(own_planes, slab, take, take, slab_sent, slab_in, (0 if at else 1, h))

        def slab_edge_copy(step):
            take, put = (rows, LEAD), (0, LEAD)
            return plane_copy(own_planes, slab, take, put, slab_edge_sent, slab_edge_in, (d + (-1 if at else 1), h + step))

        def slab_end_copy():
            take = (LEAD, span_rows)
            return plane_copy(pl.ds(2, 1), slab_end, take, take, slab_sent, slab_end_in, (0 if at else 2, h))

        flank = planes + 4
        flank_top = rows - share - LEAD
        flank_reach = (3 * planes - 1) * margin // total_planes
        flank_rows = min(extent(2)[3], -(-(flank_reach + 1) // 8) * 8)
        flank_planes = pl.ds(flank, planes)

        def flank_copy():
            take = (LEAD + flank_top, share + LEAD)
            return plane_copy(own_planes, flank_planes, take, take, flank_sent, flank_in, (3 if at == 2 else 2, h))

        def flank_edge_copy(step):
            take, put = (LEAD, flank_rows), (end, flank_rows)
            return plane_copy(own_planes, flank_planes, take, put, flank_edge_sent, flank_edge_in, (d + (1 if at == 2 else -1), h + step))

        def flank_end_copy():
            take = (LEAD + flank_top, share + LEAD + flank_rows)
            return plane_copy(pl.ds(1, 1), pl.ds(flank - 1, 1), take, take, flank_end_sent, flank_end_in, (3 if at == 2 else 2, h))

        def down_copy(step):
            return copy_to(
                volume.at[own_planes, pl.ds(rows, LEAD)],
                volume.at[own_planes, pl.ds(0, LEAD)],
                down_sent,
                halo_sem.at[down_in],
                (d, h + step),
            )

        def up_copy(step):
            return copy_to(
                volume.at[own_planes, pl.ds(LEAD, border)],
                volume.at[own_planes, pl.ds(end, border)],
                up_sent,
                halo_sem.at[up_in],
                (d, h + step),
            )

        def hand(view, block, part):
            split = block == 1 and part in halves
            index = 3 * views - 1 + halves.index(part) if split else hand_at[block, part] * views + view
            return copy_to(
                outgoing.at[block, view, :, pl.ds(*part)],
                handed.at[block, view, :, pl.ds(*part)],
                images,
                hand_sem.at[index],
                (mate, h),
            )

        def send(view, block, part):
            slot = 0 if block == mate else views
            return copy_to(
                outgoing.at[block, view, :, pl.ds(*part)],
                incoming.at[at, view, :, pl.ds(*part)],
                images,
                part_sem.at[slot + view],
                (block, h),
            )

        def receive(view, source):
            slot = 0 if source == mate else views
            return copy_to(
                outgoing.at[at, view],
                incoming.at[source, view],
                images,
                part_sem.at[slot + view],
                (source, h),
            )

        def partial(view, block, part, span=None):
            step = shear[view]
            backward = reverse[view]
            count = high - low if span is None else 2 * planes
            size = part[1]
            colour = [jnp.zeros((size, cols), jnp.float32) for _ in range(3)]
            clear = jnp.ones((size, cols), jnp.float32)
            covered = jnp.zeros((size, cols), jnp.float32)
            for i in range(count):
                index = jnp.where(backward == 1, count - 1 - i, i)
                if span is None:
                    plane, depth, limit = low + index, first + low + index, reach
                else:
                    plane, depth, limit = span(index)
                offset = lax.div(depth * step, jnp.int32(total_planes))
                offset = jnp.minimum(jnp.maximum(offset, 0), limit)
                rows_at = pl.ds(offset + block * share + part[0], size)
                for c in range(3):
                    colour[c] = colour[c] + clear * fields[c, plane, rows_at]
                covered = covered + clear * fields[3, plane, rows_at]
                clear = 1.0 - covered
            return colour + [covered]

        def send_mate():
            def one(view):
                store(outgoing, mate, view, everything, partial(view, mate, everything))
                send(view, mate, everything).start()

            each_view(one)

        def keep_own():
            def front_pair(index):
                return 2 + index, index, span_reach

            def back_pair(index):
                return jnp.where(index < planes, flank + index, index - planes + 2), 2 * planes + index, reach

            span = {0: front_pair, 3: back_pair}.get(at)
            each_view(lambda view: store(incoming, at, view, everything, partial(view, at, everything, span)))

        def hand_over(block, part=everything, which=(0, views)):
            def one(view):
                store(outgoing, block, view, part, partial(view, block, part))
                hand(view, block, part).start()

            each_view(one, *which)

        def pass_on(block, part=everything, which=(0, views)):
            def one(view):
                mine = partial(view, block, part)
                hand(view, block, part).wait_recv()
                theirs = load(handed, block, view, part)
                swap = reverse[view] == 1
                merged = over(theirs, mine, swap) if lower else over(mine, theirs, swap)
                store(outgoing, block, view, part, merged)
                send(view, block, part).start()

            each_view(one, *which)

        def images_gone(blocks):
            gone = pl.ds(0, blocks)
            copy_to(outgoing.at[gone], handed.at[gone], images, hand_sem.at[0], (mate, h)).wait_send()

        def begin():
            if at == 3:
                return
            with jax.named_scope("barrier"):
                pl.semaphore_wait(barrier, expected)
            if outer:
                pair_copy().start()
                if lower:
                    pair_rest().start()
            else:

                @pl.when(jnp.logical_not(odd))
                def _():
                    pl.semaphore_signal(go_sem, inc=1, device_id=(mate, h), device_id_type=MESH)

                peer_copy().start()
                (slab_copy if lower else slab_end_copy)().start()
                if not lower:
                    flank_copy().start()
                columns()

        def columns():
            if outer:

                @pl.when(jnp.logical_not(odd))
                def _():
                    with jax.named_scope("w_go"):
                        pl.semaphore_wait(go_sem, 1)

            @pl.when(below)
            def _():
                down_copy(1).start()
                if outer:
                    edge_copy(1).start()
                if at == 1:
                    slab_edge_copy(1).start()

            @pl.when(above)
            def _():
                if not outer:
                    peer_corner(-1, peer_border).start()
                if at == 2:
                    flank_edge_copy(-1).start()
                up_copy(-1).start()

        def blank():
            if outer:
                volume[1 if lower else planes + 2] = jnp.zeros(volume.shape[1:], jnp.float32)

            @pl.when(jnp.logical_not(above))
            def _():
                volume[:, :LEAD] = jnp.zeros((2 * planes + 5, LEAD, cols), jnp.float32)

            @pl.when(jnp.logical_not(below))
            def _():
                volume[:, end : end + border] = jnp.zeros((2 * planes + 5, border, cols), jnp.float32)

        def top_landed():
            @pl.when(above)
            def _():
                with jax.named_scope("w_down"):
                    down_copy(-1).wait_recv()

        def bottom_landed():
            @pl.when(below)
            def _():
                with jax.named_scope("w_up"):
                    up_copy(1).wait_recv()

        def peer_corner_landed():
            @pl.when(below)
            def _():
                with jax.named_scope("w_pcorner"):
                    peer_corner(1, border).wait_recv()

        def pair_corner_landed():
            @pl.when(below)
            def _():
                with jax.named_scope("w_corner"):
                    pair_relay(1).wait_recv()

        def edge_landed():
            @pl.when(above)
            def _():
                with jax.named_scope("w_edge"):
                    edge_copy(-1).wait_recv()

        blank()
        if at == 0:
            shade_box(low, high, LEAD, rows - LEAD)
            begin()
            with jax.named_scope("hand2"):
                hand_over(2)
            columns()
            top_landed()
            bottom_landed()
            shade_box(low, high, rows - LEAD, rows + extra)
            with jax.named_scope("hand3"):
                hand_over(3)
            shade_box(low, high, 0, LEAD)
            with jax.named_scope("mate"):
                send_mate()
            with jax.named_scope("w_slab"):
                slab_copy().wait_recv()

                @pl.when(above)
                def _():
                    slab_edge_copy(-1).wait_recv()

                slab_end_copy().wait_recv()
            shade_box(high, span_high, 0, -(-(share + span_reach) // 8) * 8)
            keep_own()
        elif at == 3:
            begin()
            pl.when(odd)(columns)
            shade_box(low, high, LEAD, rows - LEAD)
            with jax.named_scope("hand0b"):
                hand_over(0, halves[0])
            pair_rest().start()
            pl.when(jnp.logical_not(odd))(columns)
            shade_box(low, high, rows - LEAD, rows, True)

            def early():
                top_landed()
                shade_box(low, high, 0, LEAD)
                with jax.named_scope("hand0a"):
                    hand_over(0, halves[1])

            def late(which):
                with jax.named_scope("hand1"):
                    hand_over(1, everything, which)

            def last():
                for half in halves:
                    hand_over(1, half, (views - 1, views))

            @pl.when(distant)
            def _():
                late(some)
                early()
                late(rest)
                last()

            @pl.when(h == 0)
            def _():
                early()
                late((0, views - 1))
                last()

            @pl.when(odd)
            def _():
                early()
                late((0, views - 1))
                last()

            bottom_landed()
            shade_box(low, high, rows - LEAD, rows)
            shade_box(low, high, rows, rows + extra)
            with jax.named_scope("mate"):
                send_mate()
            with jax.named_scope("w_flank"):
                flank_copy().wait_recv()

                @pl.when(below)
                def _():
                    flank_edge_copy(1).wait_recv()

                flank_end_copy().wait_recv()
            top_row, bottom_row = rows - share, rows + flank_rows
            there = pl.ds(LEAD + top_row, bottom_row - top_row)
            volume[1, there] = volume[flank + planes - 1, there]
            volume[flank + planes, there] = volume[2, there]
            shade_box(flank, flank + planes, top_row, bottom_row)
            shade_box(2, 3, top_row, bottom_row)
            keep_own()
        else:
            shade_box(3, planes + 1, LEAD, rows - LEAD)
            begin()
            far_edge = planes + 1 if lower else 2
            seam = min(2 if lower else planes + 1, edge)


            def top():
                top_landed()
                edge_landed()
                shade_box(low, high, 0, LEAD)

            def relay():
                @pl.when(above)
                def _():
                    pair_relay(-1).start()

            def rest_landed():
                with jax.named_scope("w_rest"):
                    pair_rest().wait_recv()
                if lower:
                    relay()
                    shade_box(seam, seam + 2, LEAD, share + LEAD)
                else:
                    shade_box(seam, seam + 2, rows - share - LEAD, rows - LEAD)

            def bottom():
                bottom_landed()
                pair_corner_landed()
                if lower:
                    peer_corner_landed()
                shade_box(low, high, rows - LEAD, rows + extra)

            with jax.named_scope("w_peer"):
                peer_copy().wait_recv()
            shade_box(far_edge, far_edge + 1, LEAD, rows - LEAD)
            if lower:
                shade_box(3, planes + 2, rows - LEAD, rows, True)
            with jax.named_scope("w_pair"):
                pair_copy().wait_recv()
            if lower:
                shade_box(seam, seam + 2, share + LEAD, rows - LEAD)
                rest_landed()
                with jax.named_scope("pass2"):
                    pass_on(2)
                top()
                bottom()
                with jax.named_scope("pass3"):
                    pass_on(3)
            else:
                relay()
                shade_box(seam, seam + 2, LEAD, rows - share - LEAD)
                with jax.named_scope("pass0b"):
                    pass_on(0, halves[0])
                peer_corner_landed()
                flank_end_copy().start()
                rest_landed()

                def last():
                    for half in halves:
                        pass_on(1, half, (views - 1, views))

                def early():
                    top()
                    with jax.named_scope("pass0a"):
                        pass_on(0, halves[1])

                @pl.when(distant)
                def _():
                    with jax.named_scope("pass1"):
                        pass_on(1, everything, some)
                    early()
                    pass_on(1, everything, rest)
                    last()

                @pl.when(jnp.logical_not(distant))
                def _():
                    early()
                    with jax.named_scope("pass1"):
                        pass_on(1, everything, (0, views - 1))
                        last()

                bottom()
            keep_own()

        def finish(view):
            swap = reverse[view] == 1
            near = load(incoming, at, view, everything)
            if not outer:
                with jax.named_scope("w_mate"):
                    receive(view, mate).wait_recv()
                theirs = load(incoming, mate, view, everything)
                near = over(near, theirs, swap) if at < mate else over(theirs, near, swap)
            with jax.named_scope("w_other"):
                receive(view, other).wait_recv()
            far = load(incoming, other, view, everything)
            total = over(near, far, swap) if lower else over(far, near, swap)
            for c in range(4):
                out[c, view] = total[c]

        for view in range(views):
            finish(view)

        if outer:
            pair_copy().wait_send()
            pair_rest().wait_send()
        else:
            peer_copy().wait_send()
            (slab_copy if lower else slab_end_copy)().wait_send()
            if not lower:
                flank_copy().wait_send()
                flank_end_copy().wait_send()

        @pl.when(below)
        def _():
            down_copy(1).wait_send()
            if outer:
                edge_copy(1).wait_send()
            if at == 1:
                slab_edge_copy(1).wait_send()

        @pl.when(above)
        def _():
            up_copy(-1).wait_send()
            if not outer:
                peer_corner(-1, peer_border).wait_send()
                pair_relay(-1).wait_send()
            if at == 2:
                flank_edge_copy(-1).wait_send()

        images_gone(3 if outer else 2)
    for at in range(groups):

        @pl.when(d == at)
        def _():
            brick(at)


def kernel(
    groups,
    towers,
    density,
    light,
    gain,
    bias,
    shear,
    reverse,
    out,
    volume,
    fields,
    outgoing,
    incoming,
    handed,
    local_sem,
    halo_send,
    halo_recv,
    hand_send,
    hand_recv,
    part_send,
    part_recv,
):
    planes, rows, cols = density.shape
    margin = rows // 2
    views = shear.shape[0]
    share = rows // groups
    total_planes = planes * groups
    extinction = EXTINCTION / total_planes
    d = lax.axis_index("depth")
    h = lax.axis_index("height")
    end = LEAD + rows
    tall = end + margin

    own = pltpu.make_async_copy(
        density, volume.at[pl.ds(1, planes), pl.ds(LEAD, rows)], local_sem
    )
    own.start()

    def near(step_d, step_h):
        ok = None
        for at, step, count in ((d, step_d, groups), (h, step_h, towers)):
            if step:
                test = (at + step >= 0) & (at + step < count)
                ok = test if ok is None else ok & test
        return ok, (d + step_d, h + step_h)

    barrier = pltpu.get_barrier_semaphore()
    beside = [(0, 1), (0, -1), (1, 1), (1, -1), (-1, 1), (-1, -1), (1, 0), (-1, 0)]
    if groups > 4:
        beside += [(step * hop, 0) for hop in range(2, groups) for step in (1, -1)]
    expected = jnp.int32(0)
    for step_d, step_h in beside:
        ok, target = near(step_d, step_h)
        expected = expected + jnp.where(ok, 1, 0)

        @pl.when(ok)
        def _(target=target):
            pl.semaphore_signal(barrier, inc=1, device_id=target, device_id_type=MESH)

    pl.semaphore_wait(barrier, expected)

    whole = pl.ds(0, planes)
    inner = pl.ds(1, planes)
    first, last = pl.ds(0, 1), pl.ds(planes - 1, 1)
    low, high = pl.ds(0, 1), pl.ds(planes + 1, 1)
    routes = [
        ((1, 0), last, (0, rows), low, LEAD),
        ((-1, 0), first, (0, rows), high, LEAD),
        ((0, 1), whole, (rows - LEAD, LEAD), inner, 0),
        ((0, -1), whole, (0, margin), inner, end),
        ((1, -1), last, (0, margin), low, end),
        ((-1, -1), first, (0, margin), high, end),
    ]

    def halo(index, reach):
        step, from_planes, (row, count), to_planes, to_row = routes[index]
        return pltpu.make_async_remote_copy(
            src_ref=density.at[from_planes, pl.ds(row, count)],
            dst_ref=volume.at[to_planes, pl.ds(to_row, count)],
            send_sem=halo_send.at[index],
            recv_sem=halo_recv.at[index],
            device_id=reach,
            device_id_type=MESH,
        )

    for index, route in enumerate(routes):
        ok, target = near(*route[0])

        @pl.when(ok)
        def _(index=index, target=target):
            halo(index, target).start()

    @pl.when(d == 0)
    def _():
        volume[0] = jnp.zeros(volume.shape[1:], jnp.float32)

    @pl.when(d == groups - 1)
    def _():
        volume[planes + 1] = jnp.zeros(volume.shape[1:], jnp.float32)

    @pl.when(h == 0)
    def _():
        volume[1 : planes + 1, :LEAD] = jnp.zeros((planes, LEAD, cols), jnp.float32)

    @pl.when(h == towers - 1)
    def _():
        volume[:, end:tall] = jnp.zeros((planes + 2, margin, cols), jnp.float32)

    own.wait()

    lz, ly, lx = light[0], light[1], light[2]
    half_gain = [0.5 * gain[c] for c in range(3)]
    half_bias = [0.5 * bias[c] for c in range(3)]

    def shade(plane, row, count, keep):
        at = LEAD + row
        centre = volume[plane, at : at + count]
        lane = lax.broadcasted_iota(jnp.int32, (count, cols), 1)
        following = jnp.where(lane == cols - 1, 0.0, pltpu.roll(centre, cols - 1, 1))
        previous = jnp.where(lane == 0, 0.0, pltpu.roll(centre, 1, 1))
        dx = following - previous
        dz = volume[plane + 1, at : at + count] - volume[plane - 1, at : at + count]
        dy = volume[plane, at + 1 : at + 1 + count] - volume[plane, at - 1 : at - 1 + count]
        facing = (lz * dz + ly * dy + lx * dx) * lax.rsqrt(4.0 + dz * dz + dy * dy + dx * dx)
        shading = 0.25 + 1.5 * jnp.maximum(facing, 0.0)
        optical = extinction * (
            jnp.maximum(centre, 0.0) + jnp.log1p(jnp.exp(-jnp.abs(centre)))
        )
        opacity = jnp.tanh(0.5 * optical) * (1.0 + jnp.exp(-optical))
        if keep is not None:
            opacity = opacity * keep
        lit = 0.5 * (opacity * shading)
        to = pl.ds(row, count)
        for c in range(3):
            fields[c, plane - 1, to] = lit + lit * jnp.tanh(half_gain[c] * centre + half_bias[c])
        fields[3, plane - 1, to] = opacity

    inside = jnp.where(h < towers - 1, 1.0, 0.0)

    def early(plane, _):
        for row, count in spans(LEAD, rows - LEAD, 16):
            shade(plane, row, count, None)
        return 0

    lax.fori_loop(2, planes, early, 0)

    def landed(index):
        step_d, step_h = routes[index][0]
        ok, source = near(-step_d, -step_h)

        @pl.when(ok)
        def _():
            halo(index, source).wait_recv()

    def shade_low():
        for index in (0, 1, 2):
            landed(index)
        for plane in range(1, planes + 1):
            shade(plane, 0, LEAD, None)
        for row, count in spans(LEAD, rows - LEAD, 16):
            for plane in (1, planes):
                shade(plane, row, count, None)

    def shade_high():
        for index in (3, 4, 5):
            landed(index)

        def bottom(at, _):
            for plane in (2 * at + 1, 2 * at + 2):
                shade(plane, rows - LEAD, LEAD, None)
                for row, count in spans(rows, rows + margin, 16):
                    shade(plane, row, count, inside)
            return 0

        lax.fori_loop(0, planes // 2, bottom, 0)

    first_plane = d * planes

    def partial(view, block):
        step = shear[view]
        backward = reverse[view]
        colour = [jnp.zeros((share, cols), jnp.float32) for _ in range(3)]
        clear = jnp.ones((share, cols), jnp.float32)
        covered = jnp.zeros((share, cols), jnp.float32)
        for i in range(planes):
            plane = i + backward * (planes - 1 - 2 * i)
            offset = lax.div((first_plane + plane) * step, jnp.int32(total_planes))
            at = pl.ds(offset + block * share, share)
            for c in range(3):
                colour[c] = colour[c] + clear * fields[c, plane, at]
            covered = covered + clear * fields[3, plane, at]
            clear = 1.0 - covered
        return colour + [covered]

    odd = lax.rem(d, 2)
    out_step = 2 * odd - 1
    mate = d - out_step
    pair = lax.div(d, 2)
    beyond = odd * (groups - 1 - d) + (1 - odd) * d
    handing = odd * (d - 1) + (1 - odd) * (groups - 2 - d)

    def over(first, second, swap):
        front = [jnp.where(swap, b, a) for a, b in zip(first, second)]
        behind = [jnp.where(swap, a, b) for a, b in zip(first, second)]
        clear = 1.0 - front[3]
        return [f + clear * b for f, b in zip(front, behind)]

    def load(ref, block, view):
        return [ref[block, view, c] for c in range(4)]

    def store(ref, block, view, image):
        for c in range(4):
            ref[block, view, c] = image[c]

    def hand(view, block):
        return pltpu.make_async_remote_copy(
            src_ref=outgoing.at[block, view],
            dst_ref=handed.at[block, view],
            send_sem=hand_send.at[view, block],
            recv_sem=hand_recv.at[view, block],
            device_id=(mate, h),
            device_id_type=MESH,
        )

    def send(view, block):
        return pltpu.make_async_remote_copy(
            src_ref=outgoing.at[block, view],
            dst_ref=incoming.at[d, view],
            send_sem=part_send.at[view, block],
            recv_sem=part_recv.at[view, d],
            device_id=(block, h),
            device_id_type=MESH,
        )

    def receive(view, source):
        return pltpu.make_async_remote_copy(
            src_ref=outgoing.at[source, view],
            dst_ref=incoming.at[source, view],
            send_sem=part_send.at[view, source],
            recv_sem=part_recv.at[view, source],
            device_id=(source, h),
            device_id_type=MESH,
        )

    def each(count, body):
        def step(k, _):
            body(k)
            return 0

        lax.fori_loop(0, count, step, 0)

    def hand_over(view, k):
        block = odd * k + (1 - odd) * (groups - 1 - k)
        store(outgoing, block, view, partial(view, block))
        hand(view, block).start()

    def prepare(view, k):
        block = d + out_step * (1 + k)
        store(outgoing, block, view, partial(view, block))

    def to_mate(view):
        store(outgoing, mate, view, partial(view, mate))
        send(view, mate).start()

    def pass_on(view, k):
        block = odd * (groups - 1 - k) + (1 - odd) * k
        hand(view, block).wait_recv()
        own_part, other = load(outgoing, block, view), load(handed, block, view)
        swap = reverse[view] != odd
        store(outgoing, block, view, over(own_part, other, swap))
        send(view, block).start()

    reach = lax.div((first_plane + planes - 1) * margin, jnp.int32(total_planes))

    def hand_round(early):
        def one(k):
            block = odd * k + (1 - odd) * (groups - 1 - k)
            ready = ((block + 1) * share + reach <= rows - LEAD) & (odd == 1)

            @pl.when(ready if early else jnp.logical_not(ready))
            def _():
                each(views, lambda view: hand_over(view, k))

        each(handing, one)

    shade_low()
    hand_round(True)
    shade_high()
    hand_round(False)
    each(views, to_mate)
    each(views, lambda view: each(beyond, lambda k: prepare(view, k)))
    each(views, lambda view: store(incoming, d, view, partial(view, d)))
    each(beyond, lambda k: each(views, lambda view: pass_on(view, k)))

    def finish(view):
        swap = reverse[view] == 1
        receive(view, mate).wait_recv()
        both = over(load(incoming, d, view), load(incoming, mate, view), reverse[view] != odd)
        store(incoming, 2 * pair + 1, view, both)
        sources = [jnp.where(j > pair, 2 * j, 2 * j + 1) for j in range(groups // 2)]
        for j, source in enumerate(sources):

            @pl.when(j != pair)
            def _():
                receive(view, source).wait_recv()

        total = load(incoming, sources[0], view)
        for source in sources[1:]:
            total = over(total, load(incoming, source, view), swap)
        for c in range(4):
            out[c, view] = total[c]

    for view in range(views):
        finish(view)

    for index, route in enumerate(routes):
        ok, target = near(*route[0])

        @pl.when(ok)
        def _(index=index, target=target):
            halo(index, target).wait_send()

    def sent(view):
        send(view, mate).wait_send()
        each(handing, lambda k: hand(view, d - out_step * (2 + k)).wait_send())
        each(beyond, lambda k: send(view, d + out_step * (1 + k)).wait_send())

    each(views, sent)


def general(groups, towers, density, light, gain, bias, shear, reverse):
    planes, rows, cols = density.shape
    views = shear.shape[0]
    share = rows // groups
    tall = LEAD + rows + rows // 2
    scalars = pl.BlockSpec(memory_space=pltpu.SMEM)
    return pl.pallas_call(
        functools.partial(kernel, groups, towers),
        name="render",
        out_shape=pltpu.VMEM((4, views, share, cols), jnp.float32),
        in_specs=[pl.BlockSpec(memory_space=pltpu.HBM)] + [scalars] * 5,
        out_specs=pl.BlockSpec(memory_space=pltpu.VMEM),
        scratch_shapes=[
            pltpu.VMEM((planes + 2, tall + LEAD, cols), jnp.float32),
            pltpu.VMEM((4, planes, rows + rows // 2, cols), jnp.float32),
            pltpu.VMEM((groups, views, 4, share, cols), jnp.float32),
            pltpu.VMEM((groups, views, 4, share, cols), jnp.float32),
            pltpu.VMEM((groups, views, 4, share, cols), jnp.float32),
            pltpu.SemaphoreType.DMA,
            pltpu.SemaphoreType.DMA((6,)),
            pltpu.SemaphoreType.DMA((6,)),
            pltpu.SemaphoreType.DMA((views, groups)),
            pltpu.SemaphoreType.DMA((views, groups)),
            pltpu.SemaphoreType.DMA((views, groups)),
            pltpu.SemaphoreType.DMA((views, groups)),
        ],
        compiler_params=pltpu.CompilerParams(collective_id=0, has_side_effects=True, vmem_limit_bytes=60 * 1024 * 1024),
    )(density, light, gain, bias, shear, reverse)


def line(towers, density, light, gain, bias, shear, reverse):
    planes, rows, cols = density.shape
    views = shear.shape[0]
    groups = 4
    share = rows // groups
    whole = pl.BlockSpec(memory_space=pltpu.HBM)
    images = pltpu.VMEM((groups, views, 4, share, cols), jnp.float32)
    return pl.pallas_call(
        functools.partial(line_kernel, towers),
        name="render",
        out_shape=pltpu.VMEM((4, views, share, cols), jnp.float32),
        in_specs=[whole] * 6,
        out_specs=pl.BlockSpec(memory_space=pltpu.VMEM),
        scratch_shapes=[pltpu.SMEM(scalar.shape, scalar.dtype) for scalar in (light, gain, bias, shear, reverse)]
        + [
            pltpu.VMEM((2 * planes + 5, LEAD + rows + rows // 2 + LEAD, cols), jnp.float32),
            pltpu.VMEM((4, 2 * planes + 4, rows + rows // 2, cols), jnp.float32),
            images,
            images,
            images,
            pltpu.SemaphoreType.DMA((10,)),
            pltpu.SemaphoreType.DMA((8,)),
            pltpu.SemaphoreType.DMA((3 * views + 1,)),
            pltpu.SemaphoreType.DMA((2 * views,)),
            pltpu.SemaphoreType.REGULAR,
        ],
        compiler_params=pltpu.CompilerParams(collective_id=0, has_side_effects=True, vmem_limit_bytes=60 * 1024 * 1024),
    )(density, light, gain, bias, shear, reverse)


def on_device(groups, towers, density, light, gain, bias, shear, reverse):
    planes, rows, _ = density.shape
    if groups == 4 and planes >= 8 and rows % 64 == 0:
        return line(towers, density, light, gain, bias, shear, reverse)
    return general(groups, towers, density, light, gain, bias, shear, reverse)


def solution(mesh):
    groups, towers = mesh.shape["depth"], mesh.shape["height"]
    placed = (P("depth", "height", None), P(), P(), P(), P(), P())
    return jax.shard_map(
        functools.partial(on_device, groups, towers),
        mesh=mesh,
        in_specs=placed,
        out_specs=P(None, None, ("height", "depth"), None),
        check_vma=False,
    )
```

```python
import functools

import jax
import jax.numpy as jnp
from jax import lax
from jax.experimental import pallas as pl
from jax.experimental.pallas import tpu as pltpu
from jax.sharding import PartitionSpec as P

EXTINCTION = 2.5
LEAD = 8
TOGETHER = 6
MESH = pl.DeviceIdType.MESH


def spans(low, high, size):
    return [(at, min(size, high - at)) for at in range(low, high, size)]


def line_kernel(
    towers,
    density,
    light_in,
    gain_in,
    bias_in,
    shear_in,
    reverse_in,
    out,
    light,
    gain,
    bias,
    shear,
    reverse,
    volume,
    fields,
    outgoing,
    incoming,
    handed,
    sent_sem,
    halo_sem,
    hand_sem,
    part_sem,
    go_sem,
):
    planes, rows, cols = density.shape
    margin = rows // 2
    views = shear.shape[0]
    groups = 4
    share = rows // groups
    total_planes = planes * groups
    extinction = EXTINCTION / total_planes
    d = lax.axis_index("depth")
    h = lax.axis_index("height")
    above, below = (h - 1 >= 0) & (h - 1 < towers), (h + 1 >= 0) & (h + 1 < towers)
    end = LEAD + rows
    own_planes = pl.ds(2, planes)
    images, plane_sent, edge_sent, down_sent, up_sent, corner_sent, rest_sent, relay_sent, flank_edge_sent, flank_end_sent = range(10)
    slab_sent, slab_edge_sent, flank_sent = edge_sent, rest_sent, rest_sent
    pair_in, peer_in, edge_in, down_in, up_in, pair_corner_in, peer_corner_in, rest_in = range(8)
    slab_in, slab_edge_in, slab_end_in = pair_in, edge_in, peer_in
    flank_in, flank_edge_in, flank_end_in = pair_in, edge_in, peer_in

    early_planes = jnp.where(d < groups // 2, planes - 2, 0)
    later_planes = jnp.where(d < groups // 2, 0, 2)
    own, own_rest = (
        pltpu.make_async_copy(
            density.at[pl.ds(start, count)],
            volume.at[pl.ds(2 + start, count), pl.ds(LEAD, rows)],
            sent_sem.at[index],
        )
        for start, count, index in ((early_planes, 2, images), (later_planes, planes - 2, relay_sent))
    )
    own.start()
    own_rest.start()

    scalars = [
        pltpu.make_async_copy(source, target, sent_sem.at[(edge_sent, down_sent, up_sent, corner_sent, rest_sent)[index]])
        for index, (source, target) in enumerate(
            zip((light_in, gain_in, bias_in, shear_in, reverse_in), (light, gain, bias, shear, reverse))
        )
    ]
    for scalar in scalars:
        scalar.start()

    def valid(step_d, step_h):
        ok = None
        for at, step, count in ((d, step_d, groups), (h, step_h, towers)):
            if step:
                test = (at + step >= 0) & (at + step < count)
                ok = test if ok is None else ok & test
        return ok

    barrier = pltpu.get_barrier_semaphore()
    expected = jnp.int32(0)
    greets = {at: [] for at in range(groups)}
    awaits = {at: [] for at in range(groups)}

    def greet(at, step_d, step_h, parity=None):
        greets[at].append((step_d, step_h, parity))
        awaits[at + step_d].append((-step_d, -step_h, parity if parity is None else (parity + step_h) % 2))

    for at in range(groups):
        mate = (at ^ 1) - at
        outer = at in (0, 3)
        for step_h in (1, -1):
            greet(at, mate if outer else 0, step_h)
            greet(at, 0 if outer else mate, step_h, 0)
        greet(at, mate, 0)
        if not outer:
            greet(at, -mate, 0)
            greet(at, -mate, 1)
    greet(0, 2, 0)

    def meets(at, step_d, step_h, parity):
        ok = (d == at) & valid(step_d, step_h)
        return ok if parity is None else ok & (lax.rem(h, 2) == parity)

    for at in range(groups):

        for step_d, step_h, parity in greets[at]:

            @pl.when(meets(at, step_d, step_h, parity))
            def _(target=(d + step_d, h + step_h)):
                pl.semaphore_signal(barrier, inc=1, device_id=target, device_id_type=MESH)

        for step in awaits[at]:
            expected = expected + jnp.where(meets(at, *step), 1, 0)

    own.wait()

    @pl.when(d == groups - 1)
    def _():
        with jax.named_scope("barrier"):
            pl.semaphore_wait(barrier, expected)
        first_pair = volume.at[pl.ds(2, 2), pl.ds(LEAD, rows - share)]
        first_target = volume.at[pl.ds(planes + 2, 2), pl.ds(LEAD, rows - share)]
        pltpu.make_async_remote_copy(
            src_ref=first_pair,
            dst_ref=first_target,
            send_sem=sent_sem.at[plane_sent],
            recv_sem=halo_sem.at[pair_in],
            device_id=(d - 1, h),
            device_id_type=MESH,
        ).start()

    for scalar in scalars:
        scalar.wait()
    own_rest.wait()

    lz, ly, lx = light[0], light[1], light[2]
    half_gain = [0.5 * gain[c] for c in range(3)]
    half_bias = [0.5 * bias[c] for c in range(3)]
    inside = jnp.where(below, 1.0, 0.0)

    def shade(plane, row, count, keep, loose=False):
        at = LEAD + row
        centre = volume[plane, at : at + count]
        lane = lax.broadcasted_iota(jnp.int32, (count, cols), 1)
        following = jnp.where(lane == cols - 1, 0.0, pltpu.roll(centre, cols - 1, 1))
        previous = jnp.where(lane == 0, 0.0, pltpu.roll(centre, 1, 1))
        dx = following - previous
        dz = volume[plane + 1, at : at + count] - volume[plane - 1, at : at + count]
        below_it = pltpu.roll(centre, count - 1, 0) if loose else volume[plane, at + 1 : at + 1 + count]
        dy = below_it - volume[plane, at - 1 : at - 1 + count]
        facing = (lz * dz + ly * dy + lx * dx) * lax.rsqrt(4.0 + dz * dz + dy * dy + dx * dx)
        shading = 0.25 + 1.5 * jnp.maximum(facing, 0.0)
        optical = extinction * (
            jnp.maximum(centre, 0.0) + jnp.log1p(jnp.exp(-jnp.abs(centre)))
        )
        opacity = jnp.tanh(0.5 * optical) * (1.0 + jnp.exp(-optical))
        if keep is not None:
            opacity = opacity * keep
        lit = 0.5 * (opacity * shading)
        to = pl.ds(row, count)
        for c in range(3):
            fields[c, plane, to] = lit + lit * jnp.tanh(half_gain[c] * centre + half_bias[c])
        fields[3, plane, to] = opacity

    def shade_box(low, high, top, bottom, loose=False):
        tiles = (bottom - top) // 8
        together = max(1, min(high - low, -(-TOGETHER // tiles)))
        looped = (high - low) // together if high - low > together else 0

        def some(plane, count):
            for step in range(count):
                for row, size in spans(top, min(bottom, rows), 16):
                    shade(plane + step, row, size, None, loose)
                for row, size in spans(max(top, rows), bottom, 16):
                    shade(plane + step, row, size, inside)

        if looped:

            def step(index, _):
                some(low + index * together, together)
                return 0

            lax.fori_loop(0, looped, step, 0)
        done = low + looped * together
        if done < high:
            some(done, high - done)

    def copy_to(source, target, sent, received, device):
        return pltpu.make_async_remote_copy(
            src_ref=source,
            dst_ref=target,
            send_sem=sent_sem.at[sent],
            recv_sem=received,
            device_id=device,
            device_id_type=MESH,
        )

    def over(first, second, swap):
        front = [jnp.where(swap, b, a) for a, b in zip(first, second)]
        behind = [jnp.where(swap, a, b) for a, b in zip(first, second)]
        clear = 1.0 - front[3]
        return [f + clear * b for f, b in zip(front, behind)]

    everything = (0, share)
    odd = lax.rem(h, 2) == 1
    distant = (lax.rem(h, 2) == 0) & (h > 0)
    ahead = jnp.where(h == towers // 2, views // 2, 1)
    some, rest = (0, ahead), (ahead, views - 1)

    def load(ref, block, view, part):
        return [ref[block, view, c, pl.ds(*part)] for c in range(4)]

    def store(ref, block, view, part, image):
        for c in range(4):
            ref[block, view, c, pl.ds(*part)] = image[c]

    def each_view(body, start=0, stop=views):
        def step(view, _):
            body(view)
            return 0

        lax.fori_loop(start, stop, step, 0)

    def extent(at):
        low = {0: 2, 1: 1, 2: 2, 3: 3}[at]
        high = {0: planes + 1, 1: planes + 2, 2: planes + 3, 3: planes + 2}[at]
        reach = (at * planes + high - 3) * margin // total_planes
        return low, high, reach, min(margin, -(-(reach + 1) // 8) * 8)

    def brick(at):
        outer = at in (0, groups - 1)
        lower = at < groups // 2
        mate = at ^ 1
        first = at * planes - 2
        low, high, reach, border = extent(at)
        extra = -(-reach // 8) * 8
        mate_pair = pl.ds(0, 2) if lower else pl.ds(planes + 2, 2)
        edge = {0: planes + 1, 1: 1, 2: planes + 2, 3: 2}[at]
        mate_edge = {0: 1, 3: planes + 2}.get(at, edge)
        others = [2, 3] if lower else [0, 1]
        other = {0: 2, 1: 2, 2: 1, 3: 1}[at]
        peer = {1: 2, 2: 1}.get(at)
        halves = [(share // 2, share // 2), (0, share // 2)]
        parts = {0: halves, 1: [everything], 2: [everything], 3: [everything]}
        hand_at = {
            (block, part): index
            for index, (block, part) in enumerate((block, part) for block in others for part in parts[block])
        }

        def plane_copy(source, target, take, put, sent, received, device):
            return copy_to(
                volume.at[source, pl.ds(*take)],
                volume.at[target, pl.ds(*put)],
                sent,
                halo_sem.at[received],
                device,
            )

        own_pair = pl.ds(planes, 2) if lower else pl.ds(2, 2)
        own_peer = pl.ds(planes + 1, 1) if lower else pl.ds(2, 1)
        peer_target = pl.ds(1, 1) if lower else pl.ds(planes + 2, 1)
        peer_border = extent(peer)[3] if peer else None
        whole = (LEAD, rows)

        cut = rows - share
        soon, after = ((LEAD + share, cut), (LEAD, share)) if lower else ((LEAD, cut), (LEAD + cut, share))

        def pair_copy():
            return plane_copy(own_pair, mate_pair, soon, soon, plane_sent, pair_in, (mate, h))

        def pair_rest():
            return plane_copy(own_pair, mate_pair, after, after, rest_sent, rest_in, (mate, h))

        def peer_copy():
            return plane_copy(own_peer, peer_target, whole, whole, plane_sent, peer_in, (peer, h))

        def pair_relay(step):
            take, put = (LEAD, border), (end, border)
            return plane_copy(mate_pair, mate_pair, take, put, relay_sent, pair_corner_in, (d, h + step))

        def peer_corner(step, count):
            take, put = (LEAD, count), (end, count)
            return plane_copy(own_peer, peer_target, take, put, corner_sent, peer_corner_in, (d + peer - at, h + step))

        def edge_copy(step):
            take, put = (rows, LEAD), (0, LEAD)
            return plane_copy(edge, mate_edge, take, put, edge_sent, edge_in, (d + mate - at, h + step))

        span_high = 2 * planes + 2
        span_reach = extent(1)[2]
        span_rows = share + extent(1)[3]
        slab = pl.ds(planes + 2, planes)
        slab_end = pl.ds(2 * planes + 2, 1)

        def slab_copy():
            take = (LEAD, span_rows)
            return plane_copy(own_planes, slab, take, take, slab_sent, slab_in, (0 if at else 1, h))

        def slab_edge_copy(step):
            take, put = (rows, LEAD), (0, LEAD)
            return plane_copy(own_planes, slab, take, put, slab_edge_sent, slab_edge_in, (d + (-1 if at else 1), h + step))

        def slab_end_copy():
            take = (LEAD, span_rows)
            return plane_copy(pl.ds(2, 1), slab_end, take, take, slab_sent, slab_end_in, (0 if at else 2, h))

        flank = planes + 4
        flank_top = rows - share - LEAD
        flank_reach = (3 * planes - 1) * margin // total_planes
        flank_rows = min(extent(2)[3], -(-(flank_reach + 1) // 8) * 8)
        flank_planes = pl.ds(flank, planes)

        def flank_copy():
            take = (LEAD + flank_top, share + LEAD)
            return plane_copy(own_planes, flank_planes, take, take, flank_sent, flank_in, (3 if at == 2 else 2, h))

        def flank_edge_copy(step):
            take, put = (LEAD, flank_rows), (end, flank_rows)
            return plane_copy(own_planes, flank_planes, take, put, flank_edge_sent, flank_edge_in, (d + (1 if at == 2 else -1), h + step))

        def flank_end_copy():
            take = (LEAD + flank_top, share + LEAD + flank_rows)
            return plane_copy(pl.ds(1, 1), pl.ds(flank - 1, 1), take, take, flank_end_sent, flank_end_in, (3 if at == 2 else 2, h))

        def down_copy(step):
            return copy_to(
                volume.at[own_planes, pl.ds(rows, LEAD)],
                volume.at[own_planes, pl.ds(0, LEAD)],
                down_sent,
                halo_sem.at[down_in],
                (d, h + step),
            )

        def up_copy(step):
            return copy_to(
                volume.at[own_planes, pl.ds(LEAD, border)],
                volume.at[own_planes, pl.ds(end, border)],
                up_sent,
                halo_sem.at[up_in],
                (d, h + step),
            )

        def hand(view, block, part):
            split = block == 1 and part in halves
            index = 3 * views - 1 + halves.index(part) if split else hand_at[block, part] * views + view
            return copy_to(
                outgoing.at[block, view, :, pl.ds(*part)],
                handed.at[block, view, :, pl.ds(*part)],
                images,
                hand_sem.at[index],
                (mate, h),
            )

        def send(view, block, part):
            slot = 0 if block == mate else 1 + view
            return copy_to(
                outgoing.at[block, view, :, pl.ds(*part)],
                incoming.at[at, view, :, pl.ds(*part)],
                images,
                part_sem.at[slot],
                (block, h),
            )

        def receive(view):
            return copy_to(
                outgoing.at[at, view],
                incoming.at[other, view],
                images,
                part_sem.at[1 + view],
                (other, h),
            )

        def receive_mate():
            return copy_to(outgoing.at[at], incoming.at[mate], images, part_sem.at[0], (mate, h))

        def partial(view, block, part, span=None):
            step = shear[view]
            backward = reverse[view]
            count = high - low if span is None else 2 * planes
            size = part[1]
            colour = [jnp.zeros((size, cols), jnp.float32) for _ in range(3)]
            clear = jnp.ones((size, cols), jnp.float32)
            covered = jnp.zeros((size, cols), jnp.float32)
            for i in range(count):
                index = jnp.where(backward == 1, count - 1 - i, i)
                if span is None:
                    plane, depth, limit = low + index, first + low + index, reach
                else:
                    plane, depth, limit = span(index)
                offset = lax.div(depth * step, jnp.int32(total_planes))
                offset = jnp.minimum(jnp.maximum(offset, 0), limit)
                rows_at = pl.ds(offset + block * share + part[0], size)
                for c in range(3):
                    colour[c] = colour[c] + clear * fields[c, plane, rows_at]
                covered = covered + clear * fields[3, plane, rows_at]
                clear = 1.0 - covered
            return colour + [covered]

        def send_mate():
            def one(view):
                store(outgoing, mate, view, everything, partial(view, mate, everything))
                send(view, mate, everything).start()

            each_view(one)

        def keep_own():
            def front_pair(index):
                return 2 + index, index, span_reach

            def back_pair(index):
                return jnp.where(index < planes, flank + index, index - planes + 2), 2 * planes + index, reach

            span = {0: front_pair, 3: back_pair}.get(at)
            each_view(lambda view: store(incoming, at, view, everything, partial(view, at, everything, span)))

        def hand_over(block, part=everything, which=(0, views)):
            def one(view):
                store(outgoing, block, view, part, partial(view, block, part))
                hand(view, block, part).start()

            each_view(one, *which)

        def pass_on(block, part=everything, which=(0, views)):
            def one(view):
                mine = partial(view, block, part)
                hand(view, block, part).wait_recv()
                theirs = load(handed, block, view, part)
                swap = reverse[view] == 1
                merged = over(theirs, mine, swap) if lower else over(mine, theirs, swap)
                store(outgoing, block, view, part, merged)
                send(view, block, part).start()

            each_view(one, *which)

        def images_gone(blocks):
            gone = pl.ds(0, blocks)
            copy_to(outgoing.at[gone], handed.at[gone], images, hand_sem.at[0], (mate, h)).wait_send()

        def begin():
            if at == 3:
                return
            with jax.named_scope("barrier"):
                pl.semaphore_wait(barrier, expected)
            if outer:
                pair_copy().start()
                if lower:
                    pair_rest().start()
            else:

                @pl.when(jnp.logical_not(odd))
                def _():
                    pl.semaphore_signal(go_sem, inc=1, device_id=(mate, h), device_id_type=MESH)

                peer_copy().start()
                (slab_copy if lower else slab_end_copy)().start()
                if not lower:
                    flank_copy().start()
                columns()

        def columns():
            if outer:

                @pl.when(jnp.logical_not(odd))
                def _():
                    with jax.named_scope("w_go"):
                        pl.semaphore_wait(go_sem, 1)

            @pl.when(below)
            def _():
                down_copy(1).start()
                if outer:
                    edge_copy(1).start()
                if at == 1:
                    slab_edge_copy(1).start()

            @pl.when(above)
            def _():
                if not outer:
                    peer_corner(-1, peer_border).start()
                if at == 2:
                    flank_edge_copy(-1).start()
                up_copy(-1).start()

        def blank():
            if outer:
                volume[1 if lower else planes + 2] = jnp.zeros(volume.shape[1:], jnp.float32)

            @pl.when(jnp.logical_not(above))
            def _():
                volume[:, :LEAD] = jnp.zeros((2 * planes + 5, LEAD, cols), jnp.float32)

            @pl.when(jnp.logical_not(below))
            def _():
                volume[:, end : end + border] = jnp.zeros((2 * planes + 5, border, cols), jnp.float32)

        def top_landed():
            @pl.when(above)
            def _():
                with jax.named_scope("w_down"):
                    down_copy(-1).wait_recv()

        def bottom_landed():
            @pl.when(below)
            def _():
                with jax.named_scope("w_up"):
                    up_copy(1).wait_recv()

        def peer_corner_landed():
            @pl.when(below)
            def _():
                with jax.named_scope("w_pcorner"):
                    peer_corner(1, border).wait_recv()

        def pair_corner_landed():
            @pl.when(below)
            def _():
                with jax.named_scope("w_corner"):
                    pair_relay(1).wait_recv()

        def edge_landed():
            @pl.when(above)
            def _():
                with jax.named_scope("w_edge"):
                    edge_copy(-1).wait_recv()

        blank()
        if at == 0:
            shade_box(low, high, LEAD, rows - LEAD)
            begin()
            with jax.named_scope("hand2"):
                hand_over(2)
            columns()
            top_landed()
            bottom_landed()
            shade_box(low, high, rows - LEAD, rows + extra)
            with jax.named_scope("hand3"):
                hand_over(3)
            shade_box(low, high, 0, LEAD)
            with jax.named_scope("mate"):
                send_mate()
            with jax.named_scope("w_slab"):
                slab_copy().wait_recv()

                @pl.when(above)
                def _():
                    slab_edge_copy(-1).wait_recv()

                slab_end_copy().wait_recv()
            shade_box(high, span_high, 0, -(-(share + span_reach) // 8) * 8)
            keep_own()
        elif at == 3:
            begin()
            pl.when(odd)(columns)
            shade_box(low, high, LEAD, rows - LEAD)
            with jax.named_scope("hand0b"):
                hand_over(0, halves[0])
            pair_rest().start()
            pl.when(jnp.logical_not(odd))(columns)
            shade_box(low, high, rows - LEAD, rows, True)

            def early():
                top_landed()
                shade_box(low, high, 0, LEAD)
                with jax.named_scope("hand0a"):
                    hand_over(0, halves[1])

            def late(which):
                with jax.named_scope("hand1"):
                    hand_over(1, everything, which)

            def last():
                for half in halves:
                    hand_over(1, half, (views - 1, views))

            @pl.when(distant)
            def _():
                late(some)
                early()
                late(rest)
                last()

            @pl.when(h == 0)
            def _():
                early()
                late((0, views - 1))
                last()

            @pl.when(odd)
            def _():
                early()
                late((0, views - 1))
                last()

            bottom_landed()
            shade_box(low, high, rows - LEAD, rows)
            shade_box(low, high, rows, rows + extra)
            with jax.named_scope("mate"):
                send_mate()
            with jax.named_scope("w_flank"):
                flank_copy().wait_recv()

                @pl.when(below)
                def _():
                    flank_edge_copy(1).wait_recv()

                flank_end_copy().wait_recv()
            top_row, bottom_row = rows - share, rows + flank_rows
            there = pl.ds(LEAD + top_row, bottom_row - top_row)
            volume[1, there] = volume[flank + planes - 1, there]
            volume[flank + planes, there] = volume[2, there]
            shade_box(flank, flank + planes, top_row, bottom_row)
            shade_box(2, 3, top_row, bottom_row)
            keep_own()
        else:
            shade_box(3, planes + 1, LEAD, rows - LEAD)
            begin()
            far_edge = planes + 1 if lower else 2
            seam = min(2 if lower else planes + 1, edge)


            def top():
                top_landed()
                edge_landed()
                shade_box(low, high, 0, LEAD)

            def relay():
                @pl.when(above)
                def _():
                    pair_relay(-1).start()

            def rest_landed():
                with jax.named_scope("w_rest"):
                    pair_rest().wait_recv()
                if lower:
                    relay()
                    shade_box(seam, seam + 2, LEAD, share + LEAD)
                else:
                    shade_box(seam, seam + 2, rows - share - LEAD, rows - LEAD)

            def bottom():
                bottom_landed()
                pair_corner_landed()
                if lower:
                    peer_corner_landed()
                shade_box(low, high, rows - LEAD, rows + extra)

            with jax.named_scope("w_peer"):
                peer_copy().wait_recv()
            shade_box(far_edge, far_edge + 1, LEAD, rows - LEAD)
            if lower:
                shade_box(3, planes + 2, rows - LEAD, rows, True)
            with jax.named_scope("w_pair"):
                pair_copy().wait_recv()
            if lower:
                shade_box(seam, seam + 2, share + LEAD, rows - LEAD)
                rest_landed()
                with jax.named_scope("pass2"):
                    pass_on(2)
                top()
                bottom()
                with jax.named_scope("pass3"):
                    pass_on(3)
            else:
                relay()
                shade_box(seam, seam + 2, LEAD, rows - share - LEAD)
                with jax.named_scope("pass0b"):
                    pass_on(0, halves[0])
                peer_corner_landed()
                flank_end_copy().start()
                rest_landed()

                def last():
                    for half in halves:
                        pass_on(1, half, (views - 1, views))

                def early():
                    top()
                    with jax.named_scope("pass0a"):
                        pass_on(0, halves[1])

                @pl.when(distant)
                def _():
                    with jax.named_scope("pass1"):
                        pass_on(1, everything, some)
                    early()
                    pass_on(1, everything, rest)
                    last()

                @pl.when(jnp.logical_not(distant))
                def _():
                    early()
                    with jax.named_scope("pass1"):
                        pass_on(1, everything, (0, views - 1))
                        last()

                bottom()
            keep_own()

        def finish(view):
            swap = reverse[view] == 1
            near = load(incoming, at, view, everything)
            if not outer:
                theirs = load(incoming, mate, view, everything)
                near = over(near, theirs, swap) if at < mate else over(theirs, near, swap)
            with jax.named_scope("w_other"):
                receive(view).wait_recv()
            far = load(incoming, other, view, everything)
            total = over(near, far, swap) if lower else over(far, near, swap)
            for c in range(4):
                out[c, view] = total[c]

        if not outer:
            with jax.named_scope("w_mate"):
                receive_mate().wait_recv()

        for view in range(views):
            finish(view)

        if outer:
            pair_copy().wait_send()
            pair_rest().wait_send()
        else:
            peer_copy().wait_send()
            (slab_copy if lower else slab_end_copy)().wait_send()
            if not lower:
                flank_copy().wait_send()
                flank_end_copy().wait_send()

        @pl.when(below)
        def _():
            down_copy(1).wait_send()
            if outer:
                edge_copy(1).wait_send()
            if at == 1:
                slab_edge_copy(1).wait_send()

        @pl.when(above)
        def _():
            up_copy(-1).wait_send()
            if not outer:
                peer_corner(-1, peer_border).wait_send()
                pair_relay(-1).wait_send()
            if at == 2:
                flank_edge_copy(-1).wait_send()

        images_gone(3 if outer else 2)
    for at in range(groups):

        @pl.when(d == at)
        def _():
            brick(at)


def kernel(
    groups,
    towers,
    density,
    light,
    gain,
    bias,
    shear,
    reverse,
    out,
    volume,
    fields,
    outgoing,
    incoming,
    handed,
    local_sem,
    halo_send,
    halo_recv,
    hand_send,
    hand_recv,
    part_send,
    part_recv,
):
    planes, rows, cols = density.shape
    margin = rows // 2
    views = shear.shape[0]
    share = rows // groups
    total_planes = planes * groups
    extinction = EXTINCTION / total_planes
    d = lax.axis_index("depth")
    h = lax.axis_index("height")
    end = LEAD + rows
    tall = end + margin

    own = pltpu.make_async_copy(
        density, volume.at[pl.ds(1, planes), pl.ds(LEAD, rows)], local_sem
    )
    own.start()

    def near(step_d, step_h):
        ok = None
        for at, step, count in ((d, step_d, groups), (h, step_h, towers)):
            if step:
                test = (at + step >= 0) & (at + step < count)
                ok = test if ok is None else ok & test
        return ok, (d + step_d, h + step_h)

    barrier = pltpu.get_barrier_semaphore()
    beside = [(0, 1), (0, -1), (1, 1), (1, -1), (-1, 1), (-1, -1), (1, 0), (-1, 0)]
    if groups > 4:
        beside += [(step * hop, 0) for hop in range(2, groups) for step in (1, -1)]
    expected = jnp.int32(0)
    for step_d, step_h in beside:
        ok, target = near(step_d, step_h)
        expected = expected + jnp.where(ok, 1, 0)

        @pl.when(ok)
        def _(target=target):
            pl.semaphore_signal(barrier, inc=1, device_id=target, device_id_type=MESH)

    pl.semaphore_wait(barrier, expected)

    whole = pl.ds(0, planes)
    inner = pl.ds(1, planes)
    first, last = pl.ds(0, 1), pl.ds(planes - 1, 1)
    low, high = pl.ds(0, 1), pl.ds(planes + 1, 1)
    routes = [
        ((1, 0), last, (0, rows), low, LEAD),
        ((-1, 0), first, (0, rows), high, LEAD),
        ((0, 1), whole, (rows - LEAD, LEAD), inner, 0),
        ((0, -1), whole, (0, margin), inner, end),
        ((1, -1), last, (0, margin), low, end),
        ((-1, -1), first, (0, margin), high, end),
    ]

    def halo(index, reach):
        step, from_planes, (row, count), to_planes, to_row = routes[index]
        return pltpu.make_async_remote_copy(
            src_ref=density.at[from_planes, pl.ds(row, count)],
            dst_ref=volume.at[to_planes, pl.ds(to_row, count)],
            send_sem=halo_send.at[index],
            recv_sem=halo_recv.at[index],
            device_id=reach,
            device_id_type=MESH,
        )

    for index, route in enumerate(routes):
        ok, target = near(*route[0])

        @pl.when(ok)
        def _(index=index, target=target):
            halo(index, target).start()

    @pl.when(d == 0)
    def _():
        volume[0] = jnp.zeros(volume.shape[1:], jnp.float32)

    @pl.when(d == groups - 1)
    def _():
        volume[planes + 1] = jnp.zeros(volume.shape[1:], jnp.float32)

    @pl.when(h == 0)
    def _():
        volume[1 : planes + 1, :LEAD] = jnp.zeros((planes, LEAD, cols), jnp.float32)

    @pl.when(h == towers - 1)
    def _():
        volume[:, end:tall] = jnp.zeros((planes + 2, margin, cols), jnp.float32)

    own.wait()

    lz, ly, lx = light[0], light[1], light[2]
    half_gain = [0.5 * gain[c] for c in range(3)]
    half_bias = [0.5 * bias[c] for c in range(3)]

    def shade(plane, row, count, keep):
        at = LEAD + row
        centre = volume[plane, at : at + count]
        lane = lax.broadcasted_iota(jnp.int32, (count, cols), 1)
        following = jnp.where(lane == cols - 1, 0.0, pltpu.roll(centre, cols - 1, 1))
        previous = jnp.where(lane == 0, 0.0, pltpu.roll(centre, 1, 1))
        dx = following - previous
        dz = volume[plane + 1, at : at + count] - volume[plane - 1, at : at + count]
        dy = volume[plane, at + 1 : at + 1 + count] - volume[plane, at - 1 : at - 1 + count]
        facing = (lz * dz + ly * dy + lx * dx) * lax.rsqrt(4.0 + dz * dz + dy * dy + dx * dx)
        shading = 0.25 + 1.5 * jnp.maximum(facing, 0.0)
        optical = extinction * (
            jnp.maximum(centre, 0.0) + jnp.log1p(jnp.exp(-jnp.abs(centre)))
        )
        opacity = jnp.tanh(0.5 * optical) * (1.0 + jnp.exp(-optical))
        if keep is not None:
            opacity = opacity * keep
        lit = 0.5 * (opacity * shading)
        to = pl.ds(row, count)
        for c in range(3):
            fields[c, plane - 1, to] = lit + lit * jnp.tanh(half_gain[c] * centre + half_bias[c])
        fields[3, plane - 1, to] = opacity

    inside = jnp.where(h < towers - 1, 1.0, 0.0)

    def early(plane, _):
        for row, count in spans(LEAD, rows - LEAD, 16):
            shade(plane, row, count, None)
        return 0

    lax.fori_loop(2, planes, early, 0)

    def landed(index):
        step_d, step_h = routes[index][0]
        ok, source = near(-step_d, -step_h)

        @pl.when(ok)
        def _():
            halo(index, source).wait_recv()

    def shade_low():
        for index in (0, 1, 2):
            landed(index)
        for plane in range(1, planes + 1):
            shade(plane, 0, LEAD, None)
        for row, count in spans(LEAD, rows - LEAD, 16):
            for plane in (1, planes):
                shade(plane, row, count, None)

    def shade_high():
        for index in (3, 4, 5):
            landed(index)

        def bottom(at, _):
            for plane in (2 * at + 1, 2 * at + 2):
                shade(plane, rows - LEAD, LEAD, None)
                for row, count in spans(rows, rows + margin, 16):
                    shade(plane, row, count, inside)
            return 0

        lax.fori_loop(0, planes // 2, bottom, 0)

    first_plane = d * planes

    def partial(view, block):
        step = shear[view]
        backward = reverse[view]
        colour = [jnp.zeros((share, cols), jnp.float32) for _ in range(3)]
        clear = jnp.ones((share, cols), jnp.float32)
        covered = jnp.zeros((share, cols), jnp.float32)
        for i in range(planes):
            plane = i + backward * (planes - 1 - 2 * i)
            offset = lax.div((first_plane + plane) * step, jnp.int32(total_planes))
            at = pl.ds(offset + block * share, share)
            for c in range(3):
                colour[c] = colour[c] + clear * fields[c, plane, at]
            covered = covered + clear * fields[3, plane, at]
            clear = 1.0 - covered
        return colour + [covered]

    odd = lax.rem(d, 2)
    out_step = 2 * odd - 1
    mate = d - out_step
    pair = lax.div(d, 2)
    beyond = odd * (groups - 1 - d) + (1 - odd) * d
    handing = odd * (d - 1) + (1 - odd) * (groups - 2 - d)

    def over(first, second, swap):
        front = [jnp.where(swap, b, a) for a, b in zip(first, second)]
        behind = [jnp.where(swap, a, b) for a, b in zip(first, second)]
        clear = 1.0 - front[3]
        return [f + clear * b for f, b in zip(front, behind)]

    def load(ref, block, view):
        return [ref[block, view, c] for c in range(4)]

    def store(ref, block, view, image):
        for c in range(4):
            ref[block, view, c] = image[c]

    def hand(view, block):
        return pltpu.make_async_remote_copy(
            src_ref=outgoing.at[block, view],
            dst_ref=handed.at[block, view],
            send_sem=hand_send.at[view, block],
            recv_sem=hand_recv.at[view, block],
            device_id=(mate, h),
            device_id_type=MESH,
        )

    def send(view, block):
        return pltpu.make_async_remote_copy(
            src_ref=outgoing.at[block, view],
            dst_ref=incoming.at[d, view],
            send_sem=part_send.at[view, block],
            recv_sem=part_recv.at[view, d],
            device_id=(block, h),
            device_id_type=MESH,
        )

    def receive(view, source):
        return pltpu.make_async_remote_copy(
            src_ref=outgoing.at[source, view],
            dst_ref=incoming.at[source, view],
            send_sem=part_send.at[view, source],
            recv_sem=part_recv.at[view, source],
            device_id=(source, h),
            device_id_type=MESH,
        )

    def each(count, body):
        def step(k, _):
            body(k)
            return 0

        lax.fori_loop(0, count, step, 0)

    def hand_over(view, k):
        block = odd * k + (1 - odd) * (groups - 1 - k)
        store(outgoing, block, view, partial(view, block))
        hand(view, block).start()

    def prepare(view, k):
        block = d + out_step * (1 + k)
        store(outgoing, block, view, partial(view, block))

    def to_mate(view):
        store(outgoing, mate, view, partial(view, mate))
        send(view, mate).start()

    def pass_on(view, k):
        block = odd * (groups - 1 - k) + (1 - odd) * k
        hand(view, block).wait_recv()
        own_part, other = load(outgoing, block, view), load(handed, block, view)
        swap = reverse[view] != odd
        store(outgoing, block, view, over(own_part, other, swap))
        send(view, block).start()

    reach = lax.div((first_plane + planes - 1) * margin, jnp.int32(total_planes))

    def hand_round(early):
        def one(k):
            block = odd * k + (1 - odd) * (groups - 1 - k)
            ready = ((block + 1) * share + reach <= rows - LEAD) & (odd == 1)

            @pl.when(ready if early else jnp.logical_not(ready))
            def _():
                each(views, lambda view: hand_over(view, k))

        each(handing, one)

    shade_low()
    hand_round(True)
    shade_high()
    hand_round(False)
    each(views, to_mate)
    each(views, lambda view: each(beyond, lambda k: prepare(view, k)))
    each(views, lambda view: store(incoming, d, view, partial(view, d)))
    each(beyond, lambda k: each(views, lambda view: pass_on(view, k)))

    def finish(view):
        swap = reverse[view] == 1
        receive(view, mate).wait_recv()
        both = over(load(incoming, d, view), load(incoming, mate, view), reverse[view] != odd)
        store(incoming, 2 * pair + 1, view, both)
        sources = [jnp.where(j > pair, 2 * j, 2 * j + 1) for j in range(groups // 2)]
        for j, source in enumerate(sources):

            @pl.when(j != pair)
            def _():
                receive(view, source).wait_recv()

        total = load(incoming, sources[0], view)
        for source in sources[1:]:
            total = over(total, load(incoming, source, view), swap)
        for c in range(4):
            out[c, view] = total[c]

    for view in range(views):
        finish(view)

    for index, route in enumerate(routes):
        ok, target = near(*route[0])

        @pl.when(ok)
        def _(index=index, target=target):
            halo(index, target).wait_send()

    def sent(view):
        send(view, mate).wait_send()
        each(handing, lambda k: hand(view, d - out_step * (2 + k)).wait_send())
        each(beyond, lambda k: send(view, d + out_step * (1 + k)).wait_send())

    each(views, sent)


def general(groups, towers, density, light, gain, bias, shear, reverse):
    planes, rows, cols = density.shape
    views = shear.shape[0]
    share = rows // groups
    tall = LEAD + rows + rows // 2
    scalars = pl.BlockSpec(memory_space=pltpu.SMEM)
    return pl.pallas_call(
        functools.partial(kernel, groups, towers),
        name="render",
        out_shape=pltpu.VMEM((4, views, share, cols), jnp.float32),
        in_specs=[pl.BlockSpec(memory_space=pltpu.HBM)] + [scalars] * 5,
        out_specs=pl.BlockSpec(memory_space=pltpu.VMEM),
        scratch_shapes=[
            pltpu.VMEM((planes + 2, tall + LEAD, cols), jnp.float32),
            pltpu.VMEM((4, planes, rows + rows // 2, cols), jnp.float32),
            pltpu.VMEM((groups, views, 4, share, cols), jnp.float32),
            pltpu.VMEM((groups, views, 4, share, cols), jnp.float32),
            pltpu.VMEM((groups, views, 4, share, cols), jnp.float32),
            pltpu.SemaphoreType.DMA,
            pltpu.SemaphoreType.DMA((6,)),
            pltpu.SemaphoreType.DMA((6,)),
            pltpu.SemaphoreType.DMA((views, groups)),
            pltpu.SemaphoreType.DMA((views, groups)),
            pltpu.SemaphoreType.DMA((views, groups)),
            pltpu.SemaphoreType.DMA((views, groups)),
        ],
        compiler_params=pltpu.CompilerParams(collective_id=0, has_side_effects=True, vmem_limit_bytes=60 * 1024 * 1024),
    )(density, light, gain, bias, shear, reverse)


def line(towers, density, light, gain, bias, shear, reverse):
    planes, rows, cols = density.shape
    views = shear.shape[0]
    groups = 4
    share = rows // groups
    whole = pl.BlockSpec(memory_space=pltpu.HBM)
    images = pltpu.VMEM((groups, views, 4, share, cols), jnp.float32)
    return pl.pallas_call(
        functools.partial(line_kernel, towers),
        name="render",
        out_shape=pltpu.VMEM((4, views, share, cols), jnp.float32),
        in_specs=[whole] * 6,
        out_specs=pl.BlockSpec(memory_space=pltpu.VMEM),
        scratch_shapes=[pltpu.SMEM(scalar.shape, scalar.dtype) for scalar in (light, gain, bias, shear, reverse)]
        + [
            pltpu.VMEM((2 * planes + 5, LEAD + rows + rows // 2 + LEAD, cols), jnp.float32),
            pltpu.VMEM((4, 2 * planes + 4, rows + rows // 2, cols), jnp.float32),
            images,
            images,
            images,
            pltpu.SemaphoreType.DMA((10,)),
            pltpu.SemaphoreType.DMA((8,)),
            pltpu.SemaphoreType.DMA((3 * views + 1,)),
            pltpu.SemaphoreType.DMA((1 + views,)),
            pltpu.SemaphoreType.REGULAR,
        ],
        compiler_params=pltpu.CompilerParams(collective_id=0, has_side_effects=True, vmem_limit_bytes=60 * 1024 * 1024),
    )(density, light, gain, bias, shear, reverse)


def on_device(groups, towers, density, light, gain, bias, shear, reverse):
    planes, rows, _ = density.shape
    if groups == 4 and planes >= 8 and rows % 64 == 0:
        return line(towers, density, light, gain, bias, shear, reverse)
    return general(groups, towers, density, light, gain, bias, shear, reverse)


def solution(mesh):
    groups, towers = mesh.shape["depth"], mesh.shape["height"]
    placed = (P("depth", "height", None), P(), P(), P(), P(), P())
    return jax.shard_map(
        functools.partial(on_device, groups, towers),
        mesh=mesh,
        in_specs=placed,
        out_specs=P(None, None, ("height", "depth"), None),
        check_vma=False,
    )
```

```python
import functools

import jax
import jax.numpy as jnp
from jax import lax
from jax.experimental import pallas as pl
from jax.experimental.pallas import tpu as pltpu
from jax.sharding import PartitionSpec as P

EXTINCTION = 2.5
LEAD = 8
TOGETHER = 6
MESH = pl.DeviceIdType.MESH


def spans(low, high, size):
    return [(at, min(size, high - at)) for at in range(low, high, size)]


def line_kernel(
    towers,
    density,
    light_in,
    gain_in,
    bias_in,
    shear_in,
    reverse_in,
    out,
    light,
    gain,
    bias,
    shear,
    reverse,
    volume,
    fields,
    outgoing,
    incoming,
    handed,
    sent_sem,
    halo_sem,
    hand_sem,
    part_sem,
    go_sem,
):
    planes, rows, cols = density.shape
    margin = rows // 2
    views = shear.shape[0]
    groups = 4
    share = rows // groups
    total_planes = planes * groups
    extinction = EXTINCTION / total_planes
    d = lax.axis_index("depth")
    h = lax.axis_index("height")
    above, below = (h - 1 >= 0) & (h - 1 < towers), (h + 1 >= 0) & (h + 1 < towers)
    end = LEAD + rows
    own_planes = pl.ds(2, planes)
    images, plane_sent, edge_sent, down_sent, up_sent, corner_sent, rest_sent, relay_sent, flank_edge_sent, flank_end_sent = range(10)
    slab_sent, slab_edge_sent, flank_sent = edge_sent, rest_sent, rest_sent
    pair_in, peer_in, edge_in, down_in, up_in, pair_corner_in, peer_corner_in, rest_in = range(8)
    slab_in, slab_edge_in, slab_end_in = pair_in, edge_in, peer_in
    flank_in, flank_edge_in, flank_end_in = pair_in, edge_in, peer_in

    early_planes = jnp.where(d < groups // 2, planes - 2, 0)
    later_planes = jnp.where(d < groups // 2, 0, 2)
    own, own_rest = (
        pltpu.make_async_copy(
            density.at[pl.ds(start, count)],
            volume.at[pl.ds(2 + start, count), pl.ds(LEAD, rows)],
            sent_sem.at[index],
        )
        for start, count, index in ((early_planes, 2, images), (later_planes, planes - 2, relay_sent))
    )
    own.start()
    own_rest.start()

    scalars = [
        pltpu.make_async_copy(source, target, sent_sem.at[(edge_sent, down_sent, up_sent, corner_sent, rest_sent)[index]])
        for index, (source, target) in enumerate(
            zip((light_in, gain_in, bias_in, shear_in, reverse_in), (light, gain, bias, shear, reverse))
        )
    ]
    for scalar in scalars:
        scalar.start()

    def valid(step_d, step_h):
        ok = None
        for at, step, count in ((d, step_d, groups), (h, step_h, towers)):
            if step:
                test = (at + step >= 0) & (at + step < count)
                ok = test if ok is None else ok & test
        return ok

    barrier = pltpu.get_barrier_semaphore()
    expected = jnp.int32(0)
    greets = {at: [] for at in range(groups)}
    awaits = {at: [] for at in range(groups)}

    def greet(at, step_d, step_h, parity=None):
        greets[at].append((step_d, step_h, parity))
        awaits[at + step_d].append((-step_d, -step_h, parity if parity is None else (parity + step_h) % 2))

    for at in range(groups):
        mate = (at ^ 1) - at
        outer = at in (0, 3)
        for step_h in (1, -1):
            greet(at, mate if outer else 0, step_h)
            greet(at, 0 if outer else mate, step_h, 0)
        greet(at, mate, 0)
        if not outer:
            greet(at, -mate, 0)
            greet(at, -mate, 1)
    greet(0, 2, 0)

    def meets(at, step_d, step_h, parity):
        ok = (d == at) & valid(step_d, step_h)
        return ok if parity is None else ok & (lax.rem(h, 2) == parity)

    for at in range(groups):

        for step_d, step_h, parity in greets[at]:

            @pl.when(meets(at, step_d, step_h, parity))
            def _(target=(d + step_d, h + step_h)):
                pl.semaphore_signal(barrier, inc=1, device_id=target, device_id_type=MESH)

        for step in awaits[at]:
            expected = expected + jnp.where(meets(at, *step), 1, 0)

    own.wait()

    @pl.when(d == groups - 1)
    def _():
        with jax.named_scope("barrier"):
            pl.semaphore_wait(barrier, expected)
        first_pair = volume.at[pl.ds(2, 2), pl.ds(LEAD, rows - share)]
        first_target = volume.at[pl.ds(planes + 2, 2), pl.ds(LEAD, rows - share)]
        pltpu.make_async_remote_copy(
            src_ref=first_pair,
            dst_ref=first_target,
            send_sem=sent_sem.at[plane_sent],
            recv_sem=halo_sem.at[pair_in],
            device_id=(d - 1, h),
            device_id_type=MESH,
        ).start()

    for scalar in scalars:
        scalar.wait()
    own_rest.wait()

    lz, ly, lx = light[0], light[1], light[2]
    half_gain = [0.5 * gain[c] for c in range(3)]
    half_bias = [0.5 * bias[c] for c in range(3)]
    inside = jnp.where(below, 1.0, 0.0)

    def shade(plane, row, count, keep, loose=False):
        at = LEAD + row
        centre = volume[plane, at : at + count]
        lane = lax.broadcasted_iota(jnp.int32, (count, cols), 1)
        following = jnp.where(lane == cols - 1, 0.0, pltpu.roll(centre, cols - 1, 1))
        previous = jnp.where(lane == 0, 0.0, pltpu.roll(centre, 1, 1))
        dx = following - previous
        dz = volume[plane + 1, at : at + count] - volume[plane - 1, at : at + count]
        below_it = pltpu.roll(centre, count - 1, 0) if loose else volume[plane, at + 1 : at + 1 + count]
        dy = below_it - volume[plane, at - 1 : at - 1 + count]
        facing = (lz * dz + ly * dy + lx * dx) * lax.rsqrt(4.0 + dz * dz + dy * dy + dx * dx)
        shading = 0.25 + 1.5 * jnp.maximum(facing, 0.0)
        optical = extinction * (
            jnp.maximum(centre, 0.0) + jnp.log1p(jnp.exp(-jnp.abs(centre)))
        )
        opacity = jnp.tanh(0.5 * optical) * (1.0 + jnp.exp(-optical))
        if keep is not None:
            opacity = opacity * keep
        lit = 0.5 * (opacity * shading)
        to = pl.ds(row, count)
        for c in range(3):
            fields[c, plane, to] = lit + lit * jnp.tanh(half_gain[c] * centre + half_bias[c])
        fields[3, plane, to] = opacity

    def shade_box(low, high, top, bottom, loose=False):
        tiles = (bottom - top) // 8
        together = max(1, min(high - low, -(-TOGETHER // tiles)))
        looped = (high - low) // together if high - low > together else 0

        def some(plane, count):
            for step in range(count):
                for row, size in spans(top, min(bottom, rows), 16):
                    shade(plane + step, row, size, None, loose)
                for row, size in spans(max(top, rows), bottom, 16):
                    shade(plane + step, row, size, inside)

        if looped:

            def step(index, _):
                some(low + index * together, together)
                return 0

            lax.fori_loop(0, looped, step, 0)
        done = low + looped * together
        if done < high:
            some(done, high - done)

    def copy_to(source, target, sent, received, device):
        return pltpu.make_async_remote_copy(
            src_ref=source,
            dst_ref=target,
            send_sem=sent_sem.at[sent],
            recv_sem=received,
            device_id=device,
            device_id_type=MESH,
        )

    def over(first, second, swap):
        front = [jnp.where(swap, b, a) for a, b in zip(first, second)]
        behind = [jnp.where(swap, a, b) for a, b in zip(first, second)]
        clear = 1.0 - front[3]
        return [f + clear * b for f, b in zip(front, behind)]

    everything = (0, share)
    odd = lax.rem(h, 2) == 1
    distant = (lax.rem(h, 2) == 0) & (h > 0)
    ahead = jnp.where(h == towers // 2, views // 2, 1)
    some, rest = (0, ahead), (ahead, views - 1)

    def load(ref, block, view, part):
        return [ref[block, view, c, pl.ds(*part)] for c in range(4)]

    def store(ref, block, view, part, image):
        for c in range(4):
            ref[block, view, c, pl.ds(*part)] = image[c]

    def each_view(body, start=0, stop=views):
        def step(view, _):
            body(view)
            return 0

        lax.fori_loop(start, stop, step, 0)

    def extent(at):
        low = {0: 2, 1: 1, 2: 2, 3: 3}[at]
        high = {0: planes + 1, 1: planes + 2, 2: planes + 3, 3: planes + 2}[at]
        reach = (at * planes + high - 3) * margin // total_planes
        return low, high, reach, min(margin, -(-(reach + 1) // 8) * 8)

    def brick(at):
        outer = at in (0, groups - 1)
        lower = at < groups // 2
        mate = at ^ 1
        first = at * planes - 2
        low, high, reach, border = extent(at)
        extra = -(-reach // 8) * 8
        mate_pair = pl.ds(0, 2) if lower else pl.ds(planes + 2, 2)
        edge = {0: planes + 1, 1: 1, 2: planes + 2, 3: 2}[at]
        mate_edge = {0: 1, 3: planes + 2}.get(at, edge)
        others = [2, 3] if lower else [0, 1]
        other = {0: 2, 1: 2, 2: 1, 3: 1}[at]
        peer = {1: 2, 2: 1}.get(at)
        halves = [(share // 2, share // 2), (0, share // 2)]
        parts = {0: halves, 1: [everything], 2: [everything], 3: [everything]}
        hand_at = {
            (block, part): index
            for index, (block, part) in enumerate((block, part) for block in others for part in parts[block])
        }

        def plane_copy(source, target, take, put, sent, received, device):
            return copy_to(
                volume.at[source, pl.ds(*take)],
                volume.at[target, pl.ds(*put)],
                sent,
                halo_sem.at[received],
                device,
            )

        own_pair = pl.ds(planes, 2) if lower else pl.ds(2, 2)
        own_peer = pl.ds(planes + 1, 1) if lower else pl.ds(2, 1)
        peer_target = pl.ds(1, 1) if lower else pl.ds(planes + 2, 1)
        peer_border = extent(peer)[3] if peer else None
        whole = (LEAD, rows)

        cut = rows - share
        soon, after = ((LEAD + share, cut), (LEAD, share)) if lower else ((LEAD, cut), (LEAD + cut, share))

        def pair_copy():
            return plane_copy(own_pair, mate_pair, soon, soon, plane_sent, pair_in, (mate, h))

        def pair_rest():
            return plane_copy(own_pair, mate_pair, after, after, rest_sent, rest_in, (mate, h))

        def peer_copy():
            return plane_copy(own_peer, peer_target, whole, whole, plane_sent, peer_in, (peer, h))

        def pair_relay(step):
            take, put = (LEAD, border), (end, border)
            return plane_copy(mate_pair, mate_pair, take, put, relay_sent, pair_corner_in, (d, h + step))

        def peer_corner(step, count):
            take, put = (LEAD, count), (end, count)
            return plane_copy(own_peer, peer_target, take, put, corner_sent, peer_corner_in, (d + peer - at, h + step))

        def edge_copy(step):
            take, put = (rows, LEAD), (0, LEAD)
            return plane_copy(edge, mate_edge, take, put, edge_sent, edge_in, (d + mate - at, h + step))

        span_high = 2 * planes + 2
        span_reach = extent(1)[2]
        span_rows = share + extent(1)[3]
        slab = pl.ds(planes + 2, planes)
        slab_end = pl.ds(2 * planes + 2, 1)

        def slab_copy():
            take = (LEAD, span_rows)
            return plane_copy(own_planes, slab, take, take, slab_sent, slab_in, (0 if at else 1, h))

        def slab_edge_copy(step):
            take, put = (rows, LEAD), (0, LEAD)
            return plane_copy(own_planes, slab, take, put, slab_edge_sent, slab_edge_in, (d + (-1 if at else 1), h + step))

        def slab_end_copy():
            take = (LEAD, span_rows)
            return plane_copy(pl.ds(2, 1), slab_end, take, take, slab_sent, slab_end_in, (0 if at else 2, h))

        flank = planes + 4
        flank_top = rows - share - LEAD
        flank_reach = (3 * planes - 1) * margin // total_planes
        flank_rows = min(extent(2)[3], -(-(flank_reach + 1) // 8) * 8)
        flank_planes = pl.ds(flank, planes)

        def flank_copy():
            take = (LEAD + flank_top, share + LEAD)
            return plane_copy(own_planes, flank_planes, take, take, flank_sent, flank_in, (3 if at == 2 else 2, h))

        def flank_edge_copy(step):
            take, put = (LEAD, flank_rows), (end, flank_rows)
            return plane_copy(own_planes, flank_planes, take, put, flank_edge_sent, flank_edge_in, (d + (1 if at == 2 else -1), h + step))

        def flank_end_copy():
            take = (LEAD + flank_top, share + LEAD + flank_rows)
            return plane_copy(pl.ds(1, 1), pl.ds(flank - 1, 1), take, take, flank_end_sent, flank_end_in, (3 if at == 2 else 2, h))

        def down_copy(step):
            return copy_to(
                volume.at[own_planes, pl.ds(rows, LEAD)],
                volume.at[own_planes, pl.ds(0, LEAD)],
                down_sent,
                halo_sem.at[down_in],
                (d, h + step),
            )

        def up_copy(step):
            return copy_to(
                volume.at[own_planes, pl.ds(LEAD, border)],
                volume.at[own_planes, pl.ds(end, border)],
                up_sent,
                halo_sem.at[up_in],
                (d, h + step),
            )

        def hand(view, block, part):
            split = block == 1 and part in halves
            index = 3 * views - 1 + halves.index(part) if split else hand_at[block, part] * views + view
            return copy_to(
                outgoing.at[block, view, :, pl.ds(*part)],
                handed.at[block, view, :, pl.ds(*part)],
                images,
                hand_sem.at[index],
                (mate, h),
            )

        def send(view, block, part):
            slot = 0 if block == mate else 1 + view
            return copy_to(
                outgoing.at[block, view, :, pl.ds(*part)],
                incoming.at[at, view, :, pl.ds(*part)],
                images,
                part_sem.at[slot],
                (block, h),
            )

        def receive(view):
            return copy_to(
                outgoing.at[at, view],
                incoming.at[other, view],
                images,
                part_sem.at[1 + view],
                (other, h),
            )

        def receive_mate():
            return copy_to(outgoing.at[at], incoming.at[mate], images, part_sem.at[0], (mate, h))

        def partial(view, block, part, span=None):
            step = shear[view]
            backward = reverse[view]
            count = high - low if span is None else 2 * planes
            size = part[1]
            colour = [jnp.zeros((size, cols), jnp.float32) for _ in range(3)]
            clear = jnp.ones((size, cols), jnp.float32)
            covered = jnp.zeros((size, cols), jnp.float32)
            for i in range(count):
                index = jnp.where(backward == 1, count - 1 - i, i)
                if span is None:
                    plane, depth, limit = low + index, first + low + index, reach
                else:
                    plane, depth, limit = span(index)
                offset = lax.div(depth * step, jnp.int32(total_planes))
                offset = jnp.minimum(jnp.maximum(offset, 0), limit)
                rows_at = pl.ds(offset + block * share + part[0], size)
                for c in range(3):
                    colour[c] = colour[c] + clear * fields[c, plane, rows_at]
                covered = covered + clear * fields[3, plane, rows_at]
                clear = 1.0 - covered
            return colour + [covered]

        def send_mate():
            def one(view):
                store(outgoing, mate, view, everything, partial(view, mate, everything))
                send(view, mate, everything).start()

            each_view(one)

        def keep_own():
            def front_pair(index):
                return 2 + index, index, span_reach

            def back_pair(index):
                return jnp.where(index < planes, flank + index, index - planes + 2), 2 * planes + index, reach

            span = {0: front_pair, 3: back_pair}.get(at)
            each_view(lambda view: store(incoming, at, view, everything, partial(view, at, everything, span)))

        def hand_over(block, part=everything, which=(0, views)):
            def one(view):
                store(outgoing, block, view, part, partial(view, block, part))
                hand(view, block, part).start()

            each_view(one, *which)

        def pass_on(block, part=everything, which=(0, views)):
            def one(view):
                mine = partial(view, block, part)
                hand(view, block, part).wait_recv()
                theirs = load(handed, block, view, part)
                swap = reverse[view] == 1
                merged = over(theirs, mine, swap) if lower else over(mine, theirs, swap)
                store(outgoing, block, view, part, merged)
                send(view, block, part).start()

            each_view(one, *which)

        def images_gone(blocks):
            gone = pl.ds(0, blocks)
            copy_to(outgoing.at[gone], handed.at[gone], images, hand_sem.at[0], (mate, h)).wait_send()

        def begin():
            if at == 3:
                return
            with jax.named_scope("barrier"):
                pl.semaphore_wait(barrier, expected)
            if outer:
                pair_copy().start()
                if lower:
                    pair_rest().start()
            else:

                @pl.when(jnp.logical_not(odd))
                def _():
                    pl.semaphore_signal(go_sem, inc=1, device_id=(mate, h), device_id_type=MESH)

                peer_copy().start()
                (slab_copy if lower else slab_end_copy)().start()
                if not lower:
                    flank_copy().start()
                columns()

        def columns():
            if outer:

                @pl.when(jnp.logical_not(odd))
                def _():
                    with jax.named_scope("w_go"):
                        pl.semaphore_wait(go_sem, 1)

            @pl.when(below)
            def _():
                down_copy(1).start()
                if outer:
                    edge_copy(1).start()
                if at == 1:
                    slab_edge_copy(1).start()

            @pl.when(above)
            def _():
                if not outer:
                    peer_corner(-1, peer_border).start()
                if at == 2:
                    flank_edge_copy(-1).start()
                up_copy(-1).start()

        def blank():
            if outer:
                volume[1 if lower else planes + 2] = jnp.zeros(volume.shape[1:], jnp.float32)

            @pl.when(jnp.logical_not(above))
            def _():
                volume[:, :LEAD] = jnp.zeros((2 * planes + 5, LEAD, cols), jnp.float32)

            @pl.when(jnp.logical_not(below))
            def _():
                volume[:, end : end + border] = jnp.zeros((2 * planes + 5, border, cols), jnp.float32)

        def top_landed():
            @pl.when(above)
            def _():
                with jax.named_scope("w_down"):
                    down_copy(-1).wait_recv()

        def bottom_landed():
            @pl.when(below)
            def _():
                with jax.named_scope("w_up"):
                    up_copy(1).wait_recv()

        def peer_corner_landed():
            @pl.when(below)
            def _():
                with jax.named_scope("w_pcorner"):
                    peer_corner(1, border).wait_recv()

        def pair_corner_landed():
            @pl.when(below)
            def _():
                with jax.named_scope("w_corner"):
                    pair_relay(1).wait_recv()

        def edge_landed():
            @pl.when(above)
            def _():
                with jax.named_scope("w_edge"):
                    edge_copy(-1).wait_recv()

        blank()
        if at == 0:
            shade_box(low, high, LEAD, rows - LEAD)
            begin()
            with jax.named_scope("hand2"):
                hand_over(2)
            columns()
            top_landed()
            bottom_landed()
            shade_box(low, high, rows - LEAD, rows + extra)
            with jax.named_scope("hand3"):
                hand_over(3)
            shade_box(low, high, 0, LEAD)
            with jax.named_scope("mate"):
                send_mate()
            with jax.named_scope("w_slab"):
                slab_copy().wait_recv()

                @pl.when(above)
                def _():
                    slab_edge_copy(-1).wait_recv()

                slab_end_copy().wait_recv()
            shade_box(high, span_high, 0, -(-(share + span_reach) // 8) * 8)
            keep_own()
        elif at == 3:
            begin()
            pl.when(odd)(columns)
            shade_box(low, high, LEAD, rows - LEAD)
            with jax.named_scope("hand0b"):
                hand_over(0, halves[0])
            pair_rest().start()
            pl.when(jnp.logical_not(odd))(columns)
            shade_box(low, high, rows - LEAD, rows, True)

            def early():
                top_landed()
                shade_box(low, high, 0, LEAD)
                with jax.named_scope("hand0a"):
                    hand_over(0, halves[1])

            def late(which):
                with jax.named_scope("hand1"):
                    hand_over(1, everything, which)

            def last():
                for half in halves:
                    hand_over(1, half, (views - 1, views))

            @pl.when(distant)
            def _():
                late(some)
                early()
                late(rest)
                last()

            @pl.when(h == 0)
            def _():
                early()
                late((0, views - 1))
                last()

            @pl.when(odd)
            def _():
                early()
                late((0, views - 1))
                last()

            bottom_landed()
            shade_box(low, high, rows - LEAD, rows)
            shade_box(low, high, rows, rows + extra)
            images_gone(2)
            with jax.named_scope("mate"):
                send_mate()
            with jax.named_scope("w_flank"):
                flank_copy().wait_recv()

                @pl.when(below)
                def _():
                    flank_edge_copy(1).wait_recv()

                flank_end_copy().wait_recv()
            top_row, bottom_row = rows - share, rows + flank_rows
            there = pl.ds(LEAD + top_row, bottom_row - top_row)
            volume[1, there] = volume[flank + planes - 1, there]
            volume[flank + planes, there] = volume[2, there]
            shade_box(flank, flank + planes, top_row, bottom_row)
            shade_box(2, 3, top_row, bottom_row)
            keep_own()
        else:
            shade_box(3, planes + 1, LEAD, rows - LEAD)
            begin()
            far_edge = planes + 1 if lower else 2
            seam = min(2 if lower else planes + 1, edge)


            def top():
                top_landed()
                edge_landed()
                shade_box(low, high, 0, LEAD)

            def relay():
                @pl.when(above)
                def _():
                    pair_relay(-1).start()

            def rest_landed():
                with jax.named_scope("w_rest"):
                    pair_rest().wait_recv()
                if lower:
                    relay()
                    shade_box(seam, seam + 2, LEAD, share + LEAD)
                else:
                    shade_box(seam, seam + 2, rows - share - LEAD, rows - LEAD)

            def bottom():
                bottom_landed()
                pair_corner_landed()
                if lower:
                    peer_corner_landed()
                shade_box(low, high, rows - LEAD, rows + extra)

            with jax.named_scope("w_peer"):
                peer_copy().wait_recv()
            shade_box(far_edge, far_edge + 1, LEAD, rows - LEAD)
            if lower:
                shade_box(3, planes + 2, rows - LEAD, rows, True)
            with jax.named_scope("w_pair"):
                pair_copy().wait_recv()
            if lower:
                shade_box(seam, seam + 2, share + LEAD, rows - LEAD)
                rest_landed()
                with jax.named_scope("pass2"):
                    pass_on(2)
                top()
                bottom()
                with jax.named_scope("pass3"):
                    pass_on(3)
            else:
                relay()
                shade_box(seam, seam + 2, LEAD, rows - share - LEAD)
                with jax.named_scope("pass0b"):
                    pass_on(0, halves[0])
                peer_corner_landed()
                flank_end_copy().start()
                rest_landed()

                def last():
                    for half in halves:
                        pass_on(1, half, (views - 1, views))

                def early():
                    top()
                    with jax.named_scope("pass0a"):
                        pass_on(0, halves[1])

                @pl.when(distant)
                def _():
                    with jax.named_scope("pass1"):
                        pass_on(1, everything, some)
                    early()
                    pass_on(1, everything, rest)
                    last()

                @pl.when(jnp.logical_not(distant))
                def _():
                    early()
                    with jax.named_scope("pass1"):
                        pass_on(1, everything, (0, views - 1))
                        last()

                bottom()
            keep_own()

        def finish(view):
            swap = reverse[view] == 1
            near = load(incoming, at, view, everything)
            if not outer:
                theirs = load(incoming, mate, view, everything)
                near = over(near, theirs, swap) if at < mate else over(theirs, near, swap)
            with jax.named_scope("w_other"):
                receive(view).wait_recv()
            far = load(incoming, other, view, everything)
            total = over(near, far, swap) if lower else over(far, near, swap)
            for c in range(4):
                out[c, view] = total[c]

        if not outer:
            with jax.named_scope("w_mate"):
                receive_mate().wait_recv()

        for view in range(views):
            finish(view)

        if outer:
            pair_copy().wait_send()
            pair_rest().wait_send()
        else:
            peer_copy().wait_send()
            (slab_copy if lower else slab_end_copy)().wait_send()
            if not lower:
                flank_copy().wait_send()
                flank_end_copy().wait_send()

        @pl.when(below)
        def _():
            down_copy(1).wait_send()
            if outer:
                edge_copy(1).wait_send()
            if at == 1:
                slab_edge_copy(1).wait_send()

        @pl.when(above)
        def _():
            up_copy(-1).wait_send()
            if not outer:
                peer_corner(-1, peer_border).wait_send()
                pair_relay(-1).wait_send()
            if at == 2:
                flank_edge_copy(-1).wait_send()

        images_gone({0: 3, 1: 2, 2: 2, 3: 1}[at])
    for at in range(groups):

        @pl.when(d == at)
        def _():
            brick(at)


def kernel(
    groups,
    towers,
    density,
    light,
    gain,
    bias,
    shear,
    reverse,
    out,
    volume,
    fields,
    outgoing,
    incoming,
    handed,
    local_sem,
    halo_send,
    halo_recv,
    hand_send,
    hand_recv,
    part_send,
    part_recv,
):
    planes, rows, cols = density.shape
    margin = rows // 2
    views = shear.shape[0]
    share = rows // groups
    total_planes = planes * groups
    extinction = EXTINCTION / total_planes
    d = lax.axis_index("depth")
    h = lax.axis_index("height")
    end = LEAD + rows
    tall = end + margin

    own = pltpu.make_async_copy(
        density, volume.at[pl.ds(1, planes), pl.ds(LEAD, rows)], local_sem
    )
    own.start()

    def near(step_d, step_h):
        ok = None
        for at, step, count in ((d, step_d, groups), (h, step_h, towers)):
            if step:
                test = (at + step >= 0) & (at + step < count)
                ok = test if ok is None else ok & test
        return ok, (d + step_d, h + step_h)

    barrier = pltpu.get_barrier_semaphore()
    beside = [(0, 1), (0, -1), (1, 1), (1, -1), (-1, 1), (-1, -1), (1, 0), (-1, 0)]
    if groups > 4:
        beside += [(step * hop, 0) for hop in range(2, groups) for step in (1, -1)]
    expected = jnp.int32(0)
    for step_d, step_h in beside:
        ok, target = near(step_d, step_h)
        expected = expected + jnp.where(ok, 1, 0)

        @pl.when(ok)
        def _(target=target):
            pl.semaphore_signal(barrier, inc=1, device_id=target, device_id_type=MESH)

    pl.semaphore_wait(barrier, expected)

    whole = pl.ds(0, planes)
    inner = pl.ds(1, planes)
    first, last = pl.ds(0, 1), pl.ds(planes - 1, 1)
    low, high = pl.ds(0, 1), pl.ds(planes + 1, 1)
    routes = [
        ((1, 0), last, (0, rows), low, LEAD),
        ((-1, 0), first, (0, rows), high, LEAD),
        ((0, 1), whole, (rows - LEAD, LEAD), inner, 0),
        ((0, -1), whole, (0, margin), inner, end),
        ((1, -1), last, (0, margin), low, end),
        ((-1, -1), first, (0, margin), high, end),
    ]

    def halo(index, reach):
        step, from_planes, (row, count), to_planes, to_row = routes[index]
        return pltpu.make_async_remote_copy(
            src_ref=density.at[from_planes, pl.ds(row, count)],
            dst_ref=volume.at[to_planes, pl.ds(to_row, count)],
            send_sem=halo_send.at[index],
            recv_sem=halo_recv.at[index],
            device_id=reach,
            device_id_type=MESH,
        )

    for index, route in enumerate(routes):
        ok, target = near(*route[0])

        @pl.when(ok)
        def _(index=index, target=target):
            halo(index, target).start()

    @pl.when(d == 0)
    def _():
        volume[0] = jnp.zeros(volume.shape[1:], jnp.float32)

    @pl.when(d == groups - 1)
    def _():
        volume[planes + 1] = jnp.zeros(volume.shape[1:], jnp.float32)

    @pl.when(h == 0)
    def _():
        volume[1 : planes + 1, :LEAD] = jnp.zeros((planes, LEAD, cols), jnp.float32)

    @pl.when(h == towers - 1)
    def _():
        volume[:, end:tall] = jnp.zeros((planes + 2, margin, cols), jnp.float32)

    own.wait()

    lz, ly, lx = light[0], light[1], light[2]
    half_gain = [0.5 * gain[c] for c in range(3)]
    half_bias = [0.5 * bias[c] for c in range(3)]

    def shade(plane, row, count, keep):
        at = LEAD + row
        centre = volume[plane, at : at + count]
        lane = lax.broadcasted_iota(jnp.int32, (count, cols), 1)
        following = jnp.where(lane == cols - 1, 0.0, pltpu.roll(centre, cols - 1, 1))
        previous = jnp.where(lane == 0, 0.0, pltpu.roll(centre, 1, 1))
        dx = following - previous
        dz = volume[plane + 1, at : at + count] - volume[plane - 1, at : at + count]
        dy = volume[plane, at + 1 : at + 1 + count] - volume[plane, at - 1 : at - 1 + count]
        facing = (lz * dz + ly * dy + lx * dx) * lax.rsqrt(4.0 + dz * dz + dy * dy + dx * dx)
        shading = 0.25 + 1.5 * jnp.maximum(facing, 0.0)
        optical = extinction * (
            jnp.maximum(centre, 0.0) + jnp.log1p(jnp.exp(-jnp.abs(centre)))
        )
        opacity = jnp.tanh(0.5 * optical) * (1.0 + jnp.exp(-optical))
        if keep is not None:
            opacity = opacity * keep
        lit = 0.5 * (opacity * shading)
        to = pl.ds(row, count)
        for c in range(3):
            fields[c, plane - 1, to] = lit + lit * jnp.tanh(half_gain[c] * centre + half_bias[c])
        fields[3, plane - 1, to] = opacity

    inside = jnp.where(h < towers - 1, 1.0, 0.0)

    def early(plane, _):
        for row, count in spans(LEAD, rows - LEAD, 16):
            shade(plane, row, count, None)
        return 0

    lax.fori_loop(2, planes, early, 0)

    def landed(index):
        step_d, step_h = routes[index][0]
        ok, source = near(-step_d, -step_h)

        @pl.when(ok)
        def _():
            halo(index, source).wait_recv()

    def shade_low():
        for index in (0, 1, 2):
            landed(index)
        for plane in range(1, planes + 1):
            shade(plane, 0, LEAD, None)
        for row, count in spans(LEAD, rows - LEAD, 16):
            for plane in (1, planes):
                shade(plane, row, count, None)

    def shade_high():
        for index in (3, 4, 5):
            landed(index)

        def bottom(at, _):
            for plane in (2 * at + 1, 2 * at + 2):
                shade(plane, rows - LEAD, LEAD, None)
                for row, count in spans(rows, rows + margin, 16):
                    shade(plane, row, count, inside)
            return 0

        lax.fori_loop(0, planes // 2, bottom, 0)

    first_plane = d * planes

    def partial(view, block):
        step = shear[view]
        backward = reverse[view]
        colour = [jnp.zeros((share, cols), jnp.float32) for _ in range(3)]
        clear = jnp.ones((share, cols), jnp.float32)
        covered = jnp.zeros((share, cols), jnp.float32)
        for i in range(planes):
            plane = i + backward * (planes - 1 - 2 * i)
            offset = lax.div((first_plane + plane) * step, jnp.int32(total_planes))
            at = pl.ds(offset + block * share, share)
            for c in range(3):
                colour[c] = colour[c] + clear * fields[c, plane, at]
            covered = covered + clear * fields[3, plane, at]
            clear = 1.0 - covered
        return colour + [covered]

    odd = lax.rem(d, 2)
    out_step = 2 * odd - 1
    mate = d - out_step
    pair = lax.div(d, 2)
    beyond = odd * (groups - 1 - d) + (1 - odd) * d
    handing = odd * (d - 1) + (1 - odd) * (groups - 2 - d)

    def over(first, second, swap):
        front = [jnp.where(swap, b, a) for a, b in zip(first, second)]
        behind = [jnp.where(swap, a, b) for a, b in zip(first, second)]
        clear = 1.0 - front[3]
        return [f + clear * b for f, b in zip(front, behind)]

    def load(ref, block, view):
        return [ref[block, view, c] for c in range(4)]

    def store(ref, block, view, image):
        for c in range(4):
            ref[block, view, c] = image[c]

    def hand(view, block):
        return pltpu.make_async_remote_copy(
            src_ref=outgoing.at[block, view],
            dst_ref=handed.at[block, view],
            send_sem=hand_send.at[view, block],
            recv_sem=hand_recv.at[view, block],
            device_id=(mate, h),
            device_id_type=MESH,
        )

    def send(view, block):
        return pltpu.make_async_remote_copy(
            src_ref=outgoing.at[block, view],
            dst_ref=incoming.at[d, view],
            send_sem=part_send.at[view, block],
            recv_sem=part_recv.at[view, d],
            device_id=(block, h),
            device_id_type=MESH,
        )

    def receive(view, source):
        return pltpu.make_async_remote_copy(
            src_ref=outgoing.at[source, view],
            dst_ref=incoming.at[source, view],
            send_sem=part_send.at[view, source],
            recv_sem=part_recv.at[view, source],
            device_id=(source, h),
            device_id_type=MESH,
        )

    def each(count, body):
        def step(k, _):
            body(k)
            return 0

        lax.fori_loop(0, count, step, 0)

    def hand_over(view, k):
        block = odd * k + (1 - odd) * (groups - 1 - k)
        store(outgoing, block, view, partial(view, block))
        hand(view, block).start()

    def prepare(view, k):
        block = d + out_step * (1 + k)
        store(outgoing, block, view, partial(view, block))

    def to_mate(view):
        store(outgoing, mate, view, partial(view, mate))
        send(view, mate).start()

    def pass_on(view, k):
        block = odd * (groups - 1 - k) + (1 - odd) * k
        hand(view, block).wait_recv()
        own_part, other = load(outgoing, block, view), load(handed, block, view)
        swap = reverse[view] != odd
        store(outgoing, block, view, over(own_part, other, swap))
        send(view, block).start()

    reach = lax.div((first_plane + planes - 1) * margin, jnp.int32(total_planes))

    def hand_round(early):
        def one(k):
            block = odd * k + (1 - odd) * (groups - 1 - k)
            ready = ((block + 1) * share + reach <= rows - LEAD) & (odd == 1)

            @pl.when(ready if early else jnp.logical_not(ready))
            def _():
                each(views, lambda view: hand_over(view, k))

        each(handing, one)

    shade_low()
    hand_round(True)
    shade_high()
    hand_round(False)
    each(views, to_mate)
    each(views, lambda view: each(beyond, lambda k: prepare(view, k)))
    each(views, lambda view: store(incoming, d, view, partial(view, d)))
    each(beyond, lambda k: each(views, lambda view: pass_on(view, k)))

    def finish(view):
        swap = reverse[view] == 1
        receive(view, mate).wait_recv()
        both = over(load(incoming, d, view), load(incoming, mate, view), reverse[view] != odd)
        store(incoming, 2 * pair + 1, view, both)
        sources = [jnp.where(j > pair, 2 * j, 2 * j + 1) for j in range(groups // 2)]
        for j, source in enumerate(sources):

            @pl.when(j != pair)
            def _():
                receive(view, source).wait_recv()

        total = load(incoming, sources[0], view)
        for source in sources[1:]:
            total = over(total, load(incoming, source, view), swap)
        for c in range(4):
            out[c, view] = total[c]

    for view in range(views):
        finish(view)

    for index, route in enumerate(routes):
        ok, target = near(*route[0])

        @pl.when(ok)
        def _(index=index, target=target):
            halo(index, target).wait_send()

    def sent(view):
        send(view, mate).wait_send()
        each(handing, lambda k: hand(view, d - out_step * (2 + k)).wait_send())
        each(beyond, lambda k: send(view, d + out_step * (1 + k)).wait_send())

    each(views, sent)


def general(groups, towers, density, light, gain, bias, shear, reverse):
    planes, rows, cols = density.shape
    views = shear.shape[0]
    share = rows // groups
    tall = LEAD + rows + rows // 2
    scalars = pl.BlockSpec(memory_space=pltpu.SMEM)
    return pl.pallas_call(
        functools.partial(kernel, groups, towers),
        name="render",
        out_shape=pltpu.VMEM((4, views, share, cols), jnp.float32),
        in_specs=[pl.BlockSpec(memory_space=pltpu.HBM)] + [scalars] * 5,
        out_specs=pl.BlockSpec(memory_space=pltpu.VMEM),
        scratch_shapes=[
            pltpu.VMEM((planes + 2, tall + LEAD, cols), jnp.float32),
            pltpu.VMEM((4, planes, rows + rows // 2, cols), jnp.float32),
            pltpu.VMEM((groups, views, 4, share, cols), jnp.float32),
            pltpu.VMEM((groups, views, 4, share, cols), jnp.float32),
            pltpu.VMEM((groups, views, 4, share, cols), jnp.float32),
            pltpu.SemaphoreType.DMA,
            pltpu.SemaphoreType.DMA((6,)),
            pltpu.SemaphoreType.DMA((6,)),
            pltpu.SemaphoreType.DMA((views, groups)),
            pltpu.SemaphoreType.DMA((views, groups)),
            pltpu.SemaphoreType.DMA((views, groups)),
            pltpu.SemaphoreType.DMA((views, groups)),
        ],
        compiler_params=pltpu.CompilerParams(collective_id=0, has_side_effects=True, vmem_limit_bytes=60 * 1024 * 1024),
    )(density, light, gain, bias, shear, reverse)


def line(towers, density, light, gain, bias, shear, reverse):
    planes, rows, cols = density.shape
    views = shear.shape[0]
    groups = 4
    share = rows // groups
    whole = pl.BlockSpec(memory_space=pltpu.HBM)
    images = pltpu.VMEM((groups, views, 4, share, cols), jnp.float32)
    return pl.pallas_call(
        functools.partial(line_kernel, towers),
        name="render",
        out_shape=pltpu.VMEM((4, views, share, cols), jnp.float32),
        in_specs=[whole] * 6,
        out_specs=pl.BlockSpec(memory_space=pltpu.VMEM),
        scratch_shapes=[pltpu.SMEM(scalar.shape, scalar.dtype) for scalar in (light, gain, bias, shear, reverse)]
        + [
            pltpu.VMEM((2 * planes + 5, LEAD + rows + rows // 2 + LEAD, cols), jnp.float32),
            pltpu.VMEM((4, 2 * planes + 4, rows + rows // 2, cols), jnp.float32),
            images,
            images,
            images,
            pltpu.SemaphoreType.DMA((10,)),
            pltpu.SemaphoreType.DMA((8,)),
            pltpu.SemaphoreType.DMA((3 * views + 1,)),
            pltpu.SemaphoreType.DMA((1 + views,)),
            pltpu.SemaphoreType.REGULAR,
        ],
        compiler_params=pltpu.CompilerParams(collective_id=0, has_side_effects=True, vmem_limit_bytes=60 * 1024 * 1024),
    )(density, light, gain, bias, shear, reverse)


def on_device(groups, towers, density, light, gain, bias, shear, reverse):
    planes, rows, _ = density.shape
    if groups == 4 and planes >= 8 and rows % 64 == 0:
        return line(towers, density, light, gain, bias, shear, reverse)
    return general(groups, towers, density, light, gain, bias, shear, reverse)


def solution(mesh):
    groups, towers = mesh.shape["depth"], mesh.shape["height"]
    placed = (P("depth", "height", None), P(), P(), P(), P(), P())
    return jax.shard_map(
        functools.partial(on_device, groups, towers),
        mesh=mesh,
        in_specs=placed,
        out_specs=P(None, None, ("height", "depth"), None),
        check_vma=False,
    )
```
